32 devices in a mesh: groups: 2 (over y), cell: 4 (over z), wall: 4 (over x, core).
Axes of the slice: x: 2, y: 2, z: 4, core: 2. Of those that a mesh axis runs over, the one named last changes fastest.
Arguments:
- mem_pos: float32 [3, 2048], P(None, ('groups', 'cell')), parts along dimension 1, may hold values from -0.7 to 8, as said below
- forces: bfloat16 [32, 3, 2048], P(None, None, ('groups', 'cell', 'wall')), parts along dimension 2, may hold values from -1.59375 to 1.59375
- wall_pos: float32 [3, 1024], P(None, ('groups', 'wall')), parts along dimension 1, may hold values from -1 to 8, as said below
- wall_normal: float32 [3, 1024], P(None, ('groups', 'wall')), parts along dimension 1, as said below
- wall_data: float32 [32, 3, 1024], P(None, None, ('groups', 'wall')), parts along dimension 2, may hold values from -6 to 6
- lag_density: bfloat16 [16, 3, 1024], P(None, None, ('groups', 'wall', 'cell')), parts along dimension 2, may hold values from -15 to 15
- batch_order: int32 [32], replicated, may hold values from 0 to 31, each once
Outputs:
- membrane_velocity: float32 [32, 3, 2048], P(None, None, ('groups', 'cell', 'wall')), parts along dimension 2
- wall_density: float32 [16, 3, 1024], P(None, None, ('groups', 'wall', 'cell')), parts along dimension 2
The draws below stay inside these ranges and needn't reach their ends.
There are 2 independent parts, one for each index of `groups`. The reference program is written for one: setup_inputs(seed, part) draws one part's arguments, and reference() takes and returns one part's arrays. A program takes and returns all parts, laid end to end along the dimension named above; an argument that names none is the same for every part. Nothing has to cross between parts.
Inputs may be any that keep to these rules, and one draw needn't show every extreme that they name: `mem_pos`: each membrane point lies within 0.7 of the vessel axis (first two coordinates) with third coordinate between 0 and 8. `wall_pos`: each wall point lies on the unit cylinder around the vessel axis, third coordinate between 0 and 8. `wall_normal`: column w is the outward unit normal of the cylinder at wall_pos[:, w] times 16 pi / 512.
All inputs are finite; a program needn't handle non-finite values.
Results may differ from the reference program's by a relative error of at most 0.002.
Values may be sent and summed in bfloat16 or wider, within the bound.
A program may use at most 64 MiB of HBM per device.

```python
import math
import jax
import jax.numpy as jnp
from jax import lax

COLS = 32
HALF = 16
MEMBRANE = 1024
WALLS = 512


def draw_mem_pos(key, part):
    key_radius, key_angle, key_height = jax.random.split(jax.random.fold_in(key, 11), 3)
    uniform_draw = jax.random.uniform(key_radius, (MEMBRANE,), jnp.float32)
    radius = 0.7 * jnp.sqrt(uniform_draw)
    angle = jax.random.uniform(key_angle, (MEMBRANE,), jnp.float32, -math.pi, math.pi)
    height = jax.random.uniform(key_height, (MEMBRANE,), jnp.float32, 0.0, 8.0)
    return jnp.stack([radius * jnp.cos(angle), radius * jnp.sin(angle), height])


def wall_layout(key):
    key_angle, key_height = jax.random.split(jax.random.fold_in(key, 23))
    angle = jax.random.uniform(key_angle, (WALLS,), jnp.float32, -math.pi, math.pi)
    height = jax.random.uniform(key_height, (WALLS,), jnp.float32, 0.0, 8.0)
    return (angle, height)


def draw_wall_pos(key, part):
    angle, height = wall_layout(key)
    return jnp.stack([jnp.cos(angle), jnp.sin(angle), height])


def draw_wall_normal(key, part):
    angle, height = wall_layout(key)
    area = 16.0 * math.pi / WALLS
    return jnp.stack([jnp.cos(angle), jnp.sin(angle), jnp.zeros_like(height)]) * area


def level_of(key, shape, cuts, low, top_value):
    def one(axis_at, shards_of):
        draws = jax.random.uniform(jax.random.fold_in(jax.random.fold_in(key, 6), axis_at), (shards_of,), jnp.float32, low / len(cuts), top_value / len(cuts))
        return jnp.repeat(jnp.exp(draws), shape[axis_at] // shards_of).reshape((-1,) + (1,) * (len(shape) - axis_at - 1))

    loudness = one(*cuts[0])
    for cut in cuts[1:]:
        loudness = loudness * one(*cut)
    return loudness


def scatter_about(rng, dims, scale, most, shards=(), kind=jnp.bfloat16):
    entries = scale * jax.random.normal(rng, dims, jnp.float32)
    if shards:
        entries = entries * level_of(rng, dims, shards, -0.22, 0.18)
    return jnp.clip(entries, -most, most).astype(kind)


def setup_inputs(seed: int = 0, part: int = 0) -> dict:
    arg_keys = jax.random.split(jax.random.key(seed), 8)
    part_splits = jax.random.split(jax.random.fold_in(arg_keys[7], part), 8)
    mem_pos = draw_mem_pos(jax.random.fold_in(jax.random.fold_in(arg_keys[7], part), 71), part)
    forces = scatter_about(part_splits[1], (COLS, 3, MEMBRANE), 0.2, 1.59375, ((2, 16),))
    wall_pos = draw_wall_pos(jax.random.fold_in(jax.random.fold_in(arg_keys[7], part), 71), part)
    wall_normal = draw_wall_normal(jax.random.fold_in(jax.random.fold_in(arg_keys[7], part), 71), part)
    wall_data = scatter_about(part_splits[4], (COLS, 3, WALLS), 1.0, 6.0, ((2, 4),), jnp.float32)
    lag_density = scatter_about(part_splits[5], (HALF, 3, WALLS), 3.0, 15.0, ((2, 16),))
    batch_order = jax.random.permutation(arg_keys[6], COLS).astype(jnp.int32)
    return dict(mem_pos=mem_pos, forces=forces, wall_pos=wall_pos, wall_normal=wall_normal, wall_data=wall_data, lag_density=lag_density, batch_order=batch_order)


stokes_coef = 1.0 / (8.0 * math.pi)

def single_tile(targets, sources):
    separation = targets[:, None, :] - sources[:, :, None]
    inverse = lax.rsqrt(lax.optimization_barrier(jnp.sum(separation * separation, axis=0)))
    inverse_cube = inverse * inverse * inverse
    stacked = []
    for second_dim in range(3):
        entries_row = []
        for first_dim in range(3):
            element = separation[first_dim] * separation[second_dim] * inverse_cube
            if first_dim == second_dim:
                element = element + inverse
            entries_row.append(element * stokes_coef)
        stacked.append(jnp.stack(entries_row, axis=1))
    kernel_tile = jnp.stack(stacked, axis=0)
    return kernel_tile.reshape(3 * sources.shape[1], 3 * targets.shape[1]).astype(jnp.bfloat16)

def double_tile(targets, sources, normals):
    separation = targets[:, None, :] - sources[:, :, None]
    inverse = lax.rsqrt(lax.optimization_barrier(jnp.sum(separation * separation, axis=0)))
    normal_flux = lax.optimization_barrier(jnp.sum(separation * normals[:, :, None], axis=0))
    weight = -6.0 * stokes_coef * normal_flux * inverse ** 5
    stacked = []
    for second_dim in range(3):
        entries_row = []
        for first_dim in range(3):
            entries_row.append(weight * separation[first_dim] * separation[second_dim])
        stacked.append(jnp.stack(entries_row, axis=1))
    kernel_tile = jnp.stack(stacked, axis=0)
    return kernel_tile.reshape(3 * sources.shape[1], 3 * targets.shape[1]).astype(jnp.bfloat16)

def reference(mem_pos, forces, wall_pos, wall_normal, wall_data, lag_density, batch_order):
    columns = forces.shape[0]
    halfway = columns // 2
    point_count = mem_pos.shape[1]
    wall_count = wall_pos.shape[1]
    piece_len = math.gcd(point_count, 128)
    block_count = point_count // piece_len

    def add_single(running, block_index):
        offset = (block_index * piece_len).astype(jnp.int32)
        position = lax.dynamic_slice_in_dim(mem_pos, offset, piece_len, 1)
        loaded = lax.dynamic_slice_in_dim(forces, offset, piece_len, 2).reshape(columns, 3 * piece_len)
        return (running + jnp.dot(loaded, single_tile(wall_pos, position), preferred_element_type=jnp.float32), None)
    running, _ = lax.scan(add_single, jnp.zeros((columns, 3 * wall_count), jnp.float32), jnp.arange(block_count, dtype=jnp.int32))
    wall_velocity = running.reshape(columns, 3, wall_count)
    density = 2.0 * (wall_data - wall_velocity)
    first = jnp.take(density, batch_order[:halfway], axis=0).astype(jnp.bfloat16)
    wall_density = jnp.take(density, batch_order[halfway:], axis=0)
    carried = jnp.concatenate([lag_density, first], axis=0).reshape(columns, 3 * wall_count)

    def one_block(block_index):
        offset = (block_index * piece_len).astype(jnp.int32)
        position = lax.dynamic_slice_in_dim(mem_pos, offset, piece_len, 1)
        product = jnp.dot(carried, double_tile(position, wall_pos, wall_normal), preferred_element_type=jnp.float32)
        return product.reshape(columns, 3, piece_len)
    pieces = lax.map(one_block, jnp.arange(block_count, dtype=jnp.int32))
    batched = jnp.transpose(pieces, (1, 2, 0, 3)).reshape(columns, 3, point_count)
    membrane_velocity = jnp.zeros_like(batched).at[batch_order].set(batched)
    return (membrane_velocity, wall_density)
```

```python
import functools
import math

import jax
import jax.numpy as jnp
from jax import lax
from jax.experimental import pallas as pl
from jax.experimental.pallas import tpu as pltpu
from jax.sharding import PartitionSpec as P

stokes_coef = 1.0 / (8.0 * math.pi)


def single_tile(targets, sources):
    separation = targets[:, None, :] - sources[:, :, None]
    inverse = lax.rsqrt(jnp.sum(separation * separation, axis=0))
    inverse_cube = inverse * inverse * inverse
    stacked = []
    for second_dim in range(3):
        entries_row = []
        for first_dim in range(3):
            element = separation[first_dim] * separation[second_dim] * inverse_cube
            if first_dim == second_dim:
                element = element + inverse
            entries_row.append(element * stokes_coef)
        stacked.append(jnp.stack(entries_row, axis=1))
    kernel_tile = jnp.stack(stacked, axis=0)
    return kernel_tile.reshape(3 * sources.shape[1], 3 * targets.shape[1]).astype(jnp.bfloat16)


def double_tile(targets, sources, normals):
    separation = targets[:, None, :] - sources[:, :, None]
    inverse = lax.rsqrt(jnp.sum(separation * separation, axis=0))
    normal_flux = jnp.sum(separation * normals[:, :, None], axis=0)
    weight = -6.0 * stokes_coef * normal_flux * inverse**5
    stacked = []
    for second_dim in range(3):
        entries_row = []
        for first_dim in range(3):
            entries_row.append(weight * separation[first_dim] * separation[second_dim])
        stacked.append(jnp.stack(entries_row, axis=1))
    kernel_tile = jnp.stack(stacked, axis=0)
    return kernel_tile.reshape(3 * sources.shape[1], 3 * targets.shape[1]).astype(jnp.bfloat16)


def shards(mem_pos, forces, wall_pos, wall_normal, wall_data, lag_density, batch_order):
    columns = forces.shape[0]
    halfway = columns // 2
    point_count = mem_pos.shape[1]
    wall_count = wall_pos.shape[1]
    shard_width = lag_density.shape[2]
    piece_len = math.gcd(point_count, 128)
    block_count = point_count // piece_len
    first_rows = batch_order[:halfway]
    second_rows = batch_order[halfway:]
    force_block = lax.all_gather(forces, "wall", axis=2, tiled=True)
    lag_block = lax.all_gather(lag_density, "cell", axis=2, tiled=True)
    lag_flat = lag_block.reshape(halfway, 3 * wall_count)

    def position_at(block_index):
        return lax.dynamic_slice_in_dim(mem_pos, block_index * piece_len, piece_len, 1)

    def single_term(block_index):
        loaded = lax.dynamic_slice_in_dim(force_block, block_index * piece_len, piece_len, 2)
        loaded = loaded.reshape(columns, 3 * piece_len)
        return jnp.dot(
            loaded,
            single_tile(wall_pos, position_at(block_index)),
            preferred_element_type=jnp.float32,
        )

    def double_term(dense_rows, block_index):
        kernel_tile = double_tile(position_at(block_index), wall_pos, wall_normal)
        product = jnp.dot(dense_rows, kernel_tile, preferred_element_type=jnp.float32)
        return product.reshape(dense_rows.shape[0], 3, piece_len)

    def place_block(target, piece, block_index):
        return lax.dynamic_update_slice_in_dim(target, piece, block_index * piece_len, 2)

    empty_wall = jnp.zeros((columns, 3 * wall_count), jnp.float32)

    def add_single(block_index, running):
        return running + single_term(block_index)

    running = lax.fori_loop(0, block_count, add_single, empty_wall)
    wall_term = running.reshape(columns, 3, wall_count)
    position_cell = lax.axis_index("cell")
    first_sum = lax.psum(jnp.take(wall_term, first_rows, axis=0), "cell")
    first_block = (2.0 * (jnp.take(wall_data, first_rows, axis=0) - first_sum)).astype(jnp.bfloat16)
    second_sum = lax.psum_scatter(
        jnp.take(wall_term, second_rows, axis=0).astype(jnp.bfloat16),
        "cell",
        scatter_dimension=2,
        tiled=True,
    ).astype(jnp.float32)
    second_data = lax.dynamic_slice_in_dim(
        jnp.take(wall_data, second_rows, axis=0), position_cell * shard_width, shard_width, 2
    )
    wall_density = 2.0 * (second_data - second_sum)
    first_flat = first_block.reshape(halfway, 3 * wall_count)
    carried = jnp.concatenate([lag_flat, first_flat], axis=0)

    def all_terms(block_index, target):
        return place_block(target, double_term(carried, block_index), block_index)

    membrane_term = lax.fori_loop(
        0, block_count, all_terms, jnp.zeros((columns, 3, point_count), jnp.float32)
    )
    batched = lax.psum_scatter(membrane_term, "wall", scatter_dimension=2, tiled=True)
    membrane_velocity = jnp.zeros_like(batched).at[batch_order].set(batched)
    return (membrane_velocity, wall_density)

LANES = 128
MESH = pl.DeviceIdType.MESH
NT = (((1,), (1,)), ((), ()))


def fused_kernel(
    cells,
    walls,
    mem_hbm,
    force_hbm,
    wall_hbm,
    normal_hbm,
    data_hbm,
    lag_hbm,
    order_hbm,
    out_ref,
    density_ref,
    order_ref,
    force_all,
    lag_all,
    mem_all,
    wall_all,
    data_all,
    wall_cols,
    mem_cols,
    single_all,
    double_all,
    part_mine,
    part_other,
    load_sem,
    force_send,
    force_recv,
    lag_send,
    lag_recv,
    mem_send,
    mem_recv,
    wall_send,
    wall_recv,
    data_send,
    data_recv,
    part_send,
    part_recv,
    ready,
):
    cell = lax.axis_index("cell")
    wall = lax.axis_index("wall")
    chip = wall // 2
    core = wall % 2
    other_core = 1 - core
    other_chip = 1 - chip
    columns = order_ref.shape[1]
    halfway = columns // 2
    point_count = mem_hbm.shape[1]
    wall_count = wall_hbm.shape[1]
    own_points = force_hbm.shape[2]
    shard_width = lag_hbm.shape[2]
    block = 3 * wall_count

    loads = [
        pltpu.make_async_copy(given, held, load_sem.at[at])
        for at, (given, held) in enumerate(
            (
                (order_hbm, order_ref),
                (mem_hbm, mem_all.at[cell]),
                (wall_hbm, wall_all.at[wall, 0]),
                (normal_hbm, wall_all.at[wall, 1]),
                (lag_hbm, lag_all.at[cell, wall]),
                (data_hbm, data_all.at[wall]),
            )
        )
    ]

    partner = 2 * chip + other_core
    across = 2 * other_chip + core
    diagonal = 2 * other_chip + other_core
    peers = (partner, diagonal, across)

    barrier = pltpu.get_barrier_semaphore()
    for peer in peers:
        pl.semaphore_signal(barrier, inc=1, device_id={"wall": peer}, device_id_type=MESH)
    for target in range(cells - 1, 0, -1):

        @pl.when(target > cell)
        def _(target=target):
            for peer in (*peers, wall):
                pl.semaphore_signal(
                    barrier, inc=1, device_id={"cell": target, "wall": peer}, device_id_type=MESH
                )

    for load in loads:
        load.start()

    def force_copy(to_cell, to_chip, slot):
        return pltpu.make_async_remote_copy(
            force_hbm,
            force_all.at[cell, chip],
            force_send.at[slot, to_chip],
            force_recv.at[cell, chip],
            device_id={"cell": to_cell, "wall": 2 * to_chip + other_core},
            device_id_type=MESH,
        )

    def lag_copy(to_cell, to_wall, slot):
        return pltpu.make_async_remote_copy(
            lag_hbm,
            lag_all.at[cell, wall],
            lag_send.at[slot, to_wall],
            lag_recv.at[cell, wall],
            device_id={"cell": to_cell, "wall": to_wall},
            device_id_type=MESH,
        )

    def mem_copy(to_cell, slot):
        return pltpu.make_async_remote_copy(
            mem_hbm,
            mem_all.at[cell],
            mem_send.at[slot],
            mem_recv.at[cell],
            device_id={"cell": to_cell, "wall": partner},
            device_id_type=MESH,
        )

    def wall_copy(given, at, to_wall):
        return pltpu.make_async_remote_copy(
            given,
            wall_all.at[wall, at],
            wall_send.at[to_wall, at],
            wall_recv.at[wall, at],
            device_id={"wall": to_wall},
            device_id_type=MESH,
        )

    def data_copy(to_wall):
        return pltpu.make_async_remote_copy(
            data_hbm,
            data_all.at[wall],
            data_send.at[to_wall],
            data_recv.at[wall],
            device_id={"wall": to_wall},
            device_id_type=MESH,
        )

    def far_copies(target):
        copies = [mem_copy(target, target)]
        copies += [force_copy(target, to_chip, target) for to_chip in (other_chip, chip)]
        copies += [lag_copy(target, peer, target) for peer in (*peers, wall)]
        return copies

    def near_copies():
        copies = [wall_copy(wall_hbm, 0, peer) for peer in peers]
        copies += [wall_copy(normal_hbm, 1, peer) for peer in peers]
        copies += [force_copy(cell, to_chip, cells) for to_chip in (other_chip, chip)]
        copies += [data_copy(peer) for peer in peers]
        copies += [lag_copy(cell, peer, cells) for peer in peers]
        return copies

    pl.semaphore_wait(barrier, walls - 1 + walls * cell)

    for target in range(cells - 1):

        @pl.when(target < cell)
        def _(target=target):
            for copy in far_copies(target):
                copy.start()
            pl.semaphore_signal(
                ready.at[cell],
                inc=1,
                device_id={"cell": target, "wall": partner},
                device_id_type=MESH,
            )

    for copy in near_copies():
        copy.start()

    for load in loads[:4]:
        load.wait()

    order_row = order_ref[...]
    row_ids = lax.broadcasted_iota(jnp.int32, (columns, columns), 0)
    col_ids = lax.broadcasted_iota(jnp.int32, (columns, columns), 1)
    scatter = (row_ids == order_row).astype(jnp.float32).astype(jnp.bfloat16)
    unit = (row_ids == col_ids).astype(jnp.float32).astype(jnp.bfloat16)
    gather_f32 = lax.dot_general(unit, scatter, NT, preferred_element_type=jnp.float32)
    turned = ((row_ids == order_row) & (col_ids >= halfway)).astype(jnp.float32)
    is_first = jnp.sum(turned, axis=1, keepdims=True) > 0.5
    paired = jnp.concatenate([gather_f32[halfway:], gather_f32[:halfway]], axis=0)
    swap_f32 = jnp.dot(scatter, paired.astype(jnp.bfloat16), preferred_element_type=jnp.float32)
    swap = swap_f32.astype(jnp.bfloat16)

    def spread_wall(source):
        for j in range(3):
            wall_cols[source, j] = jnp.broadcast_to(
                wall_all[source, 0, j : j + 1, :], (LANES, wall_count)
            ).T

    for j in range(3):
        mem_cols[j] = jnp.broadcast_to(mem_all[cell, j : j + 1, :], (LANES, point_count)).T

    lane_ids = lax.broadcasted_iota(jnp.int32, (8, LANES), 1)

    def mem_rows(source):
        rows = []
        for j in range(3):
            low = jnp.broadcast_to(mem_all[source, j : j + 1, :LANES], (8, LANES))
            high = jnp.broadcast_to(mem_all[source, j : j + 1, LANES:], (8, LANES))
            low = pltpu.roll(low, own_points * other_core, 1)
            high = pltpu.roll(high, own_points * core, 1)
            rows.append(jnp.where(lane_ids < own_points, low, high)[0:1])
        return rows

    def fill_single(source, rows, at):
        apart = [wall_cols[at, j] - rows[j] for j in range(3)]
        square = apart[0] * apart[0] + apart[1] * apart[1] + apart[2] * apart[2]
        inverse = lax.rsqrt(square)
        scaled = stokes_coef * inverse
        cube = scaled * (inverse * inverse)
        for j in range(3):
            along = apart[j] * cube
            for i in range(j + 1):
                element = along * apart[i]
                if i == j:
                    element = element + scaled
                element = element.astype(jnp.bfloat16)
                for a, b in {(i, j), (j, i)}:
                    single_all[source, at, a, :, b * LANES : (b + 1) * LANES] = element

    def fill_double(source):
        own = pl.ds(pl.multiple_of(wall * own_points, own_points), own_points)
        apart = [mem_cols[j, own, :] - wall_all[source, 0, j : j + 1, :] for j in range(3)]
        square = apart[0] * apart[0] + apart[1] * apart[1] + apart[2] * apart[2]
        inverse = lax.rsqrt(square)
        flux = (
            apart[0] * wall_all[source, 1, 0:1, :]
            + apart[1] * wall_all[source, 1, 1:2, :]
            + apart[2] * wall_all[source, 1, 2:3, :]
        )
        inverse_square = inverse * inverse
        fifth = inverse_square * inverse_square * inverse
        weight = (-6.0 * stokes_coef) * flux * fifth
        for j in range(3):
            along = apart[j] * weight
            for i in range(j + 1):
                element = (along * apart[i]).astype(jnp.bfloat16)
                for a, b in {(i, j), (j, i)}:
                    double_all[
                        source,
                        a * own_points : (a + 1) * own_points,
                        b * wall_count : (b + 1) * wall_count,
                    ] = element

    own_rows = mem_rows(cell)
    spread_wall(wall)
    fill_single(cell, own_rows, wall)
    fill_double(wall)

    for peer in peers:
        for at in range(2):
            pltpu.make_async_remote_copy(
                wall_all.at[peer, at],
                wall_all.at[peer, at],
                wall_send.at[peer, at],
                wall_recv.at[peer, at],
                device_id={"wall": peer},
                device_id_type=MESH,
            ).wait_recv()
        spread_wall(peer)
        fill_single(cell, own_rows, peer)
        fill_double(peer)

    for target in range(1, cells):

        @pl.when(target > cell)
        def _(target=target):
            pl.semaphore_wait(ready.at[target], 1)
            for copy in far_copies(target):
                copy.start()

    def wait_force(source, at):
        pltpu.make_async_remote_copy(
            force_all.at[source, at],
            force_all.at[source, at],
            force_send.at[0, at],
            force_recv.at[source, at],
            device_id={"wall": partner},
            device_id_type=MESH,
        ).wait_recv()

    def single_layer(source):
        for at in range(2):
            wait_force(source, at)
        loaded = jnp.concatenate(
            [force_all[source, at, j] for j in range(3) for at in range(2)], axis=1
        )
        loaded = jnp.dot(swap, loaded, preferred_element_type=jnp.float32).astype(jnp.bfloat16)
        return lax.dot_general(
            loaded,
            single_all[source].reshape(walls * block, 3 * LANES),
            NT,
            preferred_element_type=jnp.float32,
        )

    partial = single_layer(cell)
    for load in loads[4:]:
        load.wait()
    for peer in peers:
        pltpu.make_async_remote_copy(
            data_all.at[peer],
            data_all.at[peer],
            data_send.at[peer],
            data_recv.at[peer],
            device_id={"wall": peer},
            device_id_type=MESH,
        ).wait_recv()
    for source in range(walls):
        for i in range(3):
            data_all[source, i] = jnp.dot(
                swap_f32, data_all[source, i], precision=lax.Precision.HIGHEST
            )

    for step in range(1, cells):
        source = jnp.where(cell + step < cells, cell + step, cells - 1 - step)
        pltpu.make_async_remote_copy(
            mem_all.at[source],
            mem_all.at[source],
            mem_send.at[0],
            mem_recv.at[source],
            device_id={"wall": partner},
            device_id_type=MESH,
        ).wait_recv()
        rows = mem_rows(source)
        for at in range(walls):
            fill_single(source, rows, at)
        partial = partial + single_layer(source)
    part_mine[...] = partial
    exchange = pltpu.make_async_remote_copy(
        part_mine,
        part_other,
        part_send,
        part_recv,
        device_id={"wall": partner},
        device_id_type=MESH,
    )
    exchange.start()

    def wait_lag(source, at):
        pltpu.make_async_remote_copy(
            lag_all.at[source, at],
            lag_all.at[source, at],
            lag_send.at[0, at],
            lag_recv.at[source, at],
            device_id={"wall": partner},
            device_id_type=MESH,
        ).wait_recv()

    for peer in peers:
        wait_lag(cell, peer)
    for step in range(1, cells):
        source = jnp.where(cell + step < cells, cell + step, cells - 1 - step)
        for at in range(walls):
            wait_lag(source, at)
    lag = jnp.concatenate(
        [lag_all[c, at, j] for at in range(walls) for j in range(3) for c in range(cells)], axis=1
    )
    placed_lag = jnp.dot(scatter[:, :halfway], lag, preferred_element_type=jnp.float32)

    for target in range(cells):

        @pl.when(target != cell)
        def _(target=target):
            for copy in far_copies(target):
                copy.wait_send()

    for copy in near_copies():
        copy.wait_send()

    exchange.wait_recv()
    total = jnp.zeros((columns, 3 * own_points), jnp.float32)
    for source in range(walls):
        pieces = []
        for i in range(3):
            lanes = slice(source * block + i * wall_count, source * block + (i + 1) * wall_count)
            dense = 2.0 * (data_all[source, i] - (partial[:, lanes] + part_other[:, lanes]))
            pieces.append(jnp.where(is_first, dense, placed_lag[:, lanes]).astype(jnp.bfloat16))
        total = total + lax.dot_general(
            jnp.concatenate(pieces, axis=1),
            double_all[source],
            NT,
            preferred_element_type=jnp.float32,
        )
    for i in range(3):
        out_ref[i] = total[:, i * own_points : (i + 1) * own_points]

    shift = lax.rem((cells - cell) * shard_width, wall_count)
    for i in range(3):
        lanes = pl.ds(pl.multiple_of(wall * block + i * wall_count, wall_count), wall_count)
        dense = 2.0 * (data_all[wall, i] - (part_mine[:, lanes] + part_other[:, lanes]))
        dense = jnp.dot(gather_f32[:halfway], dense, precision=lax.Precision.HIGHEST)
        density_ref[i] = pltpu.roll(dense, shift, 1)[:, :shard_width]
    exchange.wait_send()


def write_kernel(velocity_ref, density_ref, velocity_hbm, density_hbm, sem):
    first = pltpu.make_async_copy(velocity_ref, velocity_hbm, sem.at[0])
    second = pltpu.make_async_copy(density_ref, density_hbm, sem.at[1])
    first.start()
    second.start()
    first.wait()
    second.wait()


def fused_shards(cells, walls, mem_pos, forces, wall_pos, wall_normal, wall_data, lag_density, batch_order):
    columns = forces.shape[0]
    halfway = columns // 2
    point_count = mem_pos.shape[1]
    wall_count = wall_pos.shape[1]
    own_points = forces.shape[2]
    shard_width = lag_density.shape[2]
    dma = pltpu.SemaphoreType.DMA
    vmem = pl.BlockSpec(memory_space=pltpu.VMEM)
    hbm = pl.BlockSpec(memory_space=pltpu.HBM)
    velocity, density = pl.pallas_call(
        functools.partial(fused_kernel, cells, walls),
        out_shape=(
            pltpu.VMEM((3, columns, own_points), jnp.float32),
            pltpu.VMEM((3, halfway, shard_width), jnp.float32),
        ),
        in_specs=[hbm] * 7,
        out_specs=(vmem, vmem),
        scratch_shapes=[
            pltpu.VMEM((1, columns), jnp.int32),
            pltpu.VMEM((cells, 2, 3, columns, own_points), jnp.bfloat16),
            pltpu.VMEM((cells, walls, 3, halfway, shard_width), jnp.bfloat16),
            pltpu.VMEM((cells, 3, point_count), jnp.float32),
            pltpu.VMEM((walls, 2, 3, wall_count), jnp.float32),
            pltpu.VMEM((walls, 3, columns, wall_count), jnp.float32),
            pltpu.VMEM((walls, 3, wall_count, LANES), jnp.float32),
            pltpu.VMEM((3, point_count, LANES), jnp.float32),
            pltpu.VMEM((cells, walls, 3, wall_count, 3 * LANES), jnp.bfloat16),
            pltpu.VMEM((walls, 3 * own_points, 3 * wall_count), jnp.bfloat16),
            pltpu.VMEM((columns, walls * 3 * wall_count), jnp.float32),
            pltpu.VMEM((columns, walls * 3 * wall_count), jnp.float32),
            dma((6,)),
            dma((cells + 1, 2)),
            dma((cells, 2)),
            dma((cells + 1, walls)),
            dma((cells, walls)),
            dma((cells,)),
            dma((cells,)),
            dma((walls, 2)),
            dma((walls, 2)),
            dma((walls,)),
            dma((walls,)),
            dma,
            dma,
            pltpu.SemaphoreType.REGULAR((cells,)),
        ],
        compiler_params=pltpu.CompilerParams(
            collective_id=0, has_side_effects=True, vmem_limit_bytes=VMEM_GRANT
        ),
        name="coupling",
    )(
        mem_pos,
        jnp.transpose(forces, (1, 0, 2)),
        wall_pos,
        wall_normal,
        jnp.transpose(wall_data, (1, 0, 2)),
        jnp.transpose(lag_density, (1, 0, 2)),
        batch_order.reshape(1, columns),
    )
    velocity, density = pl.pallas_call(
        write_kernel,
        out_shape=(
            jax.ShapeDtypeStruct(velocity.shape, velocity.dtype),
            jax.ShapeDtypeStruct(density.shape, density.dtype),
        ),
        in_specs=[vmem] * 2,
        out_specs=(hbm, hbm),
        scratch_shapes=[dma((2,))],
        compiler_params=pltpu.CompilerParams(vmem_limit_bytes=1024 * 1024),
        name="write",
    )(velocity, density)
    return (jnp.transpose(velocity, (1, 0, 2)), jnp.transpose(density, (1, 0, 2)))


VMEM_GRANT = 60 * 1024 * 1024


def step(cells, walls, mem_pos, forces, wall_pos, *rest):
    point_count = mem_pos.shape[1]
    wall_count = wall_pos.shape[1]
    own_points = forces.shape[2]
    shard_width = rest[2].shape[2]
    tiles = 18 * walls * wall_count * (cells * LANES + own_points)
    fits = tiles <= VMEM_GRANT // 2
    aligned = (
        walls == 4
        and wall_count == LANES
        and 2 * own_points == LANES
        and point_count == walls * own_points
        and wall_count == cells * shard_width
    )
    if fits and aligned:
        return fused_shards(cells, walls, mem_pos, forces, wall_pos, *rest)
    return shards(mem_pos, forces, wall_pos, *rest)


def solution(mesh):
    placed = (
        P(None, ("groups", "cell")),
        P(None, None, ("groups", "cell", "wall")),
        P(None, ("groups", "wall")),
        P(None, ("groups", "wall")),
        P(None, None, ("groups", "wall")),
        P(None, None, ("groups", "wall", "cell")),
        P(),
    )
    return jax.shard_map(
        functools.partial(step, mesh.shape["cell"], mesh.shape["wall"]),
        mesh=mesh,
        in_specs=placed,
        out_specs=(
            P(None, None, ("groups", "cell", "wall")),
            P(None, None, ("groups", "wall", "cell")),
        ),
        check_vma=False,
    )
```

```python
import functools
import math

import jax
import jax.numpy as jnp
from jax import lax
from jax.experimental import pallas as pl
from jax.experimental.pallas import tpu as pltpu
from jax.sharding import PartitionSpec as P

stokes_coef = 1.0 / (8.0 * math.pi)


def single_tile(targets, sources):
    separation = targets[:, None, :] - sources[:, :, None]
    inverse = lax.rsqrt(jnp.sum(separation * separation, axis=0))
    inverse_cube = inverse * inverse * inverse
    stacked = []
    for second_dim in range(3):
        entries_row = []
        for first_dim in range(3):
            element = separation[first_dim] * separation[second_dim] * inverse_cube
            if first_dim == second_dim:
                element = element + inverse
            entries_row.append(element * stokes_coef)
        stacked.append(jnp.stack(entries_row, axis=1))
    kernel_tile = jnp.stack(stacked, axis=0)
    return kernel_tile.reshape(3 * sources.shape[1], 3 * targets.shape[1]).astype(jnp.bfloat16)


def double_tile(targets, sources, normals):
    separation = targets[:, None, :] - sources[:, :, None]
    inverse = lax.rsqrt(jnp.sum(separation * separation, axis=0))
    normal_flux = jnp.sum(separation * normals[:, :, None], axis=0)
    weight = -6.0 * stokes_coef * normal_flux * inverse**5
    stacked = []
    for second_dim in range(3):
        entries_row = []
        for first_dim in range(3):
            entries_row.append(weight * separation[first_dim] * separation[second_dim])
        stacked.append(jnp.stack(entries_row, axis=1))
    kernel_tile = jnp.stack(stacked, axis=0)
    return kernel_tile.reshape(3 * sources.shape[1], 3 * targets.shape[1]).astype(jnp.bfloat16)


def shards(mem_pos, forces, wall_pos, wall_normal, wall_data, lag_density, batch_order):
    columns = forces.shape[0]
    halfway = columns // 2
    point_count = mem_pos.shape[1]
    wall_count = wall_pos.shape[1]
    shard_width = lag_density.shape[2]
    piece_len = math.gcd(point_count, 128)
    block_count = point_count // piece_len
    first_rows = batch_order[:halfway]
    second_rows = batch_order[halfway:]
    force_block = lax.all_gather(forces, "wall", axis=2, tiled=True)
    lag_block = lax.all_gather(lag_density, "cell", axis=2, tiled=True)
    lag_flat = lag_block.reshape(halfway, 3 * wall_count)

    def position_at(block_index):
        return lax.dynamic_slice_in_dim(mem_pos, block_index * piece_len, piece_len, 1)

    def single_term(block_index):
        loaded = lax.dynamic_slice_in_dim(force_block, block_index * piece_len, piece_len, 2)
        loaded = loaded.reshape(columns, 3 * piece_len)
        return jnp.dot(
            loaded,
            single_tile(wall_pos, position_at(block_index)),
            preferred_element_type=jnp.float32,
        )

    def double_term(dense_rows, block_index):
        kernel_tile = double_tile(position_at(block_index), wall_pos, wall_normal)
        product = jnp.dot(dense_rows, kernel_tile, preferred_element_type=jnp.float32)
        return product.reshape(dense_rows.shape[0], 3, piece_len)

    def place_block(target, piece, block_index):
        return lax.dynamic_update_slice_in_dim(target, piece, block_index * piece_len, 2)

    empty_wall = jnp.zeros((columns, 3 * wall_count), jnp.float32)

    def add_single(block_index, running):
        return running + single_term(block_index)

    running = lax.fori_loop(0, block_count, add_single, empty_wall)
    wall_term = running.reshape(columns, 3, wall_count)
    position_cell = lax.axis_index("cell")
    first_sum = lax.psum(jnp.take(wall_term, first_rows, axis=0), "cell")
    first_block = (2.0 * (jnp.take(wall_data, first_rows, axis=0) - first_sum)).astype(jnp.bfloat16)
    second_sum = lax.psum_scatter(
        jnp.take(wall_term, second_rows, axis=0).astype(jnp.bfloat16),
        "cell",
        scatter_dimension=2,
        tiled=True,
    ).astype(jnp.float32)
    second_data = lax.dynamic_slice_in_dim(
        jnp.take(wall_data, second_rows, axis=0), position_cell * shard_width, shard_width, 2
    )
    wall_density = 2.0 * (second_data - second_sum)
    first_flat = first_block.reshape(halfway, 3 * wall_count)
    carried = jnp.concatenate([lag_flat, first_flat], axis=0)

    def all_terms(block_index, target):
        return place_block(target, double_term(carried, block_index), block_index)

    membrane_term = lax.fori_loop(
        0, block_count, all_terms, jnp.zeros((columns, 3, point_count), jnp.float32)
    )
    batched = lax.psum_scatter(membrane_term, "wall", scatter_dimension=2, tiled=True)
    membrane_velocity = jnp.zeros_like(batched).at[batch_order].set(batched)
    return (membrane_velocity, wall_density)

LANES = 128
MESH = pl.DeviceIdType.MESH
NT = (((1,), (1,)), ((), ()))


def fused_kernel(
    cells,
    walls,
    mem_hbm,
    force_hbm,
    wall_hbm,
    normal_hbm,
    data_hbm,
    lag_hbm,
    order_hbm,
    out_ref,
    density_ref,
    order_ref,
    force_ref,
    lag_ref,
    data_ref,
    blocks,
    passed,
    mem_all,
    wall_all,
    data_all,
    wall_cols,
    mem_cols,
    single_all,
    double_all,
    part_mine,
    part_other,
    rest_mine,
    rest_other,
    load_sem,
    block_send,
    block_recv,
    pass_send,
    pass_recv,
    mem_send,
    mem_recv,
    wall_send,
    wall_recv,
    data_send,
    data_recv,
    part_send,
    part_recv,
    ready,
):
    cell = lax.axis_index("cell")
    wall = lax.axis_index("wall")
    chip = wall // 2
    core = wall % 2
    other_core = 1 - core
    other_chip = 1 - chip
    columns = order_ref.shape[1]
    halfway = columns // 2
    point_count = mem_hbm.shape[1]
    wall_count = wall_hbm.shape[1]
    own_points = force_ref.shape[2]
    shard_width = lag_ref.shape[2]
    block = 3 * wall_count

    loads = [
        pltpu.make_async_copy(given, held, load_sem.at[at])
        for at, (given, held) in enumerate(
            (
                (order_hbm, order_ref),
                (force_hbm, force_ref),
                (lag_hbm, lag_ref),
                (mem_hbm, mem_all.at[cell]),
                (wall_hbm, wall_all.at[wall, 0]),
                (normal_hbm, wall_all.at[wall, 1]),
                (data_hbm, data_ref),
            )
        )
    ]
    for load in loads:
        load.start()

    partner = 2 * chip + other_core
    across = 2 * other_chip + core
    diagonal = 2 * other_chip + other_core
    peers = (partner, diagonal, across)

    barrier = pltpu.get_barrier_semaphore()
    for peer in peers:
        pl.semaphore_signal(barrier, inc=1, device_id={"wall": peer}, device_id_type=MESH)
    for target in range(cells - 1, 0, -1):

        @pl.when(target > cell)
        def _(target=target):
            for to_chip in range(2):
                pl.semaphore_signal(
                    barrier,
                    inc=1,
                    device_id={"cell": target, "wall": 2 * to_chip + other_core},
                    device_id_type=MESH,
                )

    loads[0].wait()
    order_row = order_ref[...]
    row_ids = lax.broadcasted_iota(jnp.int32, (columns, columns), 0)
    col_ids = lax.broadcasted_iota(jnp.int32, (columns, columns), 1)
    scatter = (row_ids == order_row).astype(jnp.float32).astype(jnp.bfloat16)
    unit = (row_ids == col_ids).astype(jnp.float32).astype(jnp.bfloat16)
    gather_f32 = lax.dot_general(unit, scatter, NT, preferred_element_type=jnp.float32)
    gather = gather_f32.astype(jnp.bfloat16)

    loads[1].wait()
    rows = [jnp.dot(gather, force_ref[j], preferred_element_type=jnp.float32) for j in range(3)]
    loads[2].wait()
    lag_rows = [lag_ref[j].astype(jnp.float32) for j in range(3)]
    spare = jnp.zeros((halfway, own_points - 2 * shard_width), jnp.float32)
    unused = jnp.zeros((halfway, own_points - shard_width), jnp.float32)
    halves = (
        ([row[:halfway] for row in rows], (lag_rows[0], lag_rows[1], spare)),
        ([row[halfway:] for row in rows], (lag_rows[2], unused)),
    )
    for wave, (part, rest) in enumerate(halves):
        rest = [piece for piece in rest if piece.shape[1]]
        pair = jnp.concatenate([part[0], part[1]], axis=1)
        blocks[wave, core, cell, chip, 0] = pair.astype(jnp.bfloat16)
        pair = jnp.concatenate([part[2], *rest], axis=1)
        blocks[wave, core, cell, chip, 1] = pair.astype(jnp.bfloat16)

    def block_copy(wave, to_cell, to_chip, slot):
        return pltpu.make_async_remote_copy(
            blocks.at[wave, core, cell, chip],
            blocks.at[wave, core, cell, chip],
            block_send.at[wave, slot, to_chip],
            block_recv.at[wave, cell, chip],
            device_id={"cell": to_cell, "wall": 2 * to_chip + other_core},
            device_id_type=MESH,
        )

    def pass_copy(wave, source, at):
        return pltpu.make_async_remote_copy(
            blocks.at[wave, other_core, source, at, 1],
            passed.at[wave, source, at],
            pass_send.at[wave, source, at],
            pass_recv.at[wave, source, at],
            device_id={"wall": partner},
            device_id_type=MESH,
        )

    def mem_copy(to_cell, slot):
        return pltpu.make_async_remote_copy(
            mem_hbm,
            mem_all.at[cell],
            mem_send.at[slot],
            mem_recv.at[cell],
            device_id={"cell": to_cell, "wall": partner},
            device_id_type=MESH,
        )

    def wall_copy(given, at, to_wall):
        return pltpu.make_async_remote_copy(
            given,
            wall_all.at[wall, at],
            wall_send.at[to_wall, at],
            wall_recv.at[wall, at],
            device_id={"wall": to_wall},
            device_id_type=MESH,
        )

    def data_copy(to_wall):
        return pltpu.make_async_remote_copy(
            data_all.at[wall],
            data_all.at[wall],
            data_send.at[to_wall],
            data_recv.at[wall],
            device_id={"wall": to_wall},
            device_id_type=MESH,
        )

    def far_copies(target):
        copies = [mem_copy(target, target)]
        for wave in range(2):
            copies += [block_copy(wave, target, to, target) for to in (other_chip, chip)]
        return copies

    def near_copies():
        copies = [wall_copy(wall_hbm, 0, peer) for peer in peers]
        copies += [wall_copy(normal_hbm, 1, peer) for peer in peers]
        for wave in range(2):
            copies += [block_copy(wave, cell, to, cells) for to in (other_chip, chip)]
        return copies

    pl.semaphore_wait(barrier, walls - 1 + 2 * cell)

    for target in range(cells - 1):

        @pl.when(target < cell)
        def _(target=target):
            for copy in far_copies(target):
                copy.start()
            pl.semaphore_signal(
                ready.at[cell],
                inc=1,
                device_id={"cell": target, "wall": partner},
                device_id_type=MESH,
            )

    for copy in near_copies():
        copy.start()

    for load in loads[3:6]:
        load.wait()

    def spread_wall(source):
        for j in range(3):
            wall_cols[source, j] = jnp.broadcast_to(
                wall_all[source, 0, j : j + 1, :], (LANES, wall_count)
            ).T

    for j in range(3):
        mem_cols[j] = jnp.broadcast_to(mem_all[cell, j : j + 1, :], (LANES, point_count)).T

    lane_ids = lax.broadcasted_iota(jnp.int32, (8, LANES), 1)

    def mem_rows(source):
        rows = []
        for j in range(3):
            low = jnp.broadcast_to(mem_all[source, j : j + 1, :LANES], (8, LANES))
            high = jnp.broadcast_to(mem_all[source, j : j + 1, LANES:], (8, LANES))
            low = pltpu.roll(low, own_points * other_core, 1)
            high = pltpu.roll(high, own_points * core, 1)
            rows.append(jnp.where(lane_ids < own_points, low, high)[0:1])
        return rows

    def fill_single(source, rows, at):
        apart = [wall_cols[at, j] - rows[j] for j in range(3)]
        square = apart[0] * apart[0] + apart[1] * apart[1] + apart[2] * apart[2]
        inverse = lax.rsqrt(square)
        scaled = stokes_coef * inverse
        cube = scaled * (inverse * inverse)
        for j in range(3):
            along = apart[j] * cube
            for i in range(j + 1):
                element = along * apart[i]
                if i == j:
                    element = element + scaled
                element = element.astype(jnp.bfloat16)
                for a, b in {(i, j), (j, i)}:
                    single_all[source, at, a, :, b * LANES : (b + 1) * LANES] = element

    def fill_double(source):
        own = pl.ds(pl.multiple_of(wall * own_points, own_points), own_points)
        apart = [mem_cols[j, own, :] - wall_all[source, 0, j : j + 1, :] for j in range(3)]
        square = apart[0] * apart[0] + apart[1] * apart[1] + apart[2] * apart[2]
        inverse = lax.rsqrt(square)
        flux = (
            apart[0] * wall_all[source, 1, 0:1, :]
            + apart[1] * wall_all[source, 1, 1:2, :]
            + apart[2] * wall_all[source, 1, 2:3, :]
        )
        inverse_square = inverse * inverse
        fifth = inverse_square * inverse_square * inverse
        weight = (-6.0 * stokes_coef) * flux * fifth
        for j in range(3):
            along = apart[j] * weight
            for i in range(j + 1):
                element = (along * apart[i]).astype(jnp.bfloat16)
                for a, b in {(i, j), (j, i)}:
                    double_all[
                        source,
                        a * own_points : (a + 1) * own_points,
                        b * wall_count : (b + 1) * wall_count,
                    ] = element

    own_rows = mem_rows(cell)
    loads[6].wait()
    data_rows = [
        jnp.dot(gather_f32, data_ref[j], precision=lax.Precision.HIGHEST) for j in range(3)
    ]
    for j in range(3):
        data_all[wall, j] = data_rows[j][:halfway]
    for peer in peers:
        data_copy(peer).start()
    spread_wall(wall)
    fill_single(cell, own_rows, wall)
    fill_double(wall)

    for peer in peers:
        for at in range(2):
            pltpu.make_async_remote_copy(
                wall_all.at[peer, at],
                wall_all.at[peer, at],
                wall_send.at[peer, at],
                wall_recv.at[peer, at],
                device_id={"wall": peer},
                device_id_type=MESH,
            ).wait_recv()
        spread_wall(peer)
        fill_single(cell, own_rows, peer)
        fill_double(peer)

    for target in range(1, cells):

        @pl.when(target > cell)
        def _(target=target):
            pl.semaphore_wait(ready.at[target], 1)
            for copy in far_copies(target):
                copy.start()

    def loaded(wave, source):
        for at in range(2):
            pltpu.make_async_remote_copy(
                blocks.at[wave, other_core, source, at],
                blocks.at[wave, other_core, source, at],
                block_send.at[wave, 0, at],
                block_recv.at[wave, source, at],
                device_id={"wall": partner},
                device_id_type=MESH,
            ).wait_recv()
        for at in range(2):
            pass_copy(wave, source, at).start()
        pairs = [blocks[wave, other_core, source, at, 0] for at in range(2)]
        thirds = [blocks[wave, other_core, source, at, 1] for at in range(2)]
        pieces = [piece[:, :own_points] for piece in pairs]
        pieces += [piece[:, own_points:] for piece in pairs]
        pieces += [piece[:, :own_points] for piece in thirds]
        return jnp.concatenate(pieces, axis=1)

    def first_layer(source):
        return lax.dot_general(
            loaded(0, source),
            single_all[source].reshape(walls * block, 3 * LANES),
            NT,
            preferred_element_type=jnp.float32,
        )

    def source_at(step):
        if step == 0:
            return cell
        return jnp.where(cell + step < cells, cell + step, cells - 1 - step)

    partial = first_layer(cell)
    for step in range(1, cells):
        source = source_at(step)
        pltpu.make_async_remote_copy(
            mem_all.at[source],
            mem_all.at[source],
            mem_send.at[0],
            mem_recv.at[source],
            device_id={"wall": partner},
            device_id_type=MESH,
        ).wait_recv()
        rows = mem_rows(source)
        for at in range(walls):
            fill_single(source, rows, at)
        partial = partial + first_layer(source)
    part_mine[...] = partial

    def part_copy(given, held, at):
        return pltpu.make_async_remote_copy(
            given,
            held,
            part_send.at[at],
            part_recv.at[at],
            device_id={"wall": partner},
            device_id_type=MESH,
        )

    exchange = part_copy(part_mine, part_other, 0)
    exchange.start()

    rest = [jnp.zeros((halfway, block), jnp.float32) for _ in range(2)]
    for step in range(cells):
        source = source_at(step)
        left = loaded(1, source)
        for at, target in enumerate((wall, partner)):
            rest[at] = rest[at] + lax.dot_general(
                left,
                single_all[source, target].reshape(block, 3 * LANES),
                NT,
                preferred_element_type=jnp.float32,
            )
    rest_mine[...] = rest[1]
    rest_exchange = part_copy(rest_mine, rest_other, 1)
    rest_exchange.start()

    lag_places = ((0, own_points), (0, own_points + shard_width), (1, own_points))
    for wave in range(2):
        for source in range(cells):
            for at in range(2):
                pass_copy(wave, source, at).wait_recv()
    lag_of = {}
    for at in range(2):
        for wave, start in lag_places:
            for k in range(cells):
                direct = blocks[wave, other_core, k, at, 1, :, start : start + shard_width]
                handed = passed[wave, k, at, :, start : start + shard_width]
                lag_of.setdefault((at, 0), []).append(direct)
                lag_of.setdefault((at, 1), []).append(handed)
    total = jnp.zeros((columns, 3 * own_points), jnp.float32)
    for at in range(2):
        for mine in range(2):
            lag = jnp.concatenate(lag_of[at, mine], axis=1)
            placed = jnp.dot(scatter[:, :halfway], lag, preferred_element_type=jnp.float32)
            total = total + lax.dot_general(
                placed.astype(jnp.bfloat16),
                double_all[2 * at + (core if mine else other_core)],
                NT,
                preferred_element_type=jnp.float32,
            )

    for target in range(cells):

        @pl.when(target != cell)
        def _(target=target):
            for copy in far_copies(target):
                copy.wait_send()

    for copy in near_copies():
        copy.wait_send()
    for peer in peers:
        data_copy(peer).wait_send()
        pltpu.make_async_remote_copy(
            data_all.at[peer],
            data_all.at[peer],
            data_send.at[peer],
            data_recv.at[peer],
            device_id={"wall": peer},
            device_id_type=MESH,
        ).wait_recv()
    for wave in range(2):
        for source in range(cells):
            for at in range(2):
                pass_copy(wave, source, at).wait_send()

    exchange.wait_recv()
    for source in range(walls):
        pieces = []
        for i in range(3):
            lanes = slice(source * block + i * wall_count, source * block + (i + 1) * wall_count)
            dense = 2.0 * (data_all[source, i] - (partial[:, lanes] + part_other[:, lanes]))
            pieces.append(dense.astype(jnp.bfloat16))
        placed = jnp.dot(
            scatter[:, halfway:], jnp.concatenate(pieces, axis=1), preferred_element_type=jnp.float32
        )
        total = total + lax.dot_general(
            placed.astype(jnp.bfloat16), double_all[source], NT, preferred_element_type=jnp.float32
        )
    for i in range(3):
        out_ref[i] = total[:, i * own_points : (i + 1) * own_points]

    rest_exchange.wait_recv()
    shift = lax.rem((cells - cell) * shard_width, wall_count)
    for i in range(3):
        lanes = slice(i * wall_count, (i + 1) * wall_count)
        dense = 2.0 * (data_rows[i][halfway:] - (rest[0][:, lanes] + rest_other[:, lanes]))
        density_ref[i] = pltpu.roll(dense, shift, 1)[:, :shard_width]
    exchange.wait_send()
    rest_exchange.wait_send()


def write_kernel(velocity_ref, density_ref, velocity_hbm, density_hbm, sem):
    first = pltpu.make_async_copy(velocity_ref, velocity_hbm, sem.at[0])
    second = pltpu.make_async_copy(density_ref, density_hbm, sem.at[1])
    first.start()
    second.start()
    first.wait()
    second.wait()


def fused_shards(cells, walls, mem_pos, forces, wall_pos, wall_normal, wall_data, lag_density, batch_order):
    columns = forces.shape[0]
    halfway = columns // 2
    point_count = mem_pos.shape[1]
    wall_count = wall_pos.shape[1]
    own_points = forces.shape[2]
    shard_width = lag_density.shape[2]
    dma = pltpu.SemaphoreType.DMA
    vmem = pl.BlockSpec(memory_space=pltpu.VMEM)
    hbm = pl.BlockSpec(memory_space=pltpu.HBM)
    velocity, density = pl.pallas_call(
        functools.partial(fused_kernel, cells, walls),
        out_shape=(
            pltpu.VMEM((3, columns, own_points), jnp.float32),
            pltpu.VMEM((3, halfway, shard_width), jnp.float32),
        ),
        in_specs=[hbm] * 7,
        out_specs=(vmem, vmem),
        scratch_shapes=[
            pltpu.VMEM((1, columns), jnp.int32),
            pltpu.VMEM((3, columns, own_points), jnp.bfloat16),
            pltpu.VMEM((3, halfway, shard_width), jnp.bfloat16),
            pltpu.VMEM((3, columns, wall_count), jnp.float32),
            pltpu.VMEM((2, 2, cells, 2, 2, halfway, 2 * own_points), jnp.bfloat16),
            pltpu.VMEM((2, cells, 2, halfway, 2 * own_points), jnp.bfloat16),
            pltpu.VMEM((cells, 3, point_count), jnp.float32),
            pltpu.VMEM((walls, 2, 3, wall_count), jnp.float32),
            pltpu.VMEM((walls, 3, halfway, wall_count), jnp.float32),
            pltpu.VMEM((walls, 3, wall_count, LANES), jnp.float32),
            pltpu.VMEM((3, point_count, LANES), jnp.float32),
            pltpu.VMEM((cells, walls, 3, wall_count, 3 * LANES), jnp.bfloat16),
            pltpu.VMEM((walls, 3 * own_points, 3 * wall_count), jnp.bfloat16),
            pltpu.VMEM((halfway, walls * 3 * wall_count), jnp.float32),
            pltpu.VMEM((halfway, walls * 3 * wall_count), jnp.float32),
            pltpu.VMEM((halfway, 3 * wall_count), jnp.float32),
            pltpu.VMEM((halfway, 3 * wall_count), jnp.float32),
            dma((7,)),
            dma((2, cells + 1, 2)),
            dma((2, cells, 2)),
            dma((2, cells, 2)),
            dma((2, cells, 2)),
            dma((cells,)),
            dma((cells,)),
            dma((walls, 2)),
            dma((walls, 2)),
            dma((walls,)),
            dma((walls,)),
            dma((2,)),
            dma((2,)),
            pltpu.SemaphoreType.REGULAR((cells,)),
        ],
        compiler_params=pltpu.CompilerParams(
            collective_id=0, has_side_effects=True, vmem_limit_bytes=VMEM_GRANT
        ),
        name="coupling",
    )(
        mem_pos,
        jnp.transpose(forces, (1, 0, 2)),
        wall_pos,
        wall_normal,
        jnp.transpose(wall_data, (1, 0, 2)),
        jnp.transpose(lag_density, (1, 0, 2)),
        batch_order.reshape(1, columns),
    )
    velocity, density = pl.pallas_call(
        write_kernel,
        out_shape=(
            jax.ShapeDtypeStruct(velocity.shape, velocity.dtype),
            jax.ShapeDtypeStruct(density.shape, density.dtype),
        ),
        in_specs=[vmem] * 2,
        out_specs=(hbm, hbm),
        scratch_shapes=[dma((2,))],
        compiler_params=pltpu.CompilerParams(vmem_limit_bytes=1024 * 1024),
        name="write",
    )(velocity, density)
    return (jnp.transpose(velocity, (1, 0, 2)), jnp.transpose(density, (1, 0, 2)))


VMEM_GRANT = 60 * 1024 * 1024


def step(cells, walls, mem_pos, forces, wall_pos, *rest):
    point_count = mem_pos.shape[1]
    wall_count = wall_pos.shape[1]
    own_points = forces.shape[2]
    shard_width = rest[2].shape[2]
    tiles = 18 * walls * wall_count * (cells * LANES + own_points)
    fits = tiles <= VMEM_GRANT // 2
    aligned = (
        walls == 4
        and wall_count == LANES
        and 2 * own_points == LANES
        and point_count == walls * own_points
        and wall_count == cells * shard_width
        and 2 * shard_width <= own_points
    )
    if fits and aligned:
        return fused_shards(cells, walls, mem_pos, forces, wall_pos, *rest)
    return shards(mem_pos, forces, wall_pos, *rest)


def solution(mesh):
    placed = (
        P(None, ("groups", "cell")),
        P(None, None, ("groups", "cell", "wall")),
        P(None, ("groups", "wall")),
        P(None, ("groups", "wall")),
        P(None, None, ("groups", "wall")),
        P(None, None, ("groups", "wall", "cell")),
        P(),
    )
    return jax.shard_map(
        functools.partial(step, mesh.shape["cell"], mesh.shape["wall"]),
        mesh=mesh,
        in_specs=placed,
        out_specs=(
            P(None, None, ("groups", "cell", "wall")),
            P(None, None, ("groups", "wall", "cell")),
        ),
        check_vma=False,
    )
```

```python
import functools
import math

import jax
import jax.numpy as jnp
from jax import lax
from jax.experimental import pallas as pl
from jax.experimental.pallas import tpu as pltpu
from jax.sharding import PartitionSpec as P

stokes_coef = 1.0 / (8.0 * math.pi)


def single_tile(targets, sources):
    separation = targets[:, None, :] - sources[:, :, None]
    inverse = lax.rsqrt(jnp.sum(separation * separation, axis=0))
    inverse_cube = inverse * inverse * inverse
    stacked = []
    for second_dim in range(3):
        entries_row = []
        for first_dim in range(3):
            element = separation[first_dim] * separation[second_dim] * inverse_cube
            if first_dim == second_dim:
                element = element + inverse
            entries_row.append(element * stokes_coef)
        stacked.append(jnp.stack(entries_row, axis=1))
    kernel_tile = jnp.stack(stacked, axis=0)
    return kernel_tile.reshape(3 * sources.shape[1], 3 * targets.shape[1]).astype(jnp.bfloat16)


def double_tile(targets, sources, normals):
    separation = targets[:, None, :] - sources[:, :, None]
    inverse = lax.rsqrt(jnp.sum(separation * separation, axis=0))
    normal_flux = jnp.sum(separation * normals[:, :, None], axis=0)
    weight = -6.0 * stokes_coef * normal_flux * inverse**5
    stacked = []
    for second_dim in range(3):
        entries_row = []
        for first_dim in range(3):
            entries_row.append(weight * separation[first_dim] * separation[second_dim])
        stacked.append(jnp.stack(entries_row, axis=1))
    kernel_tile = jnp.stack(stacked, axis=0)
    return kernel_tile.reshape(3 * sources.shape[1], 3 * targets.shape[1]).astype(jnp.bfloat16)


def shards(mem_pos, forces, wall_pos, wall_normal, wall_data, lag_density, batch_order):
    columns = forces.shape[0]
    halfway = columns // 2
    point_count = mem_pos.shape[1]
    wall_count = wall_pos.shape[1]
    shard_width = lag_density.shape[2]
    piece_len = math.gcd(point_count, 128)
    block_count = point_count // piece_len
    first_rows = batch_order[:halfway]
    second_rows = batch_order[halfway:]
    force_block = lax.all_gather(forces, "wall", axis=2, tiled=True)
    lag_block = lax.all_gather(lag_density, "cell", axis=2, tiled=True)
    lag_flat = lag_block.reshape(halfway, 3 * wall_count)

    def position_at(block_index):
        return lax.dynamic_slice_in_dim(mem_pos, block_index * piece_len, piece_len, 1)

    def single_term(block_index):
        loaded = lax.dynamic_slice_in_dim(force_block, block_index * piece_len, piece_len, 2)
        loaded = loaded.reshape(columns, 3 * piece_len)
        return jnp.dot(
            loaded,
            single_tile(wall_pos, position_at(block_index)),
            preferred_element_type=jnp.float32,
        )

    def double_term(dense_rows, block_index):
        kernel_tile = double_tile(position_at(block_index), wall_pos, wall_normal)
        product = jnp.dot(dense_rows, kernel_tile, preferred_element_type=jnp.float32)
        return product.reshape(dense_rows.shape[0], 3, piece_len)

    def place_block(target, piece, block_index):
        return lax.dynamic_update_slice_in_dim(target, piece, block_index * piece_len, 2)

    empty_wall = jnp.zeros((columns, 3 * wall_count), jnp.float32)

    def add_single(block_index, running):
        return running + single_term(block_index)

    running = lax.fori_loop(0, block_count, add_single, empty_wall)
    wall_term = running.reshape(columns, 3, wall_count)
    position_cell = lax.axis_index("cell")
    first_sum = lax.psum(jnp.take(wall_term, first_rows, axis=0), "cell")
    first_block = (2.0 * (jnp.take(wall_data, first_rows, axis=0) - first_sum)).astype(jnp.bfloat16)
    second_sum = lax.psum_scatter(
        jnp.take(wall_term, second_rows, axis=0).astype(jnp.bfloat16),
        "cell",
        scatter_dimension=2,
        tiled=True,
    ).astype(jnp.float32)
    second_data = lax.dynamic_slice_in_dim(
        jnp.take(wall_data, second_rows, axis=0), position_cell * shard_width, shard_width, 2
    )
    wall_density = 2.0 * (second_data - second_sum)
    first_flat = first_block.reshape(halfway, 3 * wall_count)
    carried = jnp.concatenate([lag_flat, first_flat], axis=0)

    def all_terms(block_index, target):
        return place_block(target, double_term(carried, block_index), block_index)

    membrane_term = lax.fori_loop(
        0, block_count, all_terms, jnp.zeros((columns, 3, point_count), jnp.float32)
    )
    batched = lax.psum_scatter(membrane_term, "wall", scatter_dimension=2, tiled=True)
    membrane_velocity = jnp.zeros_like(batched).at[batch_order].set(batched)
    return (membrane_velocity, wall_density)

LANES = 128
MESH = pl.DeviceIdType.MESH
NT = (((1,), (1,)), ((), ()))


def fused_kernel(
    cells,
    walls,
    mem_hbm,
    force_hbm,
    wall_hbm,
    normal_hbm,
    data_hbm,
    lag_hbm,
    order_hbm,
    out_ref,
    density_ref,
    order_ref,
    order_smem,
    force_ref,
    lag_ref,
    data_ref,
    own_block,
    own_lag,
    block_all,
    second_all,
    lag_all,
    lag_pass,
    mem_all,
    wall_all,
    data_all,
    wall_cols,
    mem_cols,
    single_all,
    single_rest,
    double_all,
    part_mine,
    part_other,
    share_out,
    share_in,
    load_sem,
    block_send,
    block_recv,
    second_send,
    second_recv,
    lag_send,
    lag_recv,
    pass_send,
    pass_recv,
    mem_send,
    mem_recv,
    wall_send,
    wall_recv,
    data_send,
    data_recv,
    part_send,
    part_recv,
    share_send,
    share_recv,
    ready,
    ready_near,
):
    cell = lax.axis_index("cell")
    wall = lax.axis_index("wall")
    chip = lax.div(wall, 2)
    core = lax.rem(wall, 2)
    other_core = 1 - core
    other_chip = 1 - chip
    columns = order_ref.shape[1]
    halfway = columns // 2
    point_count = mem_hbm.shape[1]
    wall_count = wall_hbm.shape[1]
    own_points = force_ref.shape[2]
    shard_width = lag_ref.shape[2]
    block = 3 * wall_count
    partner = 2 * chip + other_core

    loads = [
        pltpu.make_async_copy(given, held, load_sem.at[at])
        for at, (given, held) in enumerate(
            (
                (order_hbm, order_smem),
                (order_hbm, order_ref),
                (force_hbm, force_ref),
                (lag_hbm, lag_ref),
                (mem_hbm, mem_all.at[cell]),
                (wall_hbm, wall_all.at[wall, 0]),
                (normal_hbm, wall_all.at[wall, 1]),
                (data_hbm, data_ref),
            )
        )
    ]
    for load in loads:
        load.start()

    barrier = pltpu.get_barrier_semaphore()
    for to_cell in range(cells - 1, -1, -1):
        for to_wall in range(walls):

            @pl.when((to_cell > cell) | ((to_cell == cell) & (to_wall > wall)))
            def _(to_cell=to_cell, to_wall=to_wall):
                pl.semaphore_signal(
                    barrier,
                    inc=1,
                    device_id={"cell": to_cell, "wall": to_wall},
                    device_id_type=MESH,
                )

    below = walls * cell + wall

    @pl.when(below > 0)
    def _():
        pl.semaphore_wait(barrier, below)

    for to_cell in range(cells - 1):
        for to_wall in range(walls):

            @pl.when(to_cell < cell)
            def _(to_cell=to_cell, to_wall=to_wall):
                pl.semaphore_signal(
                    ready.at[cell],
                    inc=1,
                    device_id={"cell": to_cell, "wall": to_wall},
                    device_id_type=MESH,
                )

    for to_wall in range(walls - 1):

        @pl.when(to_wall < wall)
        def _(to_wall=to_wall):
            pl.semaphore_signal(
                ready_near.at[wall], inc=1, device_id={"wall": to_wall}, device_id_type=MESH
            )

    def remote(given, held, send, recv, **to):
        return pltpu.make_async_remote_copy(
            given, held, send, recv, device_id=to, device_id_type=MESH
        )

    def block_copy(to_cell, to_chip):
        return remote(
            own_block,
            block_all.at[cell, chip],
            block_send,
            block_recv.at[cell],
            cell=to_cell,
            wall=2 * to_chip + other_core,
        )

    def lag_copy(to_cell, to_chip):
        return remote(
            own_lag,
            lag_all.at[cell, chip],
            lag_send,
            lag_recv,
            cell=to_cell,
            wall=2 * to_chip + other_core,
        )

    def mem_copy(to_cell):
        return remote(
            mem_hbm,
            mem_all.at[cell],
            mem_send,
            mem_recv.at[cell],
            cell=to_cell,
            wall=partner,
        )

    def share_copy(to_cell):
        return remote(
            share_out.at[to_cell],
            share_in.at[cell],
            share_send,
            share_recv,
            cell=to_cell,
        )

    def wall_copies(to_wall):
        return [
            remote(
                given,
                wall_all.at[wall, at],
                wall_send,
                wall_recv.at[wall],
                wall=to_wall,
            )
            for at, given in enumerate((wall_hbm, normal_hbm))
        ]

    def second_copy(to_wall):
        held = second_all.at[wall]
        return remote(
            held, held, second_send, second_recv, wall=to_wall
        )

    def data_copy(to_wall):
        held = data_all.at[wall]
        return remote(held, held, data_send, data_recv, wall=to_wall)

    def near_walls(body):
        for to_wall in range(walls):

            @pl.when(to_wall != wall)
            def _(to_wall=to_wall):
                body(to_wall)

    def far_cells(test, body):
        for to_cell in range(cells):

            @pl.when(test(to_cell))
            def _(to_cell=to_cell):
                body(to_cell)

    def start_blocks(to_cell):
        for to_chip in (other_chip, chip):
            block_copy(to_cell, to_chip).start()

    def start_lag(to_cell):
        for to_chip in (other_chip, chip):
            lag_copy(to_cell, to_chip).start()

    for to_wall in range(walls):

        @pl.when(to_wall < wall)
        def _(to_wall=to_wall):
            for copy in wall_copies(to_wall):
                copy.start()

    far_cells(lambda to_cell: to_cell < cell, lambda to_cell: mem_copy(to_cell).start())

    row_ids = lax.broadcasted_iota(jnp.int32, (columns, columns), 0)
    col_ids = lax.broadcasted_iota(jnp.int32, (columns, columns), 1)
    loads[0].wait()
    wanted = jnp.zeros((columns, columns), jnp.int32)
    for k in range(columns):
        wanted = jnp.where(row_ids == k, order_smem[0, k], wanted)
    gather_f32 = (wanted == col_ids).astype(jnp.float32)
    gather = gather_f32.astype(jnp.bfloat16)

    loads[2].wait()
    rows = [jnp.dot(gather, force_ref[j], preferred_element_type=jnp.float32) for j in range(3)]
    folded = halfway // 2
    part = [row[:halfway] for row in rows]
    pair = jnp.concatenate([part[0], part[1]], axis=1)
    last = jnp.concatenate([part[2][:folded], part[2][folded:]], axis=1)
    own_block[...] = jnp.concatenate([pair, last], axis=0).astype(jnp.bfloat16)

    far_cells(lambda to_cell: to_cell < cell, start_blocks)

    part = [row[halfway:] for row in rows]
    unused = jnp.zeros((halfway, LANES - own_points), jnp.float32)
    second_all[wall, 0] = jnp.concatenate([part[0], part[1]], axis=1).astype(jnp.bfloat16)
    second_all[wall, 1] = jnp.concatenate([part[2], unused], axis=1).astype(jnp.bfloat16)

    loads[3].wait()
    pieces = [lag_ref[j].astype(jnp.float32) for j in range(3)]
    if LANES > 3 * shard_width:
        pieces.append(jnp.zeros((halfway, LANES - 3 * shard_width), jnp.float32))
    own_lag[...] = jnp.concatenate(pieces, axis=1).astype(jnp.bfloat16)

    far_cells(lambda to_cell: to_cell < cell, start_lag)

    def start_near(to_wall):
        @pl.when(to_wall > wall)
        def _():
            pl.semaphore_wait(ready_near.at[to_wall], 1)
            for copy in wall_copies(to_wall):
                copy.start()

        @pl.when(to_wall % 2 != core)
        def _():
            block_copy(cell, to_wall // 2).start()

        second_copy(to_wall).start()

        @pl.when(to_wall % 2 != core)
        def _():
            lag_copy(cell, to_wall // 2).start()


    near_walls(start_near)

    for load in loads[4:]:
        load.wait()
    data_rows = [
        jnp.dot(gather_f32, data_ref[j], precision=lax.Precision.HIGHEST) for j in range(3)
    ]
    for j in range(3):
        data_all[wall, j] = data_rows[j][:halfway]
    near_walls(lambda to_wall: data_copy(to_wall).start())

    loads[1].wait()
    scatter = (row_ids == order_ref[...]).astype(jnp.float32).astype(jnp.bfloat16)

    def spread_wall(source):
        for j in range(3):
            wall_cols[source, j] = jnp.broadcast_to(
                wall_all[source, 0, j : j + 1, :], (LANES, wall_count)
            ).T

    for j in range(3):
        mem_cols[j] = jnp.broadcast_to(mem_all[cell, j : j + 1, :], (LANES, point_count)).T

    lane_ids = lax.broadcasted_iota(jnp.int32, (8, LANES), 1)

    def mem_rows(source, parity):
        rows = []
        for j in range(3):
            low = jnp.broadcast_to(mem_all[source, j : j + 1, :LANES], (8, LANES))
            high = jnp.broadcast_to(mem_all[source, j : j + 1, LANES:], (8, LANES))
            low = pltpu.roll(low, own_points * parity, 1)
            high = pltpu.roll(high, own_points * (1 - parity), 1)
            rows.append(jnp.where(lane_ids < own_points, low, high)[0:1])
        return rows

    def fill_single(tile, rows, at):
        apart = [wall_cols[at, j] - rows[j] for j in range(3)]
        square = apart[0] * apart[0] + apart[1] * apart[1] + apart[2] * apart[2]
        inverse = lax.rsqrt(square)
        scaled = stokes_coef * inverse
        cube = scaled * (inverse * inverse)
        for j in range(3):
            along = apart[j] * cube
            for i in range(j + 1):
                element = along * apart[i]
                if i == j:
                    element = element + scaled
                element = element.astype(jnp.bfloat16)
                for a, b in {(i, j), (j, i)}:
                    tile[a, :, b * LANES : (b + 1) * LANES] = element

    def fill_double(source):
        own = pl.ds(pl.multiple_of(wall * own_points, own_points), own_points)
        apart = [mem_cols[j, own, :] - wall_all[source, 0, j : j + 1, :] for j in range(3)]
        square = apart[0] * apart[0] + apart[1] * apart[1] + apart[2] * apart[2]
        inverse = lax.rsqrt(square)
        flux = (
            apart[0] * wall_all[source, 1, 0:1, :]
            + apart[1] * wall_all[source, 1, 1:2, :]
            + apart[2] * wall_all[source, 1, 2:3, :]
        )
        inverse_square = inverse * inverse
        fifth = inverse_square * inverse_square * inverse
        weight = (-6.0 * stokes_coef) * flux * fifth
        for j in range(3):
            along = apart[j] * weight
            for i in range(j + 1):
                element = (along * apart[i]).astype(jnp.bfloat16)
                for a, b in {(i, j), (j, i)}:
                    lanes = pl.multiple_of(source * block + b * wall_count, wall_count)
                    double_all[
                        a * own_points : (a + 1) * own_points, pl.ds(lanes, wall_count)
                    ] = element

    own_rows = mem_rows(cell, other_core)
    spread_wall(wall)
    fill_single(single_all.at[cell, wall], own_rows, wall)
    fill_single(single_rest, mem_rows(cell, core), wall)
    fill_double(wall)

    def wait_into(held, recv):
        remote(held, held, load_sem.at[0], recv, wall=partner).wait_recv()

    def wait_out(held, send):
        remote(held, held, send, load_sem.at[0], wall=partner).wait_send()

    peers = (partner, 2 * other_chip + other_core, 2 * other_chip + core)

    def take_wall(peer):
        wait_into(wall_all.at[peer], wall_recv.at[peer])
        spread_wall(peer)
        fill_single(single_all.at[cell, peer], own_rows, peer)
        fill_double(peer)

    def start_above(up):
        def body(to_cell):
            pl.semaphore_wait(ready.at[to_cell], walls)
            mem_copy(to_cell).start()
            start_blocks(to_cell)
            start_lag(to_cell)

        far_cells(lambda to_cell: to_cell == cell + up, body)

    def second_columns(tiles):
        pieces = [tile[0][:, :own_points] for tile in tiles]
        pieces += [tile[0][:, own_points:] for tile in tiles]
        pieces += [tile[1][:, :own_points] for tile in tiles]
        return jnp.concatenate(pieces, axis=1)

    def columns_of(tiles):
        tiles = [tile.astype(jnp.float32) for tile in tiles]
        pieces = [tile[:halfway, :own_points] for tile in tiles]
        pieces += [tile[:halfway, own_points:] for tile in tiles]
        for tile in tiles:
            last = tile[halfway:]
            pieces.append(jnp.concatenate([last[:, :own_points], last[:, own_points:]], axis=0))
        return jnp.concatenate(pieces, axis=1).astype(jnp.bfloat16)

    take_wall(partner)
    start_above(1)
    take_wall(peers[1])
    for up in range(2, cells - 1):
        start_above(up)

    wait_into(second_all.at[: walls - 1], second_recv)
    share = jnp.zeros((halfway, block), jnp.float32)
    for parity, tile in ((other_core, single_all.at[cell, wall]), (core, single_rest)):
        share = share + lax.dot_general(
            second_columns([second_all[2 * at + parity] for at in range(2)]),
            tile[...].reshape(block, 3 * LANES),
            NT,
            preferred_element_type=jnp.float32,
        )
    own_share = jnp.zeros((halfway, LANES), jnp.float32)
    for to_cell in range(cells):
        pieces = [
            share[:, i * wall_count + to_cell * shard_width :][:, :shard_width] for i in range(3)
        ]
        if LANES > 3 * shard_width:
            pieces.append(jnp.zeros((halfway, LANES - 3 * shard_width), jnp.float32))
        piece = jnp.concatenate(pieces, axis=1)
        own_share = jnp.where(cell == to_cell, piece, own_share)
        share_out[to_cell] = piece.astype(jnp.bfloat16)
    far_cells(lambda to_cell: to_cell < cell, lambda to_cell: share_copy(to_cell).start())
    if cells > 2:
        start_above(cells - 1)
    far_cells(lambda to_cell: to_cell > cell, lambda to_cell: share_copy(to_cell).start())
    take_wall(peers[2])

    def source_at(step):
        if step == 0:
            return cell
        return jnp.where(cell + step < cells, cell + step, cells - 1 - step)

    def take_mem(step):
        source = source_at(step)
        wait_into(mem_all.at[source], mem_recv.at[source])
        rows = mem_rows(source, other_core)
        for at in range(walls):
            fill_single(single_all.at[source, at], rows, at)

    def first_layer(step):
        source = source_at(step)
        wait_into(block_all.at[source], block_recv.at[source])
        left = columns_of([block_all[source, at] for at in range(2)])
        return lax.dot_general(
            left,
            single_all[source].reshape(walls * block, 3 * LANES),
            NT,
            preferred_element_type=jnp.float32,
        )

    partial = jnp.zeros((halfway, walls * block), jnp.float32)
    for step in range(cells):
        if step + 1 < cells:
            take_mem(step + 1)
        partial = partial + first_layer(step)
    part_mine[...] = partial
    exchange = remote(part_mine, part_other, part_send, part_recv, wall=partner)
    exchange.start()

    wait_into(lag_all, lag_recv)
    handing = remote(lag_all, lag_pass, pass_send, pass_recv, wall=partner)
    handing.start()

    wait_out(mem_all.at[: cells - 1], mem_send)
    wait_out(block_all, block_send)
    wait_out(lag_all, lag_send)
    wait_out(wall_all.at[: walls - 1], wall_send)
    wait_out(second_all.at[: walls - 1], second_send)
    wait_into(data_all.at[: walls - 1], data_recv)
    wait_out(data_all.at[: walls - 1], data_send)
    wait_out(share_in.at[: cells - 1], share_send)

    def layer(rows):
        return lax.dot_general(rows, double_all[...], NT, preferred_element_type=jnp.float32)

    handing.wait_recv()
    lag_row = []
    for at in range(2):
        for parity in range(2):
            lag_row += [
                jnp.where(core == parity, lag_pass[k, at], lag_all[k, at])[
                    :, j * shard_width : (j + 1) * shard_width
                ]
                for j in range(3)
                for k in range(cells)
            ]
    lag_part = layer(jnp.concatenate(lag_row, axis=1))

    exchange.wait_recv()
    pieces = []
    for source in range(walls):
        for i in range(3):
            lanes = slice(source * block + i * wall_count, source * block + (i + 1) * wall_count)
            dense = 2.0 * (data_all[source, i] - (part_mine[:, lanes] + part_other[:, lanes]))
            pieces.append(dense.astype(jnp.bfloat16))
    batched = jnp.concatenate([lag_part, layer(jnp.concatenate(pieces, axis=1))], axis=0)
    total = jnp.zeros((columns, 3 * own_points), jnp.float32)
    for _ in range(3):
        piece = batched.astype(jnp.bfloat16)
        total = total + jnp.dot(scatter, piece, preferred_element_type=jnp.float32)
        batched = batched - piece.astype(jnp.float32)
    for i in range(3):
        out_ref[i] = total[:, i * own_points : (i + 1) * own_points]

    wait_into(share_in.at[: cells - 1], share_recv)
    second_sum = own_share
    for step in range(1, cells):
        second_sum = second_sum + share_in[source_at(step)].astype(jnp.float32)
    shift = lax.rem((cells - cell) * shard_width, wall_count)
    for i in range(3):
        held = pltpu.roll(data_rows[i][halfway:], shift, 1)[:, :shard_width]
        density_ref[i] = 2.0 * (held - second_sum[:, i * shard_width : (i + 1) * shard_width])

    exchange.wait_send()
    handing.wait_send()


def write_kernel(velocity_ref, density_ref, velocity_hbm, density_hbm, sem):
    first = pltpu.make_async_copy(velocity_ref, velocity_hbm, sem.at[0])
    second = pltpu.make_async_copy(density_ref, density_hbm, sem.at[1])
    first.start()
    second.start()
    first.wait()
    second.wait()


def fused_shards(cells, walls, mem_pos, forces, wall_pos, wall_normal, wall_data, lag_density, batch_order):
    columns = forces.shape[0]
    halfway = columns // 2
    point_count = mem_pos.shape[1]
    wall_count = wall_pos.shape[1]
    own_points = forces.shape[2]
    shard_width = lag_density.shape[2]
    dma = pltpu.SemaphoreType.DMA
    vmem = pl.BlockSpec(memory_space=pltpu.VMEM)
    hbm = pl.BlockSpec(memory_space=pltpu.HBM)
    velocity, density = pl.pallas_call(
        functools.partial(fused_kernel, cells, walls),
        out_shape=(
            pltpu.VMEM((3, columns, own_points), jnp.float32),
            pltpu.VMEM((3, halfway, shard_width), jnp.float32),
        ),
        in_specs=[hbm] * 7,
        out_specs=(vmem, vmem),
        scratch_shapes=[
            pltpu.VMEM((1, columns), jnp.int32),
            pltpu.SMEM((1, columns), jnp.int32),
            pltpu.VMEM((3, columns, own_points), jnp.bfloat16),
            pltpu.VMEM((3, halfway, shard_width), jnp.bfloat16),
            pltpu.VMEM((3, columns, wall_count), jnp.float32),
            pltpu.VMEM((3 * halfway // 2, LANES), jnp.bfloat16),
            pltpu.VMEM((halfway, LANES), jnp.bfloat16),
            pltpu.VMEM((cells, 2, 3 * halfway // 2, LANES), jnp.bfloat16),
            pltpu.VMEM((walls, 2, halfway, LANES), jnp.bfloat16),
            pltpu.VMEM((cells, 2, halfway, LANES), jnp.bfloat16),
            pltpu.VMEM((cells, 2, halfway, LANES), jnp.bfloat16),
            pltpu.VMEM((cells, 3, point_count), jnp.float32),
            pltpu.VMEM((walls, 2, 3, wall_count), jnp.float32),
            pltpu.VMEM((walls, 3, halfway, wall_count), jnp.float32),
            pltpu.VMEM((walls, 3, wall_count, LANES), jnp.float32),
            pltpu.VMEM((3, point_count, LANES), jnp.float32),
            pltpu.VMEM((cells, walls, 3, wall_count, 3 * LANES), jnp.bfloat16),
            pltpu.VMEM((3, wall_count, 3 * LANES), jnp.bfloat16),
            pltpu.VMEM((3 * own_points, walls * 3 * wall_count), jnp.bfloat16),
            pltpu.VMEM((halfway, walls * 3 * wall_count), jnp.float32),
            pltpu.VMEM((halfway, walls * 3 * wall_count), jnp.float32),
            pltpu.VMEM((cells, halfway, LANES), jnp.bfloat16),
            pltpu.VMEM((cells, halfway, LANES), jnp.bfloat16),
            dma((8,)),
            dma,
            dma((cells,)),
            dma,
            dma,
            dma,
            dma,
            dma,
            dma,
            dma,
            dma((cells,)),
            dma,
            dma((walls,)),
            dma,
            dma,
            dma,
            dma,
            dma,
            dma,
            pltpu.SemaphoreType.REGULAR((cells,)),
            pltpu.SemaphoreType.REGULAR((walls,)),
        ],
        compiler_params=pltpu.CompilerParams(
            collective_id=0, has_side_effects=True, vmem_limit_bytes=VMEM_GRANT
        ),
        name="coupling",
    )(
        mem_pos,
        jnp.transpose(forces, (1, 0, 2)),
        wall_pos,
        wall_normal,
        jnp.transpose(wall_data, (1, 0, 2)),
        jnp.transpose(lag_density, (1, 0, 2)),
        batch_order.reshape(1, columns),
    )
    velocity, density = pl.pallas_call(
        write_kernel,
        out_shape=(
            jax.ShapeDtypeStruct(velocity.shape, velocity.dtype),
            jax.ShapeDtypeStruct(density.shape, density.dtype),
        ),
        in_specs=[vmem] * 2,
        out_specs=(hbm, hbm),
        scratch_shapes=[dma((2,))],
        compiler_params=pltpu.CompilerParams(vmem_limit_bytes=1024 * 1024),
        name="write",
    )(velocity, density)
    return (jnp.transpose(velocity, (1, 0, 2)), jnp.transpose(density, (1, 0, 2)))


VMEM_GRANT = 60 * 1024 * 1024


def step(cells, walls, mem_pos, forces, wall_pos, *rest):
    point_count = mem_pos.shape[1]
    wall_count = wall_pos.shape[1]
    own_points = forces.shape[2]
    shard_width = rest[2].shape[2]
    tiles = 18 * walls * wall_count * (cells * LANES + own_points)
    fits = tiles <= VMEM_GRANT // 2
    aligned = (
        walls == 4
        and wall_count == LANES
        and 2 * own_points == LANES
        and point_count == walls * own_points
        and wall_count == cells * shard_width
        and 3 * shard_width <= LANES
    )
    if fits and aligned:
        return fused_shards(cells, walls, mem_pos, forces, wall_pos, *rest)
    return shards(mem_pos, forces, wall_pos, *rest)


def solution(mesh):
    placed = (
        P(None, ("groups", "cell")),
        P(None, None, ("groups", "cell", "wall")),
        P(None, ("groups", "wall")),
        P(None, ("groups", "wall")),
        P(None, None, ("groups", "wall")),
        P(None, None, ("groups", "wall", "cell")),
        P(),
    )
    return jax.shard_map(
        functools.partial(step, mesh.shape["cell"], mesh.shape["wall"]),
        mesh=mesh,
        in_specs=placed,
        out_specs=(
            P(None, None, ("groups", "cell", "wall")),
            P(None, None, ("groups", "wall", "cell")),
        ),
        check_vma=False,
    )
```

```python
import functools
import math

import jax
import jax.numpy as jnp
from jax import lax
from jax.experimental import pallas as pl
from jax.experimental.pallas import tpu as pltpu
from jax.sharding import PartitionSpec as P

stokes_coef = 1.0 / (8.0 * math.pi)


def single_tile(targets, sources):
    separation = targets[:, None, :] - sources[:, :, None]
    inverse = lax.rsqrt(jnp.sum(separation * separation, axis=0))
    inverse_cube = inverse * inverse * inverse
    stacked = []
    for second_dim in range(3):
        entries_row = []
        for first_dim in range(3):
            element = separation[first_dim] * separation[second_dim] * inverse_cube
            if first_dim == second_dim:
                element = element + inverse
            entries_row.append(element * stokes_coef)
        stacked.append(jnp.stack(entries_row, axis=1))
    kernel_tile = jnp.stack(stacked, axis=0)
    return kernel_tile.reshape(3 * sources.shape[1], 3 * targets.shape[1]).astype(jnp.bfloat16)


def double_tile(targets, sources, normals):
    separation = targets[:, None, :] - sources[:, :, None]
    inverse = lax.rsqrt(jnp.sum(separation * separation, axis=0))
    normal_flux = jnp.sum(separation * normals[:, :, None], axis=0)
    weight = -6.0 * stokes_coef * normal_flux * inverse**5
    stacked = []
    for second_dim in range(3):
        entries_row = []
        for first_dim in range(3):
            entries_row.append(weight * separation[first_dim] * separation[second_dim])
        stacked.append(jnp.stack(entries_row, axis=1))
    kernel_tile = jnp.stack(stacked, axis=0)
    return kernel_tile.reshape(3 * sources.shape[1], 3 * targets.shape[1]).astype(jnp.bfloat16)


def shards(mem_pos, forces, wall_pos, wall_normal, wall_data, lag_density, batch_order):
    columns = forces.shape[0]
    halfway = columns // 2
    point_count = mem_pos.shape[1]
    wall_count = wall_pos.shape[1]
    shard_width = lag_density.shape[2]
    piece_len = math.gcd(point_count, 128)
    block_count = point_count // piece_len
    first_rows = batch_order[:halfway]
    second_rows = batch_order[halfway:]
    force_block = lax.all_gather(forces, "wall", axis=2, tiled=True)
    lag_block = lax.all_gather(lag_density, "cell", axis=2, tiled=True)
    lag_flat = lag_block.reshape(halfway, 3 * wall_count)

    def position_at(block_index):
        return lax.dynamic_slice_in_dim(mem_pos, block_index * piece_len, piece_len, 1)

    def single_term(block_index):
        loaded = lax.dynamic_slice_in_dim(force_block, block_index * piece_len, piece_len, 2)
        loaded = loaded.reshape(columns, 3 * piece_len)
        return jnp.dot(
            loaded,
            single_tile(wall_pos, position_at(block_index)),
            preferred_element_type=jnp.float32,
        )

    def double_term(dense_rows, block_index):
        kernel_tile = double_tile(position_at(block_index), wall_pos, wall_normal)
        product = jnp.dot(dense_rows, kernel_tile, preferred_element_type=jnp.float32)
        return product.reshape(dense_rows.shape[0], 3, piece_len)

    def place_block(target, piece, block_index):
        return lax.dynamic_update_slice_in_dim(target, piece, block_index * piece_len, 2)

    empty_wall = jnp.zeros((columns, 3 * wall_count), jnp.float32)

    def add_single(block_index, running):
        return running + single_term(block_index)

    running = lax.fori_loop(0, block_count, add_single, empty_wall)
    wall_term = running.reshape(columns, 3, wall_count)
    position_cell = lax.axis_index("cell")
    first_sum = lax.psum(jnp.take(wall_term, first_rows, axis=0), "cell")
    first_block = (2.0 * (jnp.take(wall_data, first_rows, axis=0) - first_sum)).astype(jnp.bfloat16)
    second_sum = lax.psum_scatter(
        jnp.take(wall_term, second_rows, axis=0).astype(jnp.bfloat16),
        "cell",
        scatter_dimension=2,
        tiled=True,
    ).astype(jnp.float32)
    second_data = lax.dynamic_slice_in_dim(
        jnp.take(wall_data, second_rows, axis=0), position_cell * shard_width, shard_width, 2
    )
    wall_density = 2.0 * (second_data - second_sum)
    first_flat = first_block.reshape(halfway, 3 * wall_count)
    carried = jnp.concatenate([lag_flat, first_flat], axis=0)

    def all_terms(block_index, target):
        return place_block(target, double_term(carried, block_index), block_index)

    membrane_term = lax.fori_loop(
        0, block_count, all_terms, jnp.zeros((columns, 3, point_count), jnp.float32)
    )
    batched = lax.psum_scatter(membrane_term, "wall", scatter_dimension=2, tiled=True)
    membrane_velocity = jnp.zeros_like(batched).at[batch_order].set(batched)
    return (membrane_velocity, wall_density)

LANES = 128
MESH = pl.DeviceIdType.MESH
NT = (((1,), (1,)), ((), ()))


def fused_kernel(
    cells,
    walls,
    mem_hbm,
    force_hbm,
    wall_hbm,
    normal_hbm,
    data_hbm,
    lag_hbm,
    order_hbm,
    out_ref,
    density_ref,
    order_ref,
    order_smem,
    force_ref,
    lag_ref,
    data_ref,
    own_block,
    own_lag,
    block_all,
    second_all,
    lag_all,
    mem_all,
    wall_all,
    data_all,
    wall_cols,
    mem_cols,
    single_all,
    single_rest,
    double_all,
    part_mine,
    part_other,
    share_out,
    share_in,
    load_sem,
    block_send,
    block_recv,
    second_send,
    second_recv,
    lag_send,
    lag_recv,
    mem_send,
    mem_recv,
    wall_send,
    wall_recv,
    data_send,
    data_recv,
    part_send,
    part_recv,
    share_send,
    share_recv,
    ready,
    ready_near,
):
    cell = lax.axis_index("cell")
    wall = lax.axis_index("wall")
    chip = lax.div(wall, 2)
    core = lax.rem(wall, 2)
    other_core = 1 - core
    other_chip = 1 - chip
    columns = order_ref.shape[1]
    halfway = columns // 2
    point_count = mem_hbm.shape[1]
    wall_count = wall_hbm.shape[1]
    own_points = force_ref.shape[2]
    shard_width = lag_ref.shape[2]
    block = 3 * wall_count
    partner = 2 * chip + other_core

    loads = [
        pltpu.make_async_copy(given, held, load_sem.at[at])
        for at, (given, held) in enumerate(
            (
                (order_hbm, order_smem),
                (order_hbm, order_ref),
                (force_hbm, force_ref),
                (lag_hbm, lag_ref),
                (mem_hbm, mem_all.at[cell]),
                (wall_hbm, wall_all.at[wall, 0]),
                (normal_hbm, wall_all.at[wall, 1]),
                (data_hbm, data_ref),
            )
        )
    ]
    for load in loads:
        load.start()

    barrier = pltpu.get_barrier_semaphore()
    for to_cell in range(cells - 1, -1, -1):
        for to_wall in range(walls):

            @pl.when((to_cell > cell) | ((to_cell == cell) & (to_wall > wall)))
            def _(to_cell=to_cell, to_wall=to_wall):
                pl.semaphore_signal(
                    barrier,
                    inc=1,
                    device_id={"cell": to_cell, "wall": to_wall},
                    device_id_type=MESH,
                )

    below = walls * cell + wall

    @pl.when(below > 0)
    def _():
        pl.semaphore_wait(barrier, below)

    for to_cell in range(cells - 1):
        for to_wall in range(walls):

            @pl.when(to_cell < cell)
            def _(to_cell=to_cell, to_wall=to_wall):
                pl.semaphore_signal(
                    ready.at[cell],
                    inc=1,
                    device_id={"cell": to_cell, "wall": to_wall},
                    device_id_type=MESH,
                )

    for to_wall in range(walls - 1):

        @pl.when(to_wall < wall)
        def _(to_wall=to_wall):
            pl.semaphore_signal(
                ready_near.at[wall], inc=1, device_id={"wall": to_wall}, device_id_type=MESH
            )

    def remote(given, held, send, recv, **to):
        return pltpu.make_async_remote_copy(
            given, held, send, recv, device_id=to, device_id_type=MESH
        )

    def block_copy(to_cell, to_chip):
        return remote(
            own_block,
            block_all.at[cell, chip],
            block_send,
            block_recv.at[cell],
            cell=to_cell,
            wall=2 * to_chip + other_core,
        )

    def lag_copy(to_cell, to_wall):
        return remote(
            own_lag, lag_all.at[cell * walls + wall], lag_send, lag_recv, cell=to_cell, wall=to_wall
        )

    def mem_copy(to_cell):
        return remote(
            mem_hbm,
            mem_all.at[cell],
            mem_send,
            mem_recv.at[cell],
            cell=to_cell,
            wall=partner,
        )

    def share_copy(to_cell):
        return remote(
            share_out.at[to_cell],
            share_in.at[cell],
            share_send,
            share_recv,
            cell=to_cell,
        )

    def wall_copies(to_wall):
        return [
            remote(
                given,
                wall_all.at[wall, at],
                wall_send,
                wall_recv.at[wall],
                wall=to_wall,
            )
            for at, given in enumerate((wall_hbm, normal_hbm))
        ]

    def second_copy(to_wall):
        held = second_all.at[wall]
        return remote(
            held, held, second_send, second_recv, wall=to_wall
        )

    def data_copy(to_wall):
        held = data_all.at[wall]
        return remote(held, held, data_send, data_recv, wall=to_wall)

    def near_walls(body):
        for to_wall in range(walls):

            @pl.when(to_wall != wall)
            def _(to_wall=to_wall):
                body(to_wall)

    def far_cells(test, body):
        for to_cell in range(cells):

            @pl.when(test(to_cell))
            def _(to_cell=to_cell):
                body(to_cell)

    def start_blocks(to_cell):
        for to_chip in (other_chip, chip):
            block_copy(to_cell, to_chip).start()

    def start_lag(to_cell):
        for to_wall in range(walls):
            lag_copy(to_cell, to_wall).start()

    for to_wall in range(walls):

        @pl.when(to_wall < wall)
        def _(to_wall=to_wall):
            for copy in wall_copies(to_wall):
                copy.start()

    far_cells(lambda to_cell: to_cell < cell, lambda to_cell: mem_copy(to_cell).start())

    row_ids = lax.broadcasted_iota(jnp.int32, (columns, columns), 0)
    col_ids = lax.broadcasted_iota(jnp.int32, (columns, columns), 1)
    loads[0].wait()
    wanted = jnp.zeros((columns, columns), jnp.int32)
    for k in range(columns):
        wanted = jnp.where(row_ids == k, order_smem[0, k], wanted)
    gather_f32 = (wanted == col_ids).astype(jnp.float32)
    gather = gather_f32.astype(jnp.bfloat16)

    loads[2].wait()
    rows = [jnp.dot(gather, force_ref[j], preferred_element_type=jnp.float32) for j in range(3)]
    folded = halfway // 2
    part = [row[:halfway] for row in rows]
    pair = jnp.concatenate([part[0], part[1]], axis=1)
    last = jnp.concatenate([part[2][:folded], part[2][folded:]], axis=1)
    own_block[...] = jnp.concatenate([pair, last], axis=0).astype(jnp.bfloat16)

    part = [row[halfway:] for row in rows]
    unused = jnp.zeros((halfway, LANES - own_points), jnp.float32)
    second_all[wall, 0] = jnp.concatenate([part[0], part[1]], axis=1).astype(jnp.bfloat16)
    second_all[wall, 1] = jnp.concatenate([part[2], unused], axis=1).astype(jnp.bfloat16)

    for to_wall in range(walls - 1):

        @pl.when(to_wall < wall)
        def _(to_wall=to_wall):
            second_copy(to_wall).start()

    far_cells(lambda to_cell: to_cell < cell, start_blocks)

    loads[3].wait()
    pieces = [lag_ref[j].astype(jnp.float32) for j in range(3)]
    if LANES > 3 * shard_width:
        pieces.append(jnp.zeros((halfway, LANES - 3 * shard_width), jnp.float32))
    packed_lag = jnp.concatenate(pieces, axis=1).astype(jnp.bfloat16)
    own_lag[...] = packed_lag
    lag_all[cell * walls + wall] = packed_lag

    far_cells(lambda to_cell: to_cell < cell, start_lag)

    def start_near(to_wall):
        @pl.when(to_wall > wall)
        def _():
            pl.semaphore_wait(ready_near.at[to_wall], 1)
            for copy in wall_copies(to_wall):
                copy.start()
            second_copy(to_wall).start()

        @pl.when(to_wall % 2 != core)
        def _():
            block_copy(cell, to_wall // 2).start()

        lag_copy(cell, to_wall).start()


    near_walls(start_near)

    for load in loads[4:]:
        load.wait()
    data_rows = [
        jnp.dot(gather_f32, data_ref[j], precision=lax.Precision.HIGHEST) for j in range(3)
    ]
    for j in range(3):
        data_all[wall, j] = data_rows[j][:halfway]
    near_walls(lambda to_wall: data_copy(to_wall).start())

    loads[1].wait()
    scatter = (row_ids == order_ref[...]).astype(jnp.float32).astype(jnp.bfloat16)

    def spread_wall(source):
        for j in range(3):
            wall_cols[source, j] = jnp.broadcast_to(
                wall_all[source, 0, j : j + 1, :], (LANES, wall_count)
            ).T

    for j in range(3):
        mem_cols[j] = jnp.broadcast_to(mem_all[cell, j : j + 1, :], (LANES, point_count)).T

    lane_ids = lax.broadcasted_iota(jnp.int32, (8, LANES), 1)

    def mem_rows(source, parity):
        rows = []
        for j in range(3):
            low = jnp.broadcast_to(mem_all[source, j : j + 1, :LANES], (8, LANES))
            high = jnp.broadcast_to(mem_all[source, j : j + 1, LANES:], (8, LANES))
            low = pltpu.roll(low, own_points * parity, 1)
            high = pltpu.roll(high, own_points * (1 - parity), 1)
            rows.append(jnp.where(lane_ids < own_points, low, high)[0:1])
        return rows

    def fill_single(tile, rows, at):
        apart = [wall_cols[at, j] - rows[j] for j in range(3)]
        square = apart[0] * apart[0] + apart[1] * apart[1] + apart[2] * apart[2]
        inverse = lax.rsqrt(square)
        scaled = stokes_coef * inverse
        cube = scaled * (inverse * inverse)
        for j in range(3):
            along = apart[j] * cube
            for i in range(j + 1):
                element = along * apart[i]
                if i == j:
                    element = element + scaled
                element = element.astype(jnp.bfloat16)
                for a, b in {(i, j), (j, i)}:
                    tile[a, :, b * LANES : (b + 1) * LANES] = element

    def fill_double(source):
        own = pl.ds(pl.multiple_of(wall * own_points, own_points), own_points)
        apart = [mem_cols[j, own, :] - wall_all[source, 0, j : j + 1, :] for j in range(3)]
        square = apart[0] * apart[0] + apart[1] * apart[1] + apart[2] * apart[2]
        inverse = lax.rsqrt(square)
        flux = (
            apart[0] * wall_all[source, 1, 0:1, :]
            + apart[1] * wall_all[source, 1, 1:2, :]
            + apart[2] * wall_all[source, 1, 2:3, :]
        )
        inverse_square = inverse * inverse
        fifth = inverse_square * inverse_square * inverse
        weight = (-6.0 * stokes_coef) * flux * fifth
        for j in range(3):
            along = apart[j] * weight
            for i in range(j + 1):
                element = (along * apart[i]).astype(jnp.bfloat16)
                for a, b in {(i, j), (j, i)}:
                    lanes = pl.multiple_of(source * block + b * wall_count, wall_count)
                    double_all[
                        a * own_points : (a + 1) * own_points, pl.ds(lanes, wall_count)
                    ] = element

    own_rows = mem_rows(cell, other_core)
    spread_wall(wall)
    fill_single(single_all.at[cell, wall], own_rows, wall)
    fill_single(single_rest, mem_rows(cell, core), wall)
    fill_double(wall)

    def wait_into(held, recv):
        remote(held, held, load_sem.at[0], recv, wall=partner).wait_recv()

    def wait_out(held, send):
        remote(held, held, send, load_sem.at[0], wall=partner).wait_send()

    peers = (partner, 2 * other_chip + other_core, 2 * other_chip + core)

    def take_wall(peer):
        wait_into(wall_all.at[peer], wall_recv.at[peer])
        spread_wall(peer)
        fill_single(single_all.at[cell, peer], own_rows, peer)
        fill_double(peer)

    def start_above(up):
        def body(to_cell):
            pl.semaphore_wait(ready.at[to_cell], walls)
            mem_copy(to_cell).start()
            start_blocks(to_cell)

        far_cells(lambda to_cell: to_cell == cell + up, body)

    def second_columns(tiles):
        pieces = [tile[0][:, :own_points] for tile in tiles]
        pieces += [tile[0][:, own_points:] for tile in tiles]
        pieces += [tile[1][:, :own_points] for tile in tiles]
        return jnp.concatenate(pieces, axis=1)

    def columns_of(tiles):
        tiles = [tile.astype(jnp.float32) for tile in tiles]
        pieces = [tile[:halfway, :own_points] for tile in tiles]
        pieces += [tile[:halfway, own_points:] for tile in tiles]
        for tile in tiles:
            last = tile[halfway:]
            pieces.append(jnp.concatenate([last[:, :own_points], last[:, own_points:]], axis=0))
        return jnp.concatenate(pieces, axis=1).astype(jnp.bfloat16)

    take_wall(partner)
    start_above(1)
    take_wall(peers[1])
    for up in range(2, cells - 1):
        start_above(up)

    wait_into(second_all.at[: walls - 1], second_recv)
    share = jnp.zeros((halfway, block), jnp.float32)
    for parity, tile in ((other_core, single_all.at[cell, wall]), (core, single_rest)):
        share = share + lax.dot_general(
            second_columns([second_all[2 * at + parity] for at in range(2)]),
            tile[...].reshape(block, 3 * LANES),
            NT,
            preferred_element_type=jnp.float32,
        )
    own_share = jnp.zeros((halfway, LANES), jnp.float32)
    for to_cell in range(cells):
        pieces = [
            share[:, i * wall_count + to_cell * shard_width :][:, :shard_width] for i in range(3)
        ]
        if LANES > 3 * shard_width:
            pieces.append(jnp.zeros((halfway, LANES - 3 * shard_width), jnp.float32))
        piece = jnp.concatenate(pieces, axis=1)
        own_share = jnp.where(cell == to_cell, piece, own_share)
        share_out[to_cell] = piece.astype(jnp.bfloat16)
    far_cells(lambda to_cell: to_cell < cell, lambda to_cell: share_copy(to_cell).start())
    if cells > 2:
        start_above(cells - 1)
    far_cells(lambda to_cell: to_cell > cell, lambda to_cell: share_copy(to_cell).start())
    far_cells(lambda to_cell: to_cell > cell, start_lag)
    take_wall(peers[2])

    def source_at(step):
        if step == 0:
            return cell
        return jnp.where(cell + step < cells, cell + step, cells - 1 - step)

    def take_mem(step):
        source = source_at(step)
        wait_into(mem_all.at[source], mem_recv.at[source])
        rows = mem_rows(source, other_core)
        for at in range(walls):
            fill_single(single_all.at[source, at], rows, at)

    def first_columns(step):
        source = source_at(step)
        wait_into(block_all.at[source], block_recv.at[source])
        return columns_of([block_all[source, at] for at in range(2)])

    def exchange(half):
        return remote(
            part_mine.at[half],
            part_other.at[half],
            part_send.at[half],
            part_recv.at[half],
            wall=partner,
        )

    width = walls // 2 * block
    partial = [jnp.zeros((halfway, width), jnp.float32) for _ in range(2)]
    for step in range(cells):
        if step + 1 < cells:
            take_mem(step + 1)
        left = first_columns(step)
        for half in range(2):
            tile = single_all[source_at(step), half * (walls // 2) : (half + 1) * (walls // 2)]
            partial[half] = partial[half] + lax.dot_general(
                left,
                tile.reshape(width, 3 * LANES),
                NT,
                preferred_element_type=jnp.float32,
            )
            if step == cells - 1:
                part_mine[half] = partial[half]
                exchange(half).start()

    wait_out(mem_all.at[: cells - 1], mem_send)
    wait_out(block_all, block_send)
    wait_out(lag_all.at[: cells * walls - 1], lag_send)
    wait_out(wall_all.at[: walls - 1], wall_send)
    wait_out(second_all.at[: walls - 1], second_send)
    wait_into(data_all.at[: walls - 1], data_recv)
    wait_out(data_all.at[: walls - 1], data_send)
    wait_out(share_in.at[: cells - 1], share_send)

    wait_into(lag_all.at[: cells * walls - 1], lag_recv)

    def layer(rows):
        return lax.dot_general(rows, double_all[...], NT, preferred_element_type=jnp.float32)

    lag_row = []
    for source in range(walls):
        lag_row += [
            lag_all[k * walls + source, :, j * shard_width : (j + 1) * shard_width]
            for j in range(3)
            for k in range(cells)
        ]
    lag_part = layer(jnp.concatenate(lag_row, axis=1))

    for half in range(2):
        exchange(half).wait_recv()
    pieces = []
    for source in range(walls):
        for i in range(3):
            half, at = divmod(source, walls // 2)
            lanes = slice(at * block + i * wall_count, at * block + (i + 1) * wall_count)
            velocity = part_mine[half, :, lanes] + part_other[half, :, lanes]
            dense = 2.0 * (data_all[source, i] - velocity)
            pieces.append(dense.astype(jnp.bfloat16))
    batched = jnp.concatenate([lag_part, layer(jnp.concatenate(pieces, axis=1))], axis=0)
    total = jnp.zeros((columns, 3 * own_points), jnp.float32)
    for _ in range(3):
        piece = batched.astype(jnp.bfloat16)
        total = total + jnp.dot(scatter, piece, preferred_element_type=jnp.float32)
        batched = batched - piece.astype(jnp.float32)
    for i in range(3):
        out_ref[i] = total[:, i * own_points : (i + 1) * own_points]

    wait_into(share_in.at[: cells - 1], share_recv)
    second_sum = own_share
    for step in range(1, cells):
        second_sum = second_sum + share_in[source_at(step)].astype(jnp.float32)
    shift = lax.rem((cells - cell) * shard_width, wall_count)
    for i in range(3):
        held = pltpu.roll(data_rows[i][halfway:], shift, 1)[:, :shard_width]
        density_ref[i] = 2.0 * (held - second_sum[:, i * shard_width : (i + 1) * shard_width])

    for half in range(2):
        exchange(half).wait_send()


def write_kernel(velocity_ref, density_ref, velocity_hbm, density_hbm, sem):
    first = pltpu.make_async_copy(velocity_ref, velocity_hbm, sem.at[0])
    second = pltpu.make_async_copy(density_ref, density_hbm, sem.at[1])
    first.start()
    second.start()
    first.wait()
    second.wait()


def fused_shards(cells, walls, mem_pos, forces, wall_pos, wall_normal, wall_data, lag_density, batch_order):
    columns = forces.shape[0]
    halfway = columns // 2
    point_count = mem_pos.shape[1]
    wall_count = wall_pos.shape[1]
    own_points = forces.shape[2]
    shard_width = lag_density.shape[2]
    dma = pltpu.SemaphoreType.DMA
    vmem = pl.BlockSpec(memory_space=pltpu.VMEM)
    hbm = pl.BlockSpec(memory_space=pltpu.HBM)
    velocity, density = pl.pallas_call(
        functools.partial(fused_kernel, cells, walls),
        out_shape=(
            pltpu.VMEM((3, columns, own_points), jnp.float32),
            pltpu.VMEM((3, halfway, shard_width), jnp.float32),
        ),
        in_specs=[hbm] * 7,
        out_specs=(vmem, vmem),
        scratch_shapes=[
            pltpu.VMEM((1, columns), jnp.int32),
            pltpu.SMEM((1, columns), jnp.int32),
            pltpu.VMEM((3, columns, own_points), jnp.bfloat16),
            pltpu.VMEM((3, halfway, shard_width), jnp.bfloat16),
            pltpu.VMEM((3, columns, wall_count), jnp.float32),
            pltpu.VMEM((3 * halfway // 2, LANES), jnp.bfloat16),
            pltpu.VMEM((halfway, LANES), jnp.bfloat16),
            pltpu.VMEM((cells, 2, 3 * halfway // 2, LANES), jnp.bfloat16),
            pltpu.VMEM((walls, 2, halfway, LANES), jnp.bfloat16),
            pltpu.VMEM((cells * walls, halfway, LANES), jnp.bfloat16),
            pltpu.VMEM((cells, 3, point_count), jnp.float32),
            pltpu.VMEM((walls, 2, 3, wall_count), jnp.float32),
            pltpu.VMEM((walls, 3, halfway, wall_count), jnp.float32),
            pltpu.VMEM((walls, 3, wall_count, LANES), jnp.float32),
            pltpu.VMEM((3, point_count, LANES), jnp.float32),
            pltpu.VMEM((cells, walls, 3, wall_count, 3 * LANES), jnp.bfloat16),
            pltpu.VMEM((3, wall_count, 3 * LANES), jnp.bfloat16),
            pltpu.VMEM((3 * own_points, walls * 3 * wall_count), jnp.bfloat16),
            pltpu.VMEM((2, halfway, walls // 2 * 3 * wall_count), jnp.float32),
            pltpu.VMEM((2, halfway, walls // 2 * 3 * wall_count), jnp.float32),
            pltpu.VMEM((cells, halfway, LANES), jnp.bfloat16),
            pltpu.VMEM((cells, halfway, LANES), jnp.bfloat16),
            dma((8,)),
            dma,
            dma((cells,)),
            dma,
            dma,
            dma,
            dma,
            dma,
            dma((cells,)),
            dma,
            dma((walls,)),
            dma,
            dma,
            dma((2,)),
            dma((2,)),
            dma,
            dma,
            pltpu.SemaphoreType.REGULAR((cells,)),
            pltpu.SemaphoreType.REGULAR((walls,)),
        ],
        compiler_params=pltpu.CompilerParams(
            collective_id=0, has_side_effects=True, vmem_limit_bytes=VMEM_GRANT
        ),
        name="coupling",
    )(
        mem_pos,
        jnp.transpose(forces, (1, 0, 2)),
        wall_pos,
        wall_normal,
        jnp.transpose(wall_data, (1, 0, 2)),
        jnp.transpose(lag_density, (1, 0, 2)),
        batch_order.reshape(1, columns),
    )
    velocity, density = pl.pallas_call(
        write_kernel,
        out_shape=(
            jax.ShapeDtypeStruct(velocity.shape, velocity.dtype),
            jax.ShapeDtypeStruct(density.shape, density.dtype),
        ),
        in_specs=[vmem] * 2,
        out_specs=(hbm, hbm),
        scratch_shapes=[dma((2,))],
        compiler_params=pltpu.CompilerParams(vmem_limit_bytes=1024 * 1024),
        name="write",
    )(velocity, density)
    return (jnp.transpose(velocity, (1, 0, 2)), jnp.transpose(density, (1, 0, 2)))


VMEM_GRANT = 60 * 1024 * 1024


def step(cells, walls, mem_pos, forces, wall_pos, *rest):
    point_count = mem_pos.shape[1]
    wall_count = wall_pos.shape[1]
    own_points = forces.shape[2]
    shard_width = rest[2].shape[2]
    tiles = 18 * walls * wall_count * (cells * LANES + own_points)
    fits = tiles <= VMEM_GRANT // 2
    aligned = (
        walls == 4
        and wall_count == LANES
        and 2 * own_points == LANES
        and point_count == walls * own_points
        and wall_count == cells * shard_width
        and 3 * shard_width <= LANES
    )
    if fits and aligned:
        return fused_shards(cells, walls, mem_pos, forces, wall_pos, *rest)
    return shards(mem_pos, forces, wall_pos, *rest)


def solution(mesh):
    placed = (
        P(None, ("groups", "cell")),
        P(None, None, ("groups", "cell", "wall")),
        P(None, ("groups", "wall")),
        P(None, ("groups", "wall")),
        P(None, None, ("groups", "wall")),
        P(None, None, ("groups", "wall", "cell")),
        P(),
    )
    return jax.shard_map(
        functools.partial(step, mesh.shape["cell"], mesh.shape["wall"]),
        mesh=mesh,
        in_specs=placed,
        out_specs=(
            P(None, None, ("groups", "cell", "wall")),
            P(None, None, ("groups", "wall", "cell")),
        ),
        check_vma=False,
    )
```

```python
import functools
import math

import jax
import jax.numpy as jnp
from jax import lax
from jax.experimental import pallas as pl
from jax.experimental.pallas import tpu as pltpu
from jax.sharding import PartitionSpec as P

stokes_coef = 1.0 / (8.0 * math.pi)


def single_tile(targets, sources):
    separation = targets[:, None, :] - sources[:, :, None]
    inverse = lax.rsqrt(jnp.sum(separation * separation, axis=0))
    inverse_cube = inverse * inverse * inverse
    stacked = []
    for second_dim in range(3):
        entries_row = []
        for first_dim in range(3):
            element = separation[first_dim] * separation[second_dim] * inverse_cube
            if first_dim == second_dim:
                element = element + inverse
            entries_row.append(element * stokes_coef)
        stacked.append(jnp.stack(entries_row, axis=1))
    kernel_tile = jnp.stack(stacked, axis=0)
    return kernel_tile.reshape(3 * sources.shape[1], 3 * targets.shape[1]).astype(jnp.bfloat16)


def double_tile(targets, sources, normals):
    separation = targets[:, None, :] - sources[:, :, None]
    inverse = lax.rsqrt(jnp.sum(separation * separation, axis=0))
    normal_flux = jnp.sum(separation * normals[:, :, None], axis=0)
    weight = -6.0 * stokes_coef * normal_flux * inverse**5
    stacked = []
    for second_dim in range(3):
        entries_row = []
        for first_dim in range(3):
            entries_row.append(weight * separation[first_dim] * separation[second_dim])
        stacked.append(jnp.stack(entries_row, axis=1))
    kernel_tile = jnp.stack(stacked, axis=0)
    return kernel_tile.reshape(3 * sources.shape[1], 3 * targets.shape[1]).astype(jnp.bfloat16)


def shards(mem_pos, forces, wall_pos, wall_normal, wall_data, lag_density, batch_order):
    columns = forces.shape[0]
    halfway = columns // 2
    point_count = mem_pos.shape[1]
    wall_count = wall_pos.shape[1]
    shard_width = lag_density.shape[2]
    piece_len = math.gcd(point_count, 128)
    block_count = point_count // piece_len
    first_rows = batch_order[:halfway]
    second_rows = batch_order[halfway:]
    force_block = lax.all_gather(forces, "wall", axis=2, tiled=True)
    lag_block = lax.all_gather(lag_density, "cell", axis=2, tiled=True)
    lag_flat = lag_block.reshape(halfway, 3 * wall_count)

    def position_at(block_index):
        return lax.dynamic_slice_in_dim(mem_pos, block_index * piece_len, piece_len, 1)

    def single_term(block_index):
        loaded = lax.dynamic_slice_in_dim(force_block, block_index * piece_len, piece_len, 2)
        loaded = loaded.reshape(columns, 3 * piece_len)
        return jnp.dot(
            loaded,
            single_tile(wall_pos, position_at(block_index)),
            preferred_element_type=jnp.float32,
        )

    def double_term(dense_rows, block_index):
        kernel_tile = double_tile(position_at(block_index), wall_pos, wall_normal)
        product = jnp.dot(dense_rows, kernel_tile, preferred_element_type=jnp.float32)
        return product.reshape(dense_rows.shape[0], 3, piece_len)

    def place_block(target, piece, block_index):
        return lax.dynamic_update_slice_in_dim(target, piece, block_index * piece_len, 2)

    empty_wall = jnp.zeros((columns, 3 * wall_count), jnp.float32)

    def add_single(block_index, running):
        return running + single_term(block_index)

    running = lax.fori_loop(0, block_count, add_single, empty_wall)
    wall_term = running.reshape(columns, 3, wall_count)
    position_cell = lax.axis_index("cell")
    first_sum = lax.psum(jnp.take(wall_term, first_rows, axis=0), "cell")
    first_block = (2.0 * (jnp.take(wall_data, first_rows, axis=0) - first_sum)).astype(jnp.bfloat16)
    second_sum = lax.psum_scatter(
        jnp.take(wall_term, second_rows, axis=0).astype(jnp.bfloat16),
        "cell",
        scatter_dimension=2,
        tiled=True,
    ).astype(jnp.float32)
    second_data = lax.dynamic_slice_in_dim(
        jnp.take(wall_data, second_rows, axis=0), position_cell * shard_width, shard_width, 2
    )
    wall_density = 2.0 * (second_data - second_sum)
    first_flat = first_block.reshape(halfway, 3 * wall_count)
    carried = jnp.concatenate([lag_flat, first_flat], axis=0)

    def all_terms(block_index, target):
        return place_block(target, double_term(carried, block_index), block_index)

    membrane_term = lax.fori_loop(
        0, block_count, all_terms, jnp.zeros((columns, 3, point_count), jnp.float32)
    )
    batched = lax.psum_scatter(membrane_term, "wall", scatter_dimension=2, tiled=True)
    membrane_velocity = jnp.zeros_like(batched).at[batch_order].set(batched)
    return (membrane_velocity, wall_density)

LANES = 128
MESH = pl.DeviceIdType.MESH
NT = (((1,), (1,)), ((), ()))


TILES = ((0, 0), (1, 1), (2, 2), (0, 1), (0, 2), (1, 2))


def fused_kernel(
    cells,
    walls,
    mem_hbm,
    force_hbm,
    wall_hbm,
    normal_hbm,
    data_hbm,
    lag_hbm,
    order_hbm,
    out_ref,
    density_ref,
    order_ref,
    order_smem,
    force_ref,
    lag_ref,
    data_ref,
    own_block,
    own_lag,
    block_all,
    second_all,
    lag_all,
    mem_all,
    wall_all,
    data_all,
    wall_cols,
    mem_cols,
    single_all,
    single_rest,
    double_all,
    part_mine,
    part_other,
    share_out,
    share_in,
    load_sem,
    block_send,
    block_recv,
    second_send,
    second_recv,
    lag_send,
    lag_recv,
    mem_send,
    mem_recv,
    wall_send,
    wall_recv,
    data_send,
    data_recv,
    part_send,
    part_recv,
    share_send,
    share_recv,
    ready,
    ready_near,
):
    cell = lax.axis_index("cell")
    wall = lax.axis_index("wall")
    chip = lax.div(wall, 2)
    core = lax.rem(wall, 2)
    other_core = 1 - core
    other_chip = 1 - chip
    columns = order_ref.shape[1]
    halfway = columns // 2
    point_count = mem_hbm.shape[1]
    wall_count = wall_hbm.shape[1]
    own_points = force_ref.shape[2]
    shard_width = lag_ref.shape[2]
    block = 3 * wall_count
    partner = 2 * chip + other_core

    loads = [
        pltpu.make_async_copy(given, held, load_sem.at[at])
        for at, (given, held) in enumerate(
            (
                (order_hbm, order_smem),
                (order_hbm, order_ref),
                (force_hbm, force_ref),
                (lag_hbm, lag_ref),
                (mem_hbm, mem_all.at[cell]),
                (wall_hbm, wall_all.at[wall, 0]),
                (normal_hbm, wall_all.at[wall, 1]),
                (data_hbm, data_ref),
            )
        )
    ]
    for load in loads:
        load.start()

    barrier = pltpu.get_barrier_semaphore()
    for to_cell in range(cells - 1, -1, -1):
        for to_wall in range(walls):

            @pl.when((to_cell > cell) | ((to_cell == cell) & (to_wall > wall)))
            def _(to_cell=to_cell, to_wall=to_wall):
                pl.semaphore_signal(
                    barrier,
                    inc=1,
                    device_id={"cell": to_cell, "wall": to_wall},
                    device_id_type=MESH,
                )

    below = walls * cell + wall

    @pl.when(below > 0)
    def _():
        pl.semaphore_wait(barrier, below)

    for to_cell in range(cells - 1):
        for to_wall in range(walls):

            @pl.when(to_cell < cell)
            def _(to_cell=to_cell, to_wall=to_wall):
                pl.semaphore_signal(
                    ready.at[cell],
                    inc=1,
                    device_id={"cell": to_cell, "wall": to_wall},
                    device_id_type=MESH,
                )

    for to_wall in range(walls - 1):

        @pl.when(to_wall < wall)
        def _(to_wall=to_wall):
            pl.semaphore_signal(
                ready_near.at[wall], inc=1, device_id={"wall": to_wall}, device_id_type=MESH
            )

    def remote(given, held, send, recv, **to):
        return pltpu.make_async_remote_copy(
            given, held, send, recv, device_id=to, device_id_type=MESH
        )

    def block_copy(to_cell, to_chip):
        return remote(
            own_block,
            block_all.at[cell, chip],
            block_send,
            block_recv.at[cell],
            cell=to_cell,
            wall=2 * to_chip + other_core,
        )

    def lag_copy(to_cell, to_wall):
        return remote(
            own_lag, lag_all.at[cell * walls + wall], lag_send, lag_recv, cell=to_cell, wall=to_wall
        )

    def mem_copy(to_cell):
        return remote(
            mem_hbm,
            mem_all.at[cell],
            mem_send,
            mem_recv.at[cell],
            cell=to_cell,
            wall=partner,
        )

    def share_copy(to_cell):
        return remote(
            share_out.at[to_cell],
            share_in.at[cell],
            share_send,
            share_recv,
            cell=to_cell,
        )

    def wall_copies(to_wall):
        return [
            remote(
                given,
                wall_all.at[wall, at],
                wall_send,
                wall_recv.at[wall],
                wall=to_wall,
            )
            for at, given in enumerate((wall_hbm, normal_hbm))
        ]

    def second_copy(to_wall):
        held = second_all.at[wall]
        return remote(
            held, held, second_send, second_recv, wall=to_wall
        )

    def data_copy(to_wall):
        held = data_all.at[wall]
        return remote(held, held, data_send, data_recv, wall=to_wall)

    def near_walls(body):
        for to_wall in range(walls):

            @pl.when(to_wall != wall)
            def _(to_wall=to_wall):
                body(to_wall)

    def far_cells(test, body):
        for to_cell in range(cells):

            @pl.when(test(to_cell))
            def _(to_cell=to_cell):
                body(to_cell)

    def start_blocks(to_cell):
        for to_chip in (other_chip, chip):
            block_copy(to_cell, to_chip).start()

    def start_lag(to_cell):
        for to_wall in range(walls):
            lag_copy(to_cell, to_wall).start()

    for to_wall in range(walls):

        @pl.when(to_wall < wall)
        def _(to_wall=to_wall):
            for copy in wall_copies(to_wall):
                copy.start()

    far_cells(lambda to_cell: to_cell < cell, lambda to_cell: mem_copy(to_cell).start())

    row_ids = lax.broadcasted_iota(jnp.int32, (columns, columns), 0)
    col_ids = lax.broadcasted_iota(jnp.int32, (columns, columns), 1)
    loads[0].wait()
    wanted = jnp.zeros((columns, columns), jnp.int32)
    for k in range(columns):
        wanted = jnp.where(row_ids == k, order_smem[0, k], wanted)
    gather_f32 = (wanted == col_ids).astype(jnp.float32)
    gather = gather_f32.astype(jnp.bfloat16)

    loads[2].wait()
    rows = [jnp.dot(gather, force_ref[j], preferred_element_type=jnp.float32) for j in range(3)]
    folded = halfway // 2
    part = [row[:halfway] for row in rows]
    pair = jnp.concatenate([part[0], part[1]], axis=1)
    last = jnp.concatenate([part[2][:folded], part[2][folded:]], axis=1)
    own_block[...] = jnp.concatenate([pair, last], axis=0).astype(jnp.bfloat16)

    part = [row[halfway:] for row in rows]
    unused = jnp.zeros((halfway, LANES - own_points), jnp.float32)
    second_all[wall, 0] = jnp.concatenate([part[0], part[1]], axis=1).astype(jnp.bfloat16)
    second_all[wall, 1] = jnp.concatenate([part[2], unused], axis=1).astype(jnp.bfloat16)

    for to_wall in range(walls - 1):

        @pl.when(to_wall < wall)
        def _(to_wall=to_wall):
            second_copy(to_wall).start()

    far_cells(lambda to_cell: to_cell < cell, start_blocks)

    loads[3].wait()
    pieces = [lag_ref[j].astype(jnp.float32) for j in range(3)]
    if LANES > 3 * shard_width:
        pieces.append(jnp.zeros((halfway, LANES - 3 * shard_width), jnp.float32))
    packed_lag = jnp.concatenate(pieces, axis=1).astype(jnp.bfloat16)
    own_lag[...] = packed_lag
    lag_all[cell * walls + wall] = packed_lag

    far_cells(lambda to_cell: to_cell < cell, start_lag)

    def start_near(to_wall):
        @pl.when(to_wall > wall)
        def _():
            pl.semaphore_wait(ready_near.at[to_wall], 1)
            for copy in wall_copies(to_wall):
                copy.start()
            second_copy(to_wall).start()

        @pl.when(to_wall % 2 != core)
        def _():
            block_copy(cell, to_wall // 2).start()

        lag_copy(cell, to_wall).start()


    near_walls(start_near)

    for load in loads[4:]:
        load.wait()
    data_rows = [
        jnp.dot(gather_f32, data_ref[j], precision=lax.Precision.HIGHEST) for j in range(3)
    ]
    for j in range(3):
        data_all[wall, j] = data_rows[j][:halfway]
    near_walls(lambda to_wall: data_copy(to_wall).start())

    loads[1].wait()
    scatter = (row_ids == order_ref[...]).astype(jnp.float32).astype(jnp.bfloat16)

    def spread_wall(source):
        for j in range(3):
            wall_cols[source, j] = jnp.broadcast_to(
                wall_all[source, 0, j : j + 1, :], (LANES, wall_count)
            ).T

    for j in range(3):
        mem_cols[j] = jnp.broadcast_to(mem_all[cell, j : j + 1, :], (LANES, point_count)).T

    lane_ids = lax.broadcasted_iota(jnp.int32, (8, LANES), 1)

    def mem_rows(source, parity):
        rows = []
        for j in range(3):
            low = jnp.broadcast_to(mem_all[source, j : j + 1, :LANES], (8, LANES))
            high = jnp.broadcast_to(mem_all[source, j : j + 1, LANES:], (8, LANES))
            low = pltpu.roll(low, own_points * parity, 1)
            high = pltpu.roll(high, own_points * (1 - parity), 1)
            rows.append(jnp.where(lane_ids < own_points, low, high)[0:1])
        return rows

    def fill_single(tile, rows, at):
        apart = [wall_cols[at, j] - rows[j] for j in range(3)]
        square = apart[0] * apart[0] + apart[1] * apart[1] + apart[2] * apart[2]
        inverse = lax.rsqrt(square)
        scaled = stokes_coef * inverse
        cube = scaled * (inverse * inverse)
        for j in range(3):
            along = apart[j] * cube
            for i in range(j + 1):
                element = along * apart[i]
                if i == j:
                    element = element + scaled
                at_tile = TILES.index((i, j))
                tile[:, at_tile * LANES : (at_tile + 1) * LANES] = element.astype(jnp.bfloat16)

    def fill_double(source):
        own = pl.ds(pl.multiple_of(wall * own_points, own_points), own_points)
        apart = [mem_cols[j, own, :] - wall_all[source, 0, j : j + 1, :] for j in range(3)]
        square = apart[0] * apart[0] + apart[1] * apart[1] + apart[2] * apart[2]
        inverse = lax.rsqrt(square)
        flux = (
            apart[0] * wall_all[source, 1, 0:1, :]
            + apart[1] * wall_all[source, 1, 1:2, :]
            + apart[2] * wall_all[source, 1, 2:3, :]
        )
        inverse_square = inverse * inverse
        fifth = inverse_square * inverse_square * inverse
        weight = (-6.0 * stokes_coef) * flux * fifth
        for j in range(3):
            along = apart[j] * weight
            for i in range(j + 1):
                element = (along * apart[i]).astype(jnp.bfloat16)
                for a, b in {(i, j), (j, i)}:
                    lanes = pl.multiple_of(source * block + b * wall_count, wall_count)
                    double_all[
                        a * own_points : (a + 1) * own_points, pl.ds(lanes, wall_count)
                    ] = element

    own_rows = mem_rows(cell, other_core)
    spread_wall(wall)
    fill_single(single_all.at[0, wall], own_rows, wall)
    fill_single(single_rest, mem_rows(cell, core), wall)
    fill_double(wall)

    def wait_into(held, recv):
        remote(held, held, load_sem.at[0], recv, wall=partner).wait_recv()

    def wait_out(held, send):
        remote(held, held, send, load_sem.at[0], wall=partner).wait_send()

    peers = (partner, 2 * other_chip + other_core, 2 * other_chip + core)

    def take_wall(peer):
        wait_into(wall_all.at[peer], wall_recv.at[peer])
        spread_wall(peer)
        fill_single(single_all.at[0, peer], own_rows, peer)
        fill_double(peer)

    def start_above(up):
        def body(to_cell):
            pl.semaphore_wait(ready.at[to_cell], walls)
            mem_copy(to_cell).start()
            start_blocks(to_cell)

        far_cells(lambda to_cell: to_cell == cell + up, body)

    low_lanes = lax.broadcasted_iota(jnp.int32, (halfway, LANES), 1) < own_points

    def low_halves(first, second):
        mask = low_lanes[: first.shape[0]]
        return jnp.where(mask, first, pltpu.roll(second, own_points, 1))

    def high_halves(first, second):
        mask = low_lanes[: first.shape[0]]
        return jnp.where(mask, pltpu.roll(first, own_points, 1), second)

    def stack_rows(parts):
        empty = jnp.zeros((halfway, LANES), jnp.bfloat16)
        groups = []
        for i in range(3):
            row = [empty] * len(TILES)
            for at_tile, (a, b) in enumerate(TILES):
                if i in (a, b):
                    row[at_tile] = parts[a + b - i].astype(jnp.bfloat16)
            groups.append(jnp.concatenate(row, axis=1))
        return jnp.concatenate(groups, axis=0)

    def second_columns(tiles):
        pair = [tile[0].astype(jnp.float32) for tile in tiles]
        last = [tile[1].astype(jnp.float32) for tile in tiles]
        return stack_rows([low_halves(*pair), high_halves(*pair), low_halves(*last)])

    def columns_of(tiles):
        tiles = [tile.astype(jnp.float32) for tile in tiles]
        pair = [tile[:halfway] for tile in tiles]
        last = [tile[halfway:] for tile in tiles]
        last = jnp.concatenate([low_halves(*last), high_halves(*last)], axis=0)
        return stack_rows([low_halves(*pair), high_halves(*pair), last])

    take_wall(partner)
    start_above(1)
    take_wall(peers[1])
    for up in range(2, cells - 1):
        start_above(up)

    wait_into(second_all.at[: walls - 1], second_recv)
    share = jnp.zeros((3 * halfway, wall_count), jnp.float32)
    for parity, tile in ((other_core, single_all.at[0, wall]), (core, single_rest)):
        share = share + lax.dot_general(
            second_columns([second_all[2 * at + parity] for at in range(2)]),
            tile[...],
            NT,
            preferred_element_type=jnp.float32,
        )
    own_share = jnp.zeros((halfway, LANES), jnp.float32)
    for to_cell in range(cells):
        pieces = [
            share[
                i * halfway : (i + 1) * halfway,
                to_cell * shard_width : (to_cell + 1) * shard_width,
            ]
            for i in range(3)
        ]
        if LANES > 3 * shard_width:
            pieces.append(jnp.zeros((halfway, LANES - 3 * shard_width), jnp.float32))
        piece = jnp.concatenate(pieces, axis=1)
        own_share = jnp.where(cell == to_cell, piece, own_share)
        share_out[to_cell] = piece.astype(jnp.bfloat16)
    far_cells(lambda to_cell: to_cell < cell, lambda to_cell: share_copy(to_cell).start())
    if cells > 2:
        start_above(cells - 1)
    far_cells(lambda to_cell: to_cell > cell, lambda to_cell: share_copy(to_cell).start())
    far_cells(lambda to_cell: to_cell > cell, start_lag)
    take_wall(peers[2])

    def source_at(step):
        if step == 0:
            return cell
        return jnp.where(cell + step < cells, cell + step, cells - 1 - step)

    def wait_mem(step):
        source = source_at(step)
        wait_into(mem_all.at[source], mem_recv.at[source])

    def take_mem(step):
        rows = mem_rows(source_at(step), other_core)
        for at in range(walls):
            fill_single(single_all.at[step, at], rows, at)

    def first_columns(step):
        source = source_at(step)
        wait_into(block_all.at[source], block_recv.at[source])
        return columns_of([block_all[source, at] for at in range(2)])

    def exchange(half):
        return remote(
            part_mine.at[half],
            part_other.at[half],
            part_send.at[half],
            part_recv.at[half],
            wall=partner,
        )

    width = walls // 2 * wall_count
    partial = [jnp.zeros((3 * halfway, width), jnp.float32) for _ in range(2)]
    for step in range(cells):
        if step + 1 < cells:
            wait_mem(step + 1)
        left = first_columns(step)
        for half in range(2):
            tile = single_all[step, half * (walls // 2) : (half + 1) * (walls // 2)]
            partial[half] = partial[half] + lax.dot_general(
                left,
                tile.reshape(width, len(TILES) * LANES),
                NT,
                preferred_element_type=jnp.float32,
            )
            if step == cells - 1:
                part_mine[half] = partial[half]
                exchange(half).start()
        if step + 1 < cells:
            take_mem(step + 1)

    wait_out(mem_all.at[: cells - 1], mem_send)
    wait_out(block_all, block_send)
    wait_out(lag_all.at[: cells * walls - 1], lag_send)
    wait_out(wall_all.at[: walls - 1], wall_send)
    wait_out(second_all.at[: walls - 1], second_send)
    wait_into(data_all.at[: walls - 1], data_recv)
    wait_out(data_all.at[: walls - 1], data_send)
    wait_out(share_in.at[: cells - 1], share_send)

    wait_into(lag_all.at[: cells * walls - 1], lag_recv)

    def layer(rows):
        return lax.dot_general(rows, double_all[...], NT, preferred_element_type=jnp.float32)

    lag_row = []
    for source in range(walls):
        lag_row += [
            lag_all[k * walls + source, :, j * shard_width : (j + 1) * shard_width]
            for j in range(3)
            for k in range(cells)
        ]
    lag_part = layer(jnp.concatenate(lag_row, axis=1))

    for half in range(2):
        exchange(half).wait_recv()
    pieces = []
    for source in range(walls):
        for i in range(3):
            half, at = divmod(source, walls // 2)
            held = slice(i * halfway, (i + 1) * halfway)
            lanes = slice(at * wall_count, (at + 1) * wall_count)
            velocity = part_mine[half, held, lanes] + part_other[half, held, lanes]
            dense = 2.0 * (data_all[source, i] - velocity)
            pieces.append(dense.astype(jnp.bfloat16))
    batched = jnp.concatenate([lag_part, layer(jnp.concatenate(pieces, axis=1))], axis=0)
    total = jnp.zeros((columns, 3 * own_points), jnp.float32)
    for _ in range(3):
        piece = batched.astype(jnp.bfloat16)
        total = total + jnp.dot(scatter, piece, preferred_element_type=jnp.float32)
        batched = batched - piece.astype(jnp.float32)
    for i in range(3):
        out_ref[i] = total[:, i * own_points : (i + 1) * own_points]

    wait_into(share_in.at[: cells - 1], share_recv)
    second_sum = own_share
    for step in range(1, cells):
        second_sum = second_sum + share_in[source_at(step)].astype(jnp.float32)
    shift = lax.rem((cells - cell) * shard_width, wall_count)
    for i in range(3):
        held = pltpu.roll(data_rows[i][halfway:], shift, 1)[:, :shard_width]
        density_ref[i] = 2.0 * (held - second_sum[:, i * shard_width : (i + 1) * shard_width])

    for half in range(2):
        exchange(half).wait_send()


def write_kernel(velocity_ref, density_ref, velocity_hbm, density_hbm, sem):
    first = pltpu.make_async_copy(velocity_ref, velocity_hbm, sem.at[0])
    second = pltpu.make_async_copy(density_ref, density_hbm, sem.at[1])
    first.start()
    second.start()
    first.wait()
    second.wait()


def fused_shards(cells, walls, mem_pos, forces, wall_pos, wall_normal, wall_data, lag_density, batch_order):
    columns = forces.shape[0]
    halfway = columns // 2
    point_count = mem_pos.shape[1]
    wall_count = wall_pos.shape[1]
    own_points = forces.shape[2]
    shard_width = lag_density.shape[2]
    dma = pltpu.SemaphoreType.DMA
    vmem = pl.BlockSpec(memory_space=pltpu.VMEM)
    hbm = pl.BlockSpec(memory_space=pltpu.HBM)
    velocity, density = pl.pallas_call(
        functools.partial(fused_kernel, cells, walls),
        out_shape=(
            pltpu.VMEM((3, columns, own_points), jnp.float32),
            pltpu.VMEM((3, halfway, shard_width), jnp.float32),
        ),
        in_specs=[hbm] * 7,
        out_specs=(vmem, vmem),
        scratch_shapes=[
            pltpu.VMEM((1, columns), jnp.int32),
            pltpu.SMEM((1, columns), jnp.int32),
            pltpu.VMEM((3, columns, own_points), jnp.bfloat16),
            pltpu.VMEM((3, halfway, shard_width), jnp.bfloat16),
            pltpu.VMEM((3, columns, wall_count), jnp.float32),
            pltpu.VMEM((3 * halfway // 2, LANES), jnp.bfloat16),
            pltpu.VMEM((halfway, LANES), jnp.bfloat16),
            pltpu.VMEM((cells, 2, 3 * halfway // 2, LANES), jnp.bfloat16),
            pltpu.VMEM((walls, 2, halfway, LANES), jnp.bfloat16),
            pltpu.VMEM((cells * walls, halfway, LANES), jnp.bfloat16),
            pltpu.VMEM((cells, 3, point_count), jnp.float32),
            pltpu.VMEM((walls, 2, 3, wall_count), jnp.float32),
            pltpu.VMEM((walls, 3, halfway, wall_count), jnp.float32),
            pltpu.VMEM((walls, 3, wall_count, LANES), jnp.float32),
            pltpu.VMEM((3, point_count, LANES), jnp.float32),
            pltpu.VMEM((cells, walls, wall_count, len(TILES) * LANES), jnp.bfloat16),
            pltpu.VMEM((wall_count, len(TILES) * LANES), jnp.bfloat16),
            pltpu.VMEM((3 * own_points, walls * 3 * wall_count), jnp.bfloat16),
            pltpu.VMEM((2, 3 * halfway, walls // 2 * wall_count), jnp.float32),
            pltpu.VMEM((2, 3 * halfway, walls // 2 * wall_count), jnp.float32),
            pltpu.VMEM((cells, halfway, LANES), jnp.bfloat16),
            pltpu.VMEM((cells, halfway, LANES), jnp.bfloat16),
            dma((8,)),
            dma,
            dma((cells,)),
            dma,
            dma,
            dma,
            dma,
            dma,
            dma((cells,)),
            dma,
            dma((walls,)),
            dma,
            dma,
            dma((2,)),
            dma((2,)),
            dma,
            dma,
            pltpu.SemaphoreType.REGULAR((cells,)),
            pltpu.SemaphoreType.REGULAR((walls,)),
        ],
        compiler_params=pltpu.CompilerParams(
            collective_id=0, has_side_effects=True, vmem_limit_bytes=VMEM_GRANT
        ),
        name="coupling",
    )(
        mem_pos,
        jnp.transpose(forces, (1, 0, 2)),
        wall_pos,
        wall_normal,
        jnp.transpose(wall_data, (1, 0, 2)),
        jnp.transpose(lag_density, (1, 0, 2)),
        batch_order.reshape(1, columns),
    )
    velocity, density = pl.pallas_call(
        write_kernel,
        out_shape=(
            jax.ShapeDtypeStruct(velocity.shape, velocity.dtype),
            jax.ShapeDtypeStruct(density.shape, density.dtype),
        ),
        in_specs=[vmem] * 2,
        out_specs=(hbm, hbm),
        scratch_shapes=[dma((2,))],
        compiler_params=pltpu.CompilerParams(vmem_limit_bytes=1024 * 1024),
        name="write",
    )(velocity, density)
    return (jnp.transpose(velocity, (1, 0, 2)), jnp.transpose(density, (1, 0, 2)))


VMEM_GRANT = 60 * 1024 * 1024


def step(cells, walls, mem_pos, forces, wall_pos, *rest):
    point_count = mem_pos.shape[1]
    wall_count = wall_pos.shape[1]
    own_points = forces.shape[2]
    shard_width = rest[2].shape[2]
    tiles = 18 * walls * wall_count * (cells * LANES + own_points)
    fits = tiles <= VMEM_GRANT // 2
    aligned = (
        walls == 4
        and wall_count == LANES
        and 2 * own_points == LANES
        and point_count == walls * own_points
        and wall_count == cells * shard_width
        and 3 * shard_width <= LANES
    )
    if fits and aligned:
        return fused_shards(cells, walls, mem_pos, forces, wall_pos, *rest)
    return shards(mem_pos, forces, wall_pos, *rest)


def solution(mesh):
    placed = (
        P(None, ("groups", "cell")),
        P(None, None, ("groups", "cell", "wall")),
        P(None, ("groups", "wall")),
        P(None, ("groups", "wall")),
        P(None, None, ("groups", "wall")),
        P(None, None, ("groups", "wall", "cell")),
        P(),
    )
    return jax.shard_map(
        functools.partial(step, mesh.shape["cell"], mesh.shape["wall"]),
        mesh=mesh,
        in_specs=placed,
        out_specs=(
            P(None, None, ("groups", "cell", "wall")),
            P(None, None, ("groups", "wall", "cell")),
        ),
        check_vma=False,
    )
```

```python
import functools
import math

import jax
import jax.numpy as jnp
from jax import lax
from jax.experimental import pallas as pl
from jax.experimental.pallas import tpu as pltpu
from jax.sharding import PartitionSpec as P

stokes_coef = 1.0 / (8.0 * math.pi)


def single_tile(targets, sources):
    separation = targets[:, None, :] - sources[:, :, None]
    inverse = lax.rsqrt(jnp.sum(separation * separation, axis=0))
    inverse_cube = inverse * inverse * inverse
    stacked = []
    for second_dim in range(3):
        entries_row = []
        for first_dim in range(3):
            element = separation[first_dim] * separation[second_dim] * inverse_cube
            if first_dim == second_dim:
                element = element + inverse
            entries_row.append(element * stokes_coef)
        stacked.append(jnp.stack(entries_row, axis=1))
    kernel_tile = jnp.stack(stacked, axis=0)
    return kernel_tile.reshape(3 * sources.shape[1], 3 * targets.shape[1]).astype(jnp.bfloat16)


def double_tile(targets, sources, normals):
    separation = targets[:, None, :] - sources[:, :, None]
    inverse = lax.rsqrt(jnp.sum(separation * separation, axis=0))
    normal_flux = jnp.sum(separation * normals[:, :, None], axis=0)
    weight = -6.0 * stokes_coef * normal_flux * inverse**5
    stacked = []
    for second_dim in range(3):
        entries_row = []
        for first_dim in range(3):
            entries_row.append(weight * separation[first_dim] * separation[second_dim])
        stacked.append(jnp.stack(entries_row, axis=1))
    kernel_tile = jnp.stack(stacked, axis=0)
    return kernel_tile.reshape(3 * sources.shape[1], 3 * targets.shape[1]).astype(jnp.bfloat16)


def shards(mem_pos, forces, wall_pos, wall_normal, wall_data, lag_density, batch_order):
    columns = forces.shape[0]
    halfway = columns // 2
    point_count = mem_pos.shape[1]
    wall_count = wall_pos.shape[1]
    shard_width = lag_density.shape[2]
    piece_len = math.gcd(point_count, 128)
    block_count = point_count // piece_len
    first_rows = batch_order[:halfway]
    second_rows = batch_order[halfway:]
    force_block = lax.all_gather(forces, "wall", axis=2, tiled=True)
    lag_block = lax.all_gather(lag_density, "cell", axis=2, tiled=True)
    lag_flat = lag_block.reshape(halfway, 3 * wall_count)

    def position_at(block_index):
        return lax.dynamic_slice_in_dim(mem_pos, block_index * piece_len, piece_len, 1)

    def single_term(block_index):
        loaded = lax.dynamic_slice_in_dim(force_block, block_index * piece_len, piece_len, 2)
        loaded = loaded.reshape(columns, 3 * piece_len)
        return jnp.dot(
            loaded,
            single_tile(wall_pos, position_at(block_index)),
            preferred_element_type=jnp.float32,
        )

    def double_term(dense_rows, block_index):
        kernel_tile = double_tile(position_at(block_index), wall_pos, wall_normal)
        product = jnp.dot(dense_rows, kernel_tile, preferred_element_type=jnp.float32)
        return product.reshape(dense_rows.shape[0], 3, piece_len)

    def place_block(target, piece, block_index):
        return lax.dynamic_update_slice_in_dim(target, piece, block_index * piece_len, 2)

    empty_wall = jnp.zeros((columns, 3 * wall_count), jnp.float32)

    def add_single(block_index, running):
        return running + single_term(block_index)

    running = lax.fori_loop(0, block_count, add_single, empty_wall)
    wall_term = running.reshape(columns, 3, wall_count)
    position_cell = lax.axis_index("cell")
    first_sum = lax.psum(jnp.take(wall_term, first_rows, axis=0), "cell")
    first_block = (2.0 * (jnp.take(wall_data, first_rows, axis=0) - first_sum)).astype(jnp.bfloat16)
    second_sum = lax.psum_scatter(
        jnp.take(wall_term, second_rows, axis=0).astype(jnp.bfloat16),
        "cell",
        scatter_dimension=2,
        tiled=True,
    ).astype(jnp.float32)
    second_data = lax.dynamic_slice_in_dim(
        jnp.take(wall_data, second_rows, axis=0), position_cell * shard_width, shard_width, 2
    )
    wall_density = 2.0 * (second_data - second_sum)
    first_flat = first_block.reshape(halfway, 3 * wall_count)
    carried = jnp.concatenate([lag_flat, first_flat], axis=0)

    def all_terms(block_index, target):
        return place_block(target, double_term(carried, block_index), block_index)

    membrane_term = lax.fori_loop(
        0, block_count, all_terms, jnp.zeros((columns, 3, point_count), jnp.float32)
    )
    batched = lax.psum_scatter(membrane_term, "wall", scatter_dimension=2, tiled=True)
    membrane_velocity = jnp.zeros_like(batched).at[batch_order].set(batched)
    return (membrane_velocity, wall_density)

LANES = 128
MESH = pl.DeviceIdType.MESH
NT = (((1,), (1,)), ((), ()))


TILES = ((0, 0), (1, 1), (2, 2), (0, 1), (0, 2), (1, 2))


def fused_kernel(
    cells,
    walls,
    mem_hbm,
    force_hbm,
    wall_hbm,
    normal_hbm,
    data_hbm,
    lag_hbm,
    order_hbm,
    out_ref,
    density_ref,
    order_ref,
    order_smem,
    force_ref,
    lag_ref,
    data_ref,
    own_block,
    own_lag,
    block_all,
    second_all,
    lag_all,
    mem_all,
    wall_all,
    data_all,
    wall_cols,
    mem_cols,
    single_all,
    single_rest,
    double_all,
    part_mine,
    part_other,
    share_out,
    share_in,
    load_sem,
    block_send,
    block_recv,
    second_send,
    second_recv,
    lag_send,
    lag_recv,
    mem_send,
    mem_recv,
    wall_send,
    wall_recv,
    data_send,
    data_recv,
    part_send,
    part_recv,
    share_send,
    share_recv,
    ready,
    ready_near,
):
    cell = lax.axis_index("cell")
    wall = lax.axis_index("wall")
    chip = lax.div(wall, 2)
    core = lax.rem(wall, 2)
    other_core = 1 - core
    other_chip = 1 - chip
    columns = order_ref.shape[1]
    halfway = columns // 2
    point_count = mem_hbm.shape[1]
    wall_count = wall_hbm.shape[1]
    own_points = force_ref.shape[2]
    shard_width = lag_ref.shape[2]
    block = 3 * wall_count
    partner = 2 * chip + other_core

    loads = [
        pltpu.make_async_copy(given, held, load_sem.at[at])
        for at, (given, held) in enumerate(
            (
                (order_hbm, order_smem),
                (order_hbm, order_ref),
                (force_hbm, force_ref),
                (lag_hbm, lag_ref),
                (mem_hbm, mem_all.at[cell]),
                (wall_hbm, wall_all.at[wall, 0]),
                (normal_hbm, wall_all.at[wall, 1]),
                (data_hbm, data_ref),
            )
        )
    ]
    for load in loads:
        load.start()

    barrier = pltpu.get_barrier_semaphore()
    for to_cell in range(cells - 1, -1, -1):
        for to_wall in range(walls):

            @pl.when((to_cell > cell) | ((to_cell == cell) & (to_wall > wall)))
            def _(to_cell=to_cell, to_wall=to_wall):
                pl.semaphore_signal(
                    barrier,
                    inc=1,
                    device_id={"cell": to_cell, "wall": to_wall},
                    device_id_type=MESH,
                )

    below = walls * cell + wall

    @pl.when(below > 0)
    def _():
        pl.semaphore_wait(barrier, below)

    for to_cell in range(cells - 1):
        for to_wall in range(walls):

            @pl.when(to_cell < cell)
            def _(to_cell=to_cell, to_wall=to_wall):
                pl.semaphore_signal(
                    ready.at[cell],
                    inc=1,
                    device_id={"cell": to_cell, "wall": to_wall},
                    device_id_type=MESH,
                )

    for to_wall in range(walls - 1):

        @pl.when(to_wall < wall)
        def _(to_wall=to_wall):
            pl.semaphore_signal(
                ready_near.at[wall], inc=1, device_id={"wall": to_wall}, device_id_type=MESH
            )

    def remote(given, held, send, recv, **to):
        return pltpu.make_async_remote_copy(
            given, held, send, recv, device_id=to, device_id_type=MESH
        )

    def block_copy(to_cell, to_chip):
        return remote(
            own_block,
            block_all.at[cell, chip],
            block_send,
            block_recv.at[cell],
            cell=to_cell,
            wall=2 * to_chip + other_core,
        )

    def lag_copy(to_cell, to_wall):
        return remote(
            own_lag, lag_all.at[cell * walls + wall], lag_send, lag_recv, cell=to_cell, wall=to_wall
        )

    def mem_copy(to_cell):
        return remote(
            mem_all.at[cell],
            mem_all.at[cell],
            mem_send,
            mem_recv.at[cell],
            cell=to_cell,
            wall=partner,
        )

    def share_copy(to_cell):
        return remote(
            share_out.at[to_cell],
            share_in.at[cell],
            share_send,
            share_recv,
            cell=to_cell,
            wall=partner,
        )

    def wall_copy(to_wall):
        held = wall_all.at[wall]
        return remote(held, held, wall_send, wall_recv.at[wall], wall=to_wall)

    def second_copy(to_wall):
        held = second_all.at[wall]
        return remote(
            held, held, second_send, second_recv, wall=to_wall
        )

    def data_copy(to_wall):
        held = data_all.at[wall]
        return remote(held, held, data_send, data_recv, wall=to_wall)

    def near_walls(body):
        for to_wall in range(walls):

            @pl.when(to_wall != wall)
            def _(to_wall=to_wall):
                body(to_wall)

    def far_cells(test, body):
        for to_cell in range(cells):

            @pl.when(test(to_cell))
            def _(to_cell=to_cell):
                body(to_cell)

    def start_blocks(to_cell):
        for to_chip in (other_chip, chip):
            block_copy(to_cell, to_chip).start()

    def start_lag(to_cell):
        for to_wall in range(walls):
            lag_copy(to_cell, to_wall).start()

    loads[4].wait()
    far_cells(lambda to_cell: to_cell < cell, lambda to_cell: mem_copy(to_cell).start())
    for load in loads[5:7]:
        load.wait()
    for to_wall in range(walls - 1):

        @pl.when(to_wall < wall)
        def _(to_wall=to_wall):
            wall_copy(to_wall).start()

    row_ids = lax.broadcasted_iota(jnp.int32, (columns, columns), 0)
    col_ids = lax.broadcasted_iota(jnp.int32, (columns, columns), 1)
    loads[0].wait()
    wanted = jnp.zeros((columns, columns), jnp.int32)
    for k in range(columns):
        wanted = jnp.where(row_ids == k, order_smem[0, k], wanted)
    gather_f32 = (wanted == col_ids).astype(jnp.float32)
    gather = gather_f32.astype(jnp.bfloat16)

    loads[2].wait()
    rows = [jnp.dot(gather, force_ref[j], preferred_element_type=jnp.float32) for j in range(3)]
    folded = halfway // 2
    part = [row[:halfway] for row in rows]
    pair = jnp.concatenate([part[0], part[1]], axis=1)
    last = jnp.concatenate([part[2][:folded], part[2][folded:]], axis=1)
    own_block[...] = jnp.concatenate([pair, last], axis=0).astype(jnp.bfloat16)

    part = [row[halfway:] for row in rows]
    unused = jnp.zeros((halfway, LANES - own_points), jnp.float32)
    second_all[wall, 0] = jnp.concatenate([part[0], part[1]], axis=1).astype(jnp.bfloat16)
    second_all[wall, 1] = jnp.concatenate([part[2], unused], axis=1).astype(jnp.bfloat16)

    for to_wall in range(walls - 1):

        @pl.when(to_wall < wall)
        def _(to_wall=to_wall):
            second_copy(to_wall).start()

    far_cells(lambda to_cell: to_cell < cell, start_blocks)

    loads[3].wait()
    pieces = [lag_ref[j].astype(jnp.float32) for j in range(3)]
    if LANES > 3 * shard_width:
        pieces.append(jnp.zeros((halfway, LANES - 3 * shard_width), jnp.float32))
    packed_lag = jnp.concatenate(pieces, axis=1).astype(jnp.bfloat16)
    own_lag[...] = packed_lag
    lag_all[cell * walls + wall] = packed_lag

    far_cells(lambda to_cell: to_cell < cell, start_lag)

    for to_wall in range(1, walls):

        @pl.when(to_wall > wall)
        def _(to_wall=to_wall):
            pl.semaphore_wait(ready_near.at[to_wall], 1)
            wall_copy(to_wall).start()

    def start_near(to_wall):
        @pl.when(to_wall > wall)
        def _():
            second_copy(to_wall).start()

        @pl.when(to_wall % 2 != core)
        def _():
            block_copy(cell, to_wall // 2).start()

    def start_near_lag(to_wall):
        lag_copy(cell, to_wall).start()

    near_walls(start_near)
    near_walls(start_near_lag)

    loads[7].wait()
    data_rows = [
        jnp.dot(gather_f32, data_ref[j], precision=lax.Precision.HIGHEST) for j in range(3)
    ]
    for j in range(3):
        data_all[wall, j] = data_rows[j][:halfway]
    near_walls(lambda to_wall: data_copy(to_wall).start())

    loads[1].wait()
    scatter = (row_ids == order_ref[...]).astype(jnp.float32).astype(jnp.bfloat16)

    def spread_wall(source):
        for j in range(3):
            wall_cols[source, j] = jnp.broadcast_to(
                wall_all[source, 0, j : j + 1, :], (LANES, wall_count)
            ).T

    for j in range(3):
        mem_cols[j] = jnp.broadcast_to(mem_all[cell, j : j + 1, :], (LANES, point_count)).T

    lane_ids = lax.broadcasted_iota(jnp.int32, (8, LANES), 1)

    def mem_rows(source, parity):
        rows = []
        for j in range(3):
            low = jnp.broadcast_to(mem_all[source, j : j + 1, :LANES], (8, LANES))
            high = jnp.broadcast_to(mem_all[source, j : j + 1, LANES:], (8, LANES))
            low = pltpu.roll(low, own_points * parity, 1)
            high = pltpu.roll(high, own_points * (1 - parity), 1)
            rows.append(jnp.where(lane_ids < own_points, low, high)[0:1])
        return rows

    def fill_single(tile, rows, at):
        apart = [wall_cols[at, j] - rows[j] for j in range(3)]
        square = apart[0] * apart[0] + apart[1] * apart[1] + apart[2] * apart[2]
        inverse = lax.rsqrt(square)
        scaled = stokes_coef * inverse
        cube = scaled * (inverse * inverse)
        for j in range(3):
            along = apart[j] * cube
            for i in range(j + 1):
                element = along * apart[i]
                if i == j:
                    element = element + scaled
                at_tile = TILES.index((i, j))
                tile[:, at_tile * LANES : (at_tile + 1) * LANES] = element.astype(jnp.bfloat16)

    def fill_double(source):
        own = pl.ds(pl.multiple_of(wall * own_points, own_points), own_points)
        apart = [mem_cols[j, own, :] - wall_all[source, 0, j : j + 1, :] for j in range(3)]
        square = apart[0] * apart[0] + apart[1] * apart[1] + apart[2] * apart[2]
        inverse = lax.rsqrt(square)
        flux = (
            apart[0] * wall_all[source, 1, 0:1, :]
            + apart[1] * wall_all[source, 1, 1:2, :]
            + apart[2] * wall_all[source, 1, 2:3, :]
        )
        inverse_square = inverse * inverse
        fifth = inverse_square * inverse_square * inverse
        weight = (-6.0 * stokes_coef) * flux * fifth
        for j in range(3):
            along = apart[j] * weight
            for i in range(j + 1):
                element = (along * apart[i]).astype(jnp.bfloat16)
                for a, b in {(i, j), (j, i)}:
                    lanes = pl.multiple_of(source * block + b * wall_count, wall_count)
                    double_all[
                        a * own_points : (a + 1) * own_points, pl.ds(lanes, wall_count)
                    ] = element

    own_rows = mem_rows(cell, other_core)
    spread_wall(wall)
    fill_single(single_all.at[0, wall], own_rows, wall)
    fill_double(wall)

    def wait_into(held, recv):
        remote(held, held, load_sem.at[0], recv, wall=partner).wait_recv()

    def wait_out(held, send):
        remote(held, held, send, load_sem.at[0], wall=partner).wait_send()

    peers = (partner, 2 * other_chip + other_core, 2 * other_chip + core)

    def take_wall(peer):
        wait_into(wall_all.at[peer], wall_recv.at[peer])
        spread_wall(peer)
        fill_single(single_all.at[0, peer], own_rows, peer)
        fill_double(peer)

    def start_above(up):
        def body(to_cell):
            pl.semaphore_wait(ready.at[to_cell], walls)
            mem_copy(to_cell).start()
            start_blocks(to_cell)

        far_cells(lambda to_cell: to_cell == cell + up, body)

    low_lanes = lax.broadcasted_iota(jnp.int32, (halfway, LANES), 1) < own_points

    def low_halves(first, second):
        mask = low_lanes[: first.shape[0]]
        return jnp.where(mask, first, pltpu.roll(second, own_points, 1))

    def high_halves(first, second):
        mask = low_lanes[: first.shape[0]]
        return jnp.where(mask, pltpu.roll(first, own_points, 1), second)

    def stack_rows(parts):
        empty = jnp.zeros((halfway, LANES), jnp.bfloat16)
        groups = []
        for i in range(3):
            row = [empty] * len(TILES)
            for at_tile, (a, b) in enumerate(TILES):
                if i in (a, b):
                    row[at_tile] = parts[a + b - i].astype(jnp.bfloat16)
            groups.append(jnp.concatenate(row, axis=1))
        return jnp.concatenate(groups, axis=0)

    def second_columns(tiles):
        pair = [tile[0].astype(jnp.float32) for tile in tiles]
        last = [tile[1].astype(jnp.float32) for tile in tiles]
        return stack_rows([low_halves(*pair), high_halves(*pair), low_halves(*last)])

    def columns_of(tiles):
        tiles = [tile.astype(jnp.float32) for tile in tiles]
        pair = [tile[:halfway] for tile in tiles]
        last = [tile[halfway:] for tile in tiles]
        last = jnp.concatenate([low_halves(*last), high_halves(*last)], axis=0)
        return stack_rows([low_halves(*pair), high_halves(*pair), last])

    take_wall(partner)
    fill_single(single_rest, mem_rows(cell, core), partner)
    start_above(1)
    take_wall(peers[1])
    for up in range(2, cells - 1):
        start_above(up)

    wait_into(second_all.at[: walls - 1], second_recv)
    share = jnp.zeros((3 * halfway, wall_count), jnp.float32)
    for parity, tile in ((other_core, single_all.at[0, partner]), (core, single_rest)):
        share = share + lax.dot_general(
            second_columns([second_all[2 * at + parity] for at in range(2)]),
            tile[...],
            NT,
            preferred_element_type=jnp.float32,
        )
    for to_cell in range(cells):
        pieces = [
            share[
                i * halfway : (i + 1) * halfway,
                to_cell * shard_width : (to_cell + 1) * shard_width,
            ]
            for i in range(3)
        ]
        if LANES > 3 * shard_width:
            pieces.append(jnp.zeros((halfway, LANES - 3 * shard_width), jnp.float32))
        share_out[to_cell] = jnp.concatenate(pieces, axis=1).astype(jnp.bfloat16)
    far_cells(lambda to_cell: to_cell <= cell, lambda to_cell: share_copy(to_cell).start())
    if cells > 2:
        start_above(cells - 1)
    far_cells(lambda to_cell: to_cell > cell, lambda to_cell: share_copy(to_cell).start())
    far_cells(lambda to_cell: to_cell > cell, start_lag)
    take_wall(peers[2])

    def source_at(step):
        if step == 0:
            return cell
        return jnp.where(cell + step < cells, cell + step, cells - 1 - step)

    def wait_mem(step):
        source = source_at(step)
        wait_into(mem_all.at[source], mem_recv.at[source])

    def take_mem(step):
        rows = mem_rows(source_at(step), other_core)
        for at in range(walls):
            fill_single(single_all.at[step, at], rows, at)

    def first_columns(step):
        source = source_at(step)
        wait_into(block_all.at[source], block_recv.at[source])
        return columns_of([block_all[source, at] for at in range(2)])

    def exchange(half):
        return remote(
            part_mine.at[half],
            part_other.at[half],
            part_send.at[half],
            part_recv.at[half],
            wall=partner,
        )

    width = walls // 2 * wall_count
    partial = [jnp.zeros((3 * halfway, width), jnp.float32) for _ in range(2)]
    for step in range(cells):
        if step + 1 < cells:
            wait_mem(step + 1)
        left = first_columns(step)
        if step + 1 < cells:
            take_mem(step + 1)
        for half in range(2):
            tile = single_all[step, half * (walls // 2) : (half + 1) * (walls // 2)]
            partial[half] = partial[half] + lax.dot_general(
                left,
                tile.reshape(width, len(TILES) * LANES),
                NT,
                preferred_element_type=jnp.float32,
            )
            if step == cells - 1:
                part_mine[half] = partial[half]
                exchange(half).start()

    wait_out(mem_all.at[: cells - 1], mem_send)
    wait_out(block_all, block_send)
    wait_out(lag_all.at[: cells * walls - 1], lag_send)
    wait_out(wall_all.at[: walls - 1], wall_send)
    wait_out(second_all.at[: walls - 1], second_send)
    wait_into(data_all.at[: walls - 1], data_recv)
    wait_out(data_all.at[: walls - 1], data_send)
    wait_out(share_in, share_send)

    wait_into(lag_all.at[: cells * walls - 1], lag_recv)

    def layer(rows):
        return lax.dot_general(rows, double_all[...], NT, preferred_element_type=jnp.float32)

    lag_row = []
    for source in range(walls):
        lag_row += [
            lag_all[k * walls + source, :, j * shard_width : (j + 1) * shard_width]
            for j in range(3)
            for k in range(cells)
        ]
    lag_part = layer(jnp.concatenate(lag_row, axis=1))

    for half in range(2):
        exchange(half).wait_recv()
    pieces = []
    for source in range(walls):
        for i in range(3):
            half, at = divmod(source, walls // 2)
            held = slice(i * halfway, (i + 1) * halfway)
            lanes = slice(at * wall_count, (at + 1) * wall_count)
            velocity = part_mine[half, held, lanes] + part_other[half, held, lanes]
            dense = 2.0 * (data_all[source, i] - velocity)
            pieces.append(dense.astype(jnp.bfloat16))
    batched = jnp.concatenate([lag_part, layer(jnp.concatenate(pieces, axis=1))], axis=0)
    total = jnp.zeros((columns, 3 * own_points), jnp.float32)
    for _ in range(3):
        piece = batched.astype(jnp.bfloat16)
        total = total + jnp.dot(scatter, piece, preferred_element_type=jnp.float32)
        batched = batched - piece.astype(jnp.float32)
    for i in range(3):
        out_ref[i] = total[:, i * own_points : (i + 1) * own_points]

    wait_into(share_in, share_recv)
    second_sum = jnp.zeros((halfway, LANES), jnp.float32)
    for source in range(cells):
        second_sum = second_sum + share_in[source].astype(jnp.float32)
    shift = lax.rem((cells - cell) * shard_width, wall_count)
    for i in range(3):
        held = pltpu.roll(data_rows[i][halfway:], shift, 1)[:, :shard_width]
        density_ref[i] = 2.0 * (held - second_sum[:, i * shard_width : (i + 1) * shard_width])

    for half in range(2):
        exchange(half).wait_send()


def write_kernel(velocity_ref, density_ref, velocity_hbm, density_hbm, sem):
    first = pltpu.make_async_copy(velocity_ref, velocity_hbm, sem.at[0])
    second = pltpu.make_async_copy(density_ref, density_hbm, sem.at[1])
    first.start()
    second.start()
    first.wait()
    second.wait()


def fused_shards(cells, walls, mem_pos, forces, wall_pos, wall_normal, wall_data, lag_density, batch_order):
    columns = forces.shape[0]
    halfway = columns // 2
    point_count = mem_pos.shape[1]
    wall_count = wall_pos.shape[1]
    own_points = forces.shape[2]
    shard_width = lag_density.shape[2]
    dma = pltpu.SemaphoreType.DMA
    vmem = pl.BlockSpec(memory_space=pltpu.VMEM)
    hbm = pl.BlockSpec(memory_space=pltpu.HBM)
    velocity, density = pl.pallas_call(
        functools.partial(fused_kernel, cells, walls),
        out_shape=(
            pltpu.VMEM((3, columns, own_points), jnp.float32),
            pltpu.VMEM((3, halfway, shard_width), jnp.float32),
        ),
        in_specs=[hbm] * 7,
        out_specs=(vmem, vmem),
        scratch_shapes=[
            pltpu.VMEM((1, columns), jnp.int32),
            pltpu.SMEM((1, columns), jnp.int32),
            pltpu.VMEM((3, columns, own_points), jnp.bfloat16),
            pltpu.VMEM((3, halfway, shard_width), jnp.bfloat16),
            pltpu.VMEM((3, columns, wall_count), jnp.float32),
            pltpu.VMEM((3 * halfway // 2, LANES), jnp.bfloat16),
            pltpu.VMEM((halfway, LANES), jnp.bfloat16),
            pltpu.VMEM((cells, 2, 3 * halfway // 2, LANES), jnp.bfloat16),
            pltpu.VMEM((walls, 2, halfway, LANES), jnp.bfloat16),
            pltpu.VMEM((cells * walls, halfway, LANES), jnp.bfloat16),
            pltpu.VMEM((cells, 3, point_count), jnp.float32),
            pltpu.VMEM((walls, 2, 3, wall_count), jnp.float32),
            pltpu.VMEM((walls, 3, halfway, wall_count), jnp.float32),
            pltpu.VMEM((walls, 3, wall_count, LANES), jnp.float32),
            pltpu.VMEM((3, point_count, LANES), jnp.float32),
            pltpu.VMEM((cells, walls, wall_count, len(TILES) * LANES), jnp.bfloat16),
            pltpu.VMEM((wall_count, len(TILES) * LANES), jnp.bfloat16),
            pltpu.VMEM((3 * own_points, walls * 3 * wall_count), jnp.bfloat16),
            pltpu.VMEM((2, 3 * halfway, walls // 2 * wall_count), jnp.float32),
            pltpu.VMEM((2, 3 * halfway, walls // 2 * wall_count), jnp.float32),
            pltpu.VMEM((cells, halfway, LANES), jnp.bfloat16),
            pltpu.VMEM((cells, halfway, LANES), jnp.bfloat16),
            dma((8,)),
            dma,
            dma((cells,)),
            dma,
            dma,
            dma,
            dma,
            dma,
            dma((cells,)),
            dma,
            dma((walls,)),
            dma,
            dma,
            dma((2,)),
            dma((2,)),
            dma,
            dma,
            pltpu.SemaphoreType.REGULAR((cells,)),
            pltpu.SemaphoreType.REGULAR((walls,)),
        ],
        compiler_params=pltpu.CompilerParams(
            collective_id=0, has_side_effects=True, vmem_limit_bytes=VMEM_GRANT
        ),
        name="coupling",
    )(
        mem_pos,
        jnp.transpose(forces, (1, 0, 2)),
        wall_pos,
        wall_normal,
        jnp.transpose(wall_data, (1, 0, 2)),
        jnp.transpose(lag_density, (1, 0, 2)),
        batch_order.reshape(1, columns),
    )
    velocity, density = pl.pallas_call(
        write_kernel,
        out_shape=(
            jax.ShapeDtypeStruct(velocity.shape, velocity.dtype),
            jax.ShapeDtypeStruct(density.shape, density.dtype),
        ),
        in_specs=[vmem] * 2,
        out_specs=(hbm, hbm),
        scratch_shapes=[dma((2,))],
        compiler_params=pltpu.CompilerParams(vmem_limit_bytes=1024 * 1024),
        name="write",
    )(velocity, density)
    return (jnp.transpose(velocity, (1, 0, 2)), jnp.transpose(density, (1, 0, 2)))


VMEM_GRANT = 60 * 1024 * 1024


def step(cells, walls, mem_pos, forces, wall_pos, *rest):
    point_count = mem_pos.shape[1]
    wall_count = wall_pos.shape[1]
    own_points = forces.shape[2]
    shard_width = rest[2].shape[2]
    tiles = 18 * walls * wall_count * (cells * LANES + own_points)
    fits = tiles <= VMEM_GRANT // 2
    aligned = (
        walls == 4
        and wall_count == LANES
        and 2 * own_points == LANES
        and point_count == walls * own_points
        and wall_count == cells * shard_width
        and 3 * shard_width <= LANES
    )
    if fits and aligned:
        return fused_shards(cells, walls, mem_pos, forces, wall_pos, *rest)
    return shards(mem_pos, forces, wall_pos, *rest)


def solution(mesh):
    placed = (
        P(None, ("groups", "cell")),
        P(None, None, ("groups", "cell", "wall")),
        P(None, ("groups", "wall")),
        P(None, ("groups", "wall")),
        P(None, None, ("groups", "wall")),
        P(None, None, ("groups", "wall", "cell")),
        P(),
    )
    return jax.shard_map(
        functools.partial(step, mesh.shape["cell"], mesh.shape["wall"]),
        mesh=mesh,
        in_specs=placed,
        out_specs=(
            P(None, None, ("groups", "cell", "wall")),
            P(None, None, ("groups", "wall", "cell")),
        ),
        check_vma=False,
    )
```

```python
import functools
import math

import jax
import jax.numpy as jnp
from jax import lax
from jax.experimental import pallas as pl
from jax.experimental.pallas import tpu as pltpu
from jax.sharding import PartitionSpec as P

stokes_coef = 1.0 / (8.0 * math.pi)


def single_tile(targets, sources):
    separation = targets[:, None, :] - sources[:, :, None]
    inverse = lax.rsqrt(jnp.sum(separation * separation, axis=0))
    inverse_cube = inverse * inverse * inverse
    stacked = []
    for second_dim in range(3):
        entries_row = []
        for first_dim in range(3):
            element = separation[first_dim] * separation[second_dim] * inverse_cube
            if first_dim == second_dim:
                element = element + inverse
            entries_row.append(element * stokes_coef)
        stacked.append(jnp.stack(entries_row, axis=1))
    kernel_tile = jnp.stack(stacked, axis=0)
    return kernel_tile.reshape(3 * sources.shape[1], 3 * targets.shape[1]).astype(jnp.bfloat16)


def double_tile(targets, sources, normals):
    separation = targets[:, None, :] - sources[:, :, None]
    inverse = lax.rsqrt(jnp.sum(separation * separation, axis=0))
    normal_flux = jnp.sum(separation * normals[:, :, None], axis=0)
    weight = -6.0 * stokes_coef * normal_flux * inverse**5
    stacked = []
    for second_dim in range(3):
        entries_row = []
        for first_dim in range(3):
            entries_row.append(weight * separation[first_dim] * separation[second_dim])
        stacked.append(jnp.stack(entries_row, axis=1))
    kernel_tile = jnp.stack(stacked, axis=0)
    return kernel_tile.reshape(3 * sources.shape[1], 3 * targets.shape[1]).astype(jnp.bfloat16)


def shards(mem_pos, forces, wall_pos, wall_normal, wall_data, lag_density, batch_order):
    columns = forces.shape[0]
    halfway = columns // 2
    point_count = mem_pos.shape[1]
    wall_count = wall_pos.shape[1]
    shard_width = lag_density.shape[2]
    piece_len = math.gcd(point_count, 128)
    block_count = point_count // piece_len
    first_rows = batch_order[:halfway]
    second_rows = batch_order[halfway:]
    force_block = lax.all_gather(forces, "wall", axis=2, tiled=True)
    lag_block = lax.all_gather(lag_density, "cell", axis=2, tiled=True)
    lag_flat = lag_block.reshape(halfway, 3 * wall_count)

    def position_at(block_index):
        return lax.dynamic_slice_in_dim(mem_pos, block_index * piece_len, piece_len, 1)

    def single_term(block_index):
        loaded = lax.dynamic_slice_in_dim(force_block, block_index * piece_len, piece_len, 2)
        loaded = loaded.reshape(columns, 3 * piece_len)
        return jnp.dot(
            loaded,
            single_tile(wall_pos, position_at(block_index)),
            preferred_element_type=jnp.float32,
        )

    def double_term(dense_rows, block_index):
        kernel_tile = double_tile(position_at(block_index), wall_pos, wall_normal)
        product = jnp.dot(dense_rows, kernel_tile, preferred_element_type=jnp.float32)
        return product.reshape(dense_rows.shape[0], 3, piece_len)

    def place_block(target, piece, block_index):
        return lax.dynamic_update_slice_in_dim(target, piece, block_index * piece_len, 2)

    empty_wall = jnp.zeros((columns, 3 * wall_count), jnp.float32)

    def add_single(block_index, running):
        return running + single_term(block_index)

    running = lax.fori_loop(0, block_count, add_single, empty_wall)
    wall_term = running.reshape(columns, 3, wall_count)
    position_cell = lax.axis_index("cell")
    first_sum = lax.psum(jnp.take(wall_term, first_rows, axis=0), "cell")
    first_block = (2.0 * (jnp.take(wall_data, first_rows, axis=0) - first_sum)).astype(jnp.bfloat16)
    second_sum = lax.psum_scatter(
        jnp.take(wall_term, second_rows, axis=0).astype(jnp.bfloat16),
        "cell",
        scatter_dimension=2,
        tiled=True,
    ).astype(jnp.float32)
    second_data = lax.dynamic_slice_in_dim(
        jnp.take(wall_data, second_rows, axis=0), position_cell * shard_width, shard_width, 2
    )
    wall_density = 2.0 * (second_data - second_sum)
    first_flat = first_block.reshape(halfway, 3 * wall_count)
    carried = jnp.concatenate([lag_flat, first_flat], axis=0)

    def all_terms(block_index, target):
        return place_block(target, double_term(carried, block_index), block_index)

    membrane_term = lax.fori_loop(
        0, block_count, all_terms, jnp.zeros((columns, 3, point_count), jnp.float32)
    )
    batched = lax.psum_scatter(membrane_term, "wall", scatter_dimension=2, tiled=True)
    membrane_velocity = jnp.zeros_like(batched).at[batch_order].set(batched)
    return (membrane_velocity, wall_density)

LANES = 128
MESH = pl.DeviceIdType.MESH
NT = (((1,), (1,)), ((), ()))


TILES = ((0, 0), (1, 1), (2, 2), (0, 1), (0, 2), (1, 2))


def fused_kernel(
    cells,
    walls,
    mem_hbm,
    force_hbm,
    wall_hbm,
    normal_hbm,
    data_hbm,
    lag_hbm,
    order_hbm,
    out_ref,
    density_ref,
    order_ref,
    order_smem,
    force_ref,
    lag_ref,
    data_ref,
    own_block,
    own_lag,
    block_all,
    second_all,
    lag_all,
    mem_all,
    wall_all,
    data_all,
    wall_cols,
    mem_cols,
    single_all,
    single_rest,
    double_all,
    part_mine,
    part_other,
    share_out,
    share_in,
    load_sem,
    block_send,
    block_recv,
    second_send,
    second_recv,
    lag_send,
    lag_recv,
    mem_send,
    mem_recv,
    wall_send,
    wall_recv,
    data_send,
    data_recv,
    part_send,
    part_recv,
    share_send,
    share_recv,
    ready,
    ready_near,
):
    cell = lax.axis_index("cell")
    wall = lax.axis_index("wall")
    chip = lax.div(wall, 2)
    core = lax.rem(wall, 2)
    other_core = 1 - core
    other_chip = 1 - chip
    columns = order_ref.shape[1]
    halfway = columns // 2
    point_count = mem_hbm.shape[1]
    wall_count = wall_hbm.shape[1]
    own_points = force_ref.shape[2]
    shard_width = lag_ref.shape[2]
    block = 3 * wall_count
    partner = 2 * chip + other_core

    loads = [
        pltpu.make_async_copy(given, held, load_sem.at[at])
        for at, (given, held) in enumerate(
            (
                (order_hbm, order_smem),
                (order_hbm, order_ref),
                (force_hbm, force_ref),
                (lag_hbm, lag_ref),
                (mem_hbm, mem_all.at[cell]),
                (wall_hbm, wall_all.at[wall, 0]),
                (normal_hbm, wall_all.at[wall, 1]),
                (data_hbm, data_ref),
            )
        )
    ]
    for load in loads:
        load.start()

    barrier = pltpu.get_barrier_semaphore()
    for to_cell in range(cells - 1, -1, -1):
        for to_wall in range(walls):

            @pl.when((to_cell > cell) | ((to_cell == cell) & (to_wall > wall)))
            def _(to_cell=to_cell, to_wall=to_wall):
                pl.semaphore_signal(
                    barrier,
                    inc=1,
                    device_id={"cell": to_cell, "wall": to_wall},
                    device_id_type=MESH,
                )

    below = walls * cell + wall

    @pl.when(below > 0)
    def _():
        pl.semaphore_wait(barrier, below)

    for to_cell in range(cells - 1):
        for to_wall in range(walls):

            @pl.when(to_cell < cell)
            def _(to_cell=to_cell, to_wall=to_wall):
                pl.semaphore_signal(
                    ready.at[cell],
                    inc=1,
                    device_id={"cell": to_cell, "wall": to_wall},
                    device_id_type=MESH,
                )

    for to_wall in range(walls - 1):

        @pl.when(to_wall < wall)
        def _(to_wall=to_wall):
            pl.semaphore_signal(
                ready_near.at[wall], inc=1, device_id={"wall": to_wall}, device_id_type=MESH
            )

    def remote(given, held, send, recv, **to):
        return pltpu.make_async_remote_copy(
            given, held, send, recv, device_id=to, device_id_type=MESH
        )

    def block_copy(to_cell, to_chip):
        return remote(
            own_block,
            block_all.at[cell, chip],
            block_send,
            block_recv.at[cell],
            cell=to_cell,
            wall=2 * to_chip + other_core,
        )

    def lag_copy(to_cell, to_wall):
        return remote(
            own_lag, lag_all.at[cell * walls + wall], lag_send, lag_recv, cell=to_cell, wall=to_wall
        )

    def mem_copy(to_cell):
        return remote(
            mem_all.at[cell],
            mem_all.at[cell],
            mem_send,
            mem_recv.at[cell],
            cell=to_cell,
            wall=partner,
        )

    def share_copy(to_cell):
        return remote(
            share_out.at[to_cell],
            share_in.at[cell],
            share_send,
            share_recv,
            cell=to_cell,
            wall=partner,
        )

    def wall_copy(to_wall):
        held = wall_all.at[wall]
        return remote(held, held, wall_send, wall_recv.at[wall], wall=to_wall)

    def second_copy(to_wall):
        held = second_all.at[wall]
        return remote(
            held, held, second_send, second_recv, wall=to_wall
        )

    def data_copy(to_wall):
        held = data_all.at[wall]
        return remote(held, held, data_send, data_recv, wall=to_wall)

    def near_walls(body):
        for to_wall in range(walls):

            @pl.when(to_wall != wall)
            def _(to_wall=to_wall):
                body(to_wall)

    def far_cells(test, body):
        for to_cell in range(cells):

            @pl.when(test(to_cell))
            def _(to_cell=to_cell):
                body(to_cell)

    def start_blocks(to_cell):
        for to_chip in (other_chip, chip):
            block_copy(to_cell, to_chip).start()

    def start_lag(to_cell):
        for to_wall in range(walls):
            lag_copy(to_cell, to_wall).start()

    loads[4].wait()
    far_cells(lambda to_cell: to_cell < cell, lambda to_cell: mem_copy(to_cell).start())
    for load in loads[5:7]:
        load.wait()
    for to_wall in range(walls - 1):

        @pl.when(to_wall < wall)
        def _(to_wall=to_wall):
            wall_copy(to_wall).start()

    row_ids = lax.broadcasted_iota(jnp.int32, (columns, columns), 0)
    col_ids = lax.broadcasted_iota(jnp.int32, (columns, columns), 1)
    loads[0].wait()
    wanted = jnp.zeros((columns, columns), jnp.int32)
    for k in range(columns):
        wanted = jnp.where(row_ids == k, order_smem[0, k], wanted)
    gather_f32 = (wanted == col_ids).astype(jnp.float32)
    gather = gather_f32.astype(jnp.bfloat16)

    loads[2].wait()
    rows = [jnp.dot(gather, force_ref[j], preferred_element_type=jnp.float32) for j in range(3)]
    folded = halfway // 2
    part = [row[:halfway] for row in rows]
    pair = jnp.concatenate([part[0], part[1]], axis=1)
    last = jnp.concatenate([part[2][:folded], part[2][folded:]], axis=1)
    own_block[...] = jnp.concatenate([pair, last], axis=0).astype(jnp.bfloat16)

    part = [row[halfway:] for row in rows]
    unused = jnp.zeros((halfway, LANES - own_points), jnp.float32)
    second_all[wall, 0] = jnp.concatenate([part[0], part[1]], axis=1).astype(jnp.bfloat16)
    second_all[wall, 1] = jnp.concatenate([part[2], unused], axis=1).astype(jnp.bfloat16)

    for to_wall in range(walls - 1):

        @pl.when(to_wall < wall)
        def _(to_wall=to_wall):
            second_copy(to_wall).start()

    far_cells(lambda to_cell: to_cell < cell, start_blocks)

    loads[3].wait()
    pieces = [lag_ref[j].astype(jnp.float32) for j in range(3)]
    if LANES > 3 * shard_width:
        pieces.append(jnp.zeros((halfway, LANES - 3 * shard_width), jnp.float32))
    packed_lag = jnp.concatenate(pieces, axis=1).astype(jnp.bfloat16)
    own_lag[...] = packed_lag
    lag_all[cell * walls + wall] = packed_lag

    far_cells(lambda to_cell: to_cell < cell, start_lag)

    for to_wall in range(1, walls):

        @pl.when(to_wall > wall)
        def _(to_wall=to_wall):
            pl.semaphore_wait(ready_near.at[to_wall], 1)
            wall_copy(to_wall).start()

    def start_near(to_wall):
        @pl.when(to_wall > wall)
        def _():
            second_copy(to_wall).start()

        @pl.when(to_wall % 2 != core)
        def _():
            block_copy(cell, to_wall // 2).start()

    def start_near_lag(to_wall):
        lag_copy(cell, to_wall).start()

    near_walls(start_near)
    near_walls(start_near_lag)

    loads[7].wait()
    data_rows = [
        jnp.dot(gather_f32, data_ref[j], precision=lax.Precision.HIGHEST) for j in range(3)
    ]
    for j in range(3):
        data_all[wall, j] = data_rows[j][:halfway]
    near_walls(lambda to_wall: data_copy(to_wall).start())

    loads[1].wait()
    scatter = (row_ids == order_ref[...]).astype(jnp.float32).astype(jnp.bfloat16)

    def spread_wall(source):
        for j in range(3):
            wall_cols[source, j] = jnp.broadcast_to(
                wall_all[source, 0, j : j + 1, :], (LANES, wall_count)
            ).T

    for j in range(3):
        mem_cols[j] = jnp.broadcast_to(mem_all[cell, j : j + 1, :], (LANES, point_count)).T

    lane_ids = lax.broadcasted_iota(jnp.int32, (8, LANES), 1)

    def mem_rows(source, parity):
        rows = []
        for j in range(3):
            low = jnp.broadcast_to(mem_all[source, j : j + 1, :LANES], (8, LANES))
            high = jnp.broadcast_to(mem_all[source, j : j + 1, LANES:], (8, LANES))
            low = pltpu.roll(low, own_points * parity, 1)
            high = pltpu.roll(high, own_points * (1 - parity), 1)
            rows.append(jnp.where(lane_ids < own_points, low, high)[0:1])
        return rows

    def fill_single(tile, rows, at):
        apart = [wall_cols[at, j] - rows[j] for j in range(3)]
        square = apart[0] * apart[0] + apart[1] * apart[1] + apart[2] * apart[2]
        inverse = lax.rsqrt(square)
        scaled = stokes_coef * inverse
        cube = scaled * (inverse * inverse)
        for j in range(3):
            along = apart[j] * cube
            for i in range(j + 1):
                element = along * apart[i]
                if i == j:
                    element = element + scaled
                at_tile = TILES.index((i, j))
                tile[:, at_tile * LANES : (at_tile + 1) * LANES] = element.astype(jnp.bfloat16)

    def fill_double(source):
        own = pl.ds(pl.multiple_of(wall * own_points, own_points), own_points)
        apart = [mem_cols[j, own, :] - wall_all[source, 0, j : j + 1, :] for j in range(3)]
        square = apart[0] * apart[0] + apart[1] * apart[1] + apart[2] * apart[2]
        inverse = lax.rsqrt(square)
        flux = (
            apart[0] * wall_all[source, 1, 0:1, :]
            + apart[1] * wall_all[source, 1, 1:2, :]
            + apart[2] * wall_all[source, 1, 2:3, :]
        )
        inverse_square = inverse * inverse
        fifth = inverse_square * inverse_square * inverse
        weight = (-6.0 * stokes_coef) * flux * fifth
        for j in range(3):
            along = apart[j] * weight
            for i in range(j + 1):
                element = (along * apart[i]).astype(jnp.bfloat16)
                for a, b in {(i, j), (j, i)}:
                    lanes = pl.multiple_of(source * block + b * wall_count, wall_count)
                    double_all[
                        a * own_points : (a + 1) * own_points, pl.ds(lanes, wall_count)
                    ] = element

    own_rows = mem_rows(cell, other_core)
    spread_wall(wall)
    fill_single(single_all.at[0, wall], own_rows, wall)
    fill_double(wall)

    def wait_into(held, recv):
        remote(held, held, load_sem.at[0], recv, wall=partner).wait_recv()

    def wait_out(held, send):
        remote(held, held, send, load_sem.at[0], wall=partner).wait_send()

    peers = (partner, 2 * other_chip + other_core, 2 * other_chip + core)

    def take_wall(peer):
        wait_into(wall_all.at[peer], wall_recv.at[peer])
        spread_wall(peer)
        fill_single(single_all.at[0, peer], own_rows, peer)
        fill_double(peer)

    def start_above(up):
        def body(to_cell):
            pl.semaphore_wait(ready.at[to_cell], walls)
            mem_copy(to_cell).start()
            start_blocks(to_cell)

        far_cells(lambda to_cell: to_cell == cell + up, body)

    low_lanes = lax.broadcasted_iota(jnp.int32, (halfway, LANES), 1) < own_points

    def low_halves(first, second):
        mask = low_lanes[: first.shape[0]]
        return jnp.where(mask, first, pltpu.roll(second, own_points, 1))

    def high_halves(first, second):
        mask = low_lanes[: first.shape[0]]
        return jnp.where(mask, pltpu.roll(first, own_points, 1), second)

    def stack_rows(parts):
        empty = jnp.zeros((halfway, LANES), jnp.bfloat16)
        groups = []
        for i in range(3):
            row = [empty] * len(TILES)
            for at_tile, (a, b) in enumerate(TILES):
                if i in (a, b):
                    row[at_tile] = parts[a + b - i].astype(jnp.bfloat16)
            groups.append(jnp.concatenate(row, axis=1))
        return jnp.concatenate(groups, axis=0)

    def second_columns(tiles):
        pair = [tile[0].astype(jnp.float32) for tile in tiles]
        last = [tile[1].astype(jnp.float32) for tile in tiles]
        return stack_rows([low_halves(*pair), high_halves(*pair), low_halves(*last)])

    def columns_of(tiles):
        tiles = [tile.astype(jnp.float32) for tile in tiles]
        pair = [tile[:halfway] for tile in tiles]
        last = [tile[halfway:] for tile in tiles]
        last = jnp.concatenate([low_halves(*last), high_halves(*last)], axis=0)
        return stack_rows([low_halves(*pair), high_halves(*pair), last])

    take_wall(partner)
    fill_single(single_rest, mem_rows(cell, core), partner)
    start_above(1)
    for up in range(2, cells - 1):
        start_above(up)
    far_cells(lambda to_cell: (to_cell > cell) & (to_cell < cells - 1), start_lag)

    wait_into(second_all.at[: walls - 1], second_recv)
    share = jnp.zeros((3 * halfway, wall_count), jnp.float32)
    for parity, tile in ((other_core, single_all.at[0, partner]), (core, single_rest)):
        share = share + lax.dot_general(
            second_columns([second_all[2 * at + parity] for at in range(2)]),
            tile[...],
            NT,
            preferred_element_type=jnp.float32,
        )
    for to_cell in range(cells):
        pieces = [
            share[
                i * halfway : (i + 1) * halfway,
                to_cell * shard_width : (to_cell + 1) * shard_width,
            ]
            for i in range(3)
        ]
        if LANES > 3 * shard_width:
            pieces.append(jnp.zeros((halfway, LANES - 3 * shard_width), jnp.float32))
        share_out[to_cell] = jnp.concatenate(pieces, axis=1).astype(jnp.bfloat16)
    far_cells(lambda to_cell: to_cell <= cell, lambda to_cell: share_copy(to_cell).start())
    take_wall(peers[1])
    if cells > 2:
        start_above(cells - 1)
    far_cells(lambda to_cell: to_cell > cell, lambda to_cell: share_copy(to_cell).start())
    far_cells(lambda to_cell: (to_cell > cell) & (to_cell == cells - 1), start_lag)
    take_wall(peers[2])

    def source_at(step):
        if step == 0:
            return cell
        return jnp.where(cell + step < cells, cell + step, cells - 1 - step)

    def wait_mem(step):
        source = source_at(step)
        wait_into(mem_all.at[source], mem_recv.at[source])

    def take_mem(step):
        rows = mem_rows(source_at(step), other_core)
        for at in range(walls):
            fill_single(single_all.at[step, at], rows, at)

    def first_columns(step):
        source = source_at(step)
        wait_into(block_all.at[source], block_recv.at[source])
        return columns_of([block_all[source, at] for at in range(2)])

    def exchange(half):
        return remote(
            part_mine.at[half],
            part_other.at[half],
            part_send.at[half],
            part_recv.at[half],
            wall=partner,
        )

    width = walls // 2 * wall_count
    partial = [jnp.zeros((3 * halfway, width), jnp.float32) for _ in range(2)]
    for step in range(cells):
        if step + 1 < cells:
            wait_mem(step + 1)
        left = first_columns(step)
        if step + 1 < cells:
            take_mem(step + 1)
        for half in range(2):
            tile = single_all[step, half * (walls // 2) : (half + 1) * (walls // 2)]
            partial[half] = partial[half] + lax.dot_general(
                left,
                tile.reshape(width, len(TILES) * LANES),
                NT,
                preferred_element_type=jnp.float32,
            )
            if step == cells - 1:
                part_mine[half] = partial[half]
                exchange(half).start()

    wait_out(mem_all.at[: cells - 1], mem_send)
    wait_out(block_all, block_send)
    wait_out(lag_all.at[: cells * walls - 1], lag_send)
    wait_out(wall_all.at[: walls - 1], wall_send)
    wait_out(second_all.at[: walls - 1], second_send)
    wait_into(data_all.at[: walls - 1], data_recv)
    wait_out(data_all.at[: walls - 1], data_send)
    wait_out(share_in, share_send)

    wait_into(lag_all.at[: cells * walls - 1], lag_recv)

    def layer(rows):
        return lax.dot_general(rows, double_all[...], NT, preferred_element_type=jnp.float32)

    lag_row = []
    for source in range(walls):
        lag_row += [
            lag_all[k * walls + source, :, j * shard_width : (j + 1) * shard_width]
            for j in range(3)
            for k in range(cells)
        ]

    moves = [
        jnp.concatenate([scatter[:, :halfway]] * 3, axis=1),
        jnp.concatenate([scatter[:, halfway:]] * 3, axis=1),
    ]

    def move_rows(move, rows):
        held = []
        for _ in range(3):
            piece = rows.astype(jnp.bfloat16)
            held.append(piece)
            rows = rows - piece.astype(jnp.float32)
        return jnp.dot(move, jnp.concatenate(held, axis=0), preferred_element_type=jnp.float32)

    total = move_rows(moves[0], layer(jnp.concatenate(lag_row, axis=1)))

    for half in range(2):
        exchange(half).wait_recv()
    pieces = []
    for source in range(walls):
        for i in range(3):
            half, at = divmod(source, walls // 2)
            held = slice(i * halfway, (i + 1) * halfway)
            lanes = slice(at * wall_count, (at + 1) * wall_count)
            velocity = part_mine[half, held, lanes] + part_other[half, held, lanes]
            dense = 2.0 * (data_all[source, i] - velocity)
            pieces.append(dense.astype(jnp.bfloat16))
    total = total + move_rows(moves[1], layer(jnp.concatenate(pieces, axis=1)))
    for i in range(3):
        out_ref[i] = total[:, i * own_points : (i + 1) * own_points]

    wait_into(share_in, share_recv)
    second_sum = jnp.zeros((halfway, LANES), jnp.float32)
    for source in range(cells):
        second_sum = second_sum + share_in[source].astype(jnp.float32)
    shift = lax.rem((cells - cell) * shard_width, wall_count)
    for i in range(3):
        held = pltpu.roll(data_rows[i][halfway:], shift, 1)[:, :shard_width]
        density_ref[i] = 2.0 * (held - second_sum[:, i * shard_width : (i + 1) * shard_width])

    for half in range(2):
        exchange(half).wait_send()


def write_kernel(velocity_ref, density_ref, velocity_hbm, density_hbm, sem):
    first = pltpu.make_async_copy(velocity_ref, velocity_hbm, sem.at[0])
    second = pltpu.make_async_copy(density_ref, density_hbm, sem.at[1])
    first.start()
    second.start()
    first.wait()
    second.wait()


def fused_shards(cells, walls, mem_pos, forces, wall_pos, wall_normal, wall_data, lag_density, batch_order):
    columns = forces.shape[0]
    halfway = columns // 2
    point_count = mem_pos.shape[1]
    wall_count = wall_pos.shape[1]
    own_points = forces.shape[2]
    shard_width = lag_density.shape[2]
    dma = pltpu.SemaphoreType.DMA
    vmem = pl.BlockSpec(memory_space=pltpu.VMEM)
    hbm = pl.BlockSpec(memory_space=pltpu.HBM)
    velocity, density = pl.pallas_call(
        functools.partial(fused_kernel, cells, walls),
        out_shape=(
            pltpu.VMEM((3, columns, own_points), jnp.float32),
            pltpu.VMEM((3, halfway, shard_width), jnp.float32),
        ),
        in_specs=[hbm] * 7,
        out_specs=(vmem, vmem),
        scratch_shapes=[
            pltpu.VMEM((1, columns), jnp.int32),
            pltpu.SMEM((1, columns), jnp.int32),
            pltpu.VMEM((3, columns, own_points), jnp.bfloat16),
            pltpu.VMEM((3, halfway, shard_width), jnp.bfloat16),
            pltpu.VMEM((3, columns, wall_count), jnp.float32),
            pltpu.VMEM((3 * halfway // 2, LANES), jnp.bfloat16),
            pltpu.VMEM((halfway, LANES), jnp.bfloat16),
            pltpu.VMEM((cells, 2, 3 * halfway // 2, LANES), jnp.bfloat16),
            pltpu.VMEM((walls, 2, halfway, LANES), jnp.bfloat16),
            pltpu.VMEM((cells * walls, halfway, LANES), jnp.bfloat16),
            pltpu.VMEM((cells, 3, point_count), jnp.float32),
            pltpu.VMEM((walls, 2, 3, wall_count), jnp.float32),
            pltpu.VMEM((walls, 3, halfway, wall_count), jnp.float32),
            pltpu.VMEM((walls, 3, wall_count, LANES), jnp.float32),
            pltpu.VMEM((3, point_count, LANES), jnp.float32),
            pltpu.VMEM((cells, walls, wall_count, len(TILES) * LANES), jnp.bfloat16),
            pltpu.VMEM((wall_count, len(TILES) * LANES), jnp.bfloat16),
            pltpu.VMEM((3 * own_points, walls * 3 * wall_count), jnp.bfloat16),
            pltpu.VMEM((2, 3 * halfway, walls // 2 * wall_count), jnp.float32),
            pltpu.VMEM((2, 3 * halfway, walls // 2 * wall_count), jnp.float32),
            pltpu.VMEM((cells, halfway, LANES), jnp.bfloat16),
            pltpu.VMEM((cells, halfway, LANES), jnp.bfloat16),
            dma((8,)),
            dma,
            dma((cells,)),
            dma,
            dma,
            dma,
            dma,
            dma,
            dma((cells,)),
            dma,
            dma((walls,)),
            dma,
            dma,
            dma((2,)),
            dma((2,)),
            dma,
            dma,
            pltpu.SemaphoreType.REGULAR((cells,)),
            pltpu.SemaphoreType.REGULAR((walls,)),
        ],
        compiler_params=pltpu.CompilerParams(
            collective_id=0, has_side_effects=True, vmem_limit_bytes=VMEM_GRANT
        ),
        name="coupling",
    )(
        mem_pos,
        jnp.transpose(forces, (1, 0, 2)),
        wall_pos,
        wall_normal,
        jnp.transpose(wall_data, (1, 0, 2)),
        jnp.transpose(lag_density, (1, 0, 2)),
        batch_order.reshape(1, columns),
    )
    velocity, density = pl.pallas_call(
        write_kernel,
        out_shape=(
            jax.ShapeDtypeStruct(velocity.shape, velocity.dtype),
            jax.ShapeDtypeStruct(density.shape, density.dtype),
        ),
        in_specs=[vmem] * 2,
        out_specs=(hbm, hbm),
        scratch_shapes=[dma((2,))],
        compiler_params=pltpu.CompilerParams(vmem_limit_bytes=1024 * 1024),
        name="write",
    )(velocity, density)
    return (jnp.transpose(velocity, (1, 0, 2)), jnp.transpose(density, (1, 0, 2)))


VMEM_GRANT = 60 * 1024 * 1024


def step(cells, walls, mem_pos, forces, wall_pos, *rest):
    point_count = mem_pos.shape[1]
    wall_count = wall_pos.shape[1]
    own_points = forces.shape[2]
    shard_width = rest[2].shape[2]
    tiles = 18 * walls * wall_count * (cells * LANES + own_points)
    fits = tiles <= VMEM_GRANT // 2
    aligned = (
        walls == 4
        and wall_count == LANES
        and 2 * own_points == LANES
        and point_count == walls * own_points
        and wall_count == cells * shard_width
        and 3 * shard_width <= LANES
    )
    if fits and aligned:
        return fused_shards(cells, walls, mem_pos, forces, wall_pos, *rest)
    return shards(mem_pos, forces, wall_pos, *rest)


def solution(mesh):
    placed = (
        P(None, ("groups", "cell")),
        P(None, None, ("groups", "cell", "wall")),
        P(None, ("groups", "wall")),
        P(None, ("groups", "wall")),
        P(None, None, ("groups", "wall")),
        P(None, None, ("groups", "wall", "cell")),
        P(),
    )
    return jax.shard_map(
        functools.partial(step, mesh.shape["cell"], mesh.shape["wall"]),
        mesh=mesh,
        in_specs=placed,
        out_specs=(
            P(None, None, ("groups", "cell", "wall")),
            P(None, None, ("groups", "wall", "cell")),
        ),
        check_vma=False,
    )
```

```python
import functools
import math

import jax
import jax.numpy as jnp
from jax import lax
from jax.experimental import pallas as pl
from jax.experimental.pallas import tpu as pltpu
from jax.sharding import PartitionSpec as P

stokes_coef = 1.0 / (8.0 * math.pi)


def single_tile(targets, sources):
    separation = targets[:, None, :] - sources[:, :, None]
    inverse = lax.rsqrt(jnp.sum(separation * separation, axis=0))
    inverse_cube = inverse * inverse * inverse
    stacked = []
    for second_dim in range(3):
        entries_row = []
        for first_dim in range(3):
            element = separation[first_dim] * separation[second_dim] * inverse_cube
            if first_dim == second_dim:
                element = element + inverse
            entries_row.append(element * stokes_coef)
        stacked.append(jnp.stack(entries_row, axis=1))
    kernel_tile = jnp.stack(stacked, axis=0)
    return kernel_tile.reshape(3 * sources.shape[1], 3 * targets.shape[1]).astype(jnp.bfloat16)


def double_tile(targets, sources, normals):
    separation = targets[:, None, :] - sources[:, :, None]
    inverse = lax.rsqrt(jnp.sum(separation * separation, axis=0))
    normal_flux = jnp.sum(separation * normals[:, :, None], axis=0)
    weight = -6.0 * stokes_coef * normal_flux * inverse**5
    stacked = []
    for second_dim in range(3):
        entries_row = []
        for first_dim in range(3):
            entries_row.append(weight * separation[first_dim] * separation[second_dim])
        stacked.append(jnp.stack(entries_row, axis=1))
    kernel_tile = jnp.stack(stacked, axis=0)
    return kernel_tile.reshape(3 * sources.shape[1], 3 * targets.shape[1]).astype(jnp.bfloat16)


def shards(mem_pos, forces, wall_pos, wall_normal, wall_data, lag_density, batch_order):
    columns = forces.shape[0]
    halfway = columns // 2
    point_count = mem_pos.shape[1]
    wall_count = wall_pos.shape[1]
    shard_width = lag_density.shape[2]
    piece_len = math.gcd(point_count, 128)
    block_count = point_count // piece_len
    first_rows = batch_order[:halfway]
    second_rows = batch_order[halfway:]
    force_block = lax.all_gather(forces, "wall", axis=2, tiled=True)
    lag_block = lax.all_gather(lag_density, "cell", axis=2, tiled=True)
    lag_flat = lag_block.reshape(halfway, 3 * wall_count)

    def position_at(block_index):
        return lax.dynamic_slice_in_dim(mem_pos, block_index * piece_len, piece_len, 1)

    def single_term(block_index):
        loaded = lax.dynamic_slice_in_dim(force_block, block_index * piece_len, piece_len, 2)
        loaded = loaded.reshape(columns, 3 * piece_len)
        return jnp.dot(
            loaded,
            single_tile(wall_pos, position_at(block_index)),
            preferred_element_type=jnp.float32,
        )

    def double_term(dense_rows, block_index):
        kernel_tile = double_tile(position_at(block_index), wall_pos, wall_normal)
        product = jnp.dot(dense_rows, kernel_tile, preferred_element_type=jnp.float32)
        return product.reshape(dense_rows.shape[0], 3, piece_len)

    def place_block(target, piece, block_index):
        return lax.dynamic_update_slice_in_dim(target, piece, block_index * piece_len, 2)

    empty_wall = jnp.zeros((columns, 3 * wall_count), jnp.float32)

    def add_single(block_index, running):
        return running + single_term(block_index)

    running = lax.fori_loop(0, block_count, add_single, empty_wall)
    wall_term = running.reshape(columns, 3, wall_count)
    position_cell = lax.axis_index("cell")
    first_sum = lax.psum(jnp.take(wall_term, first_rows, axis=0), "cell")
    first_block = (2.0 * (jnp.take(wall_data, first_rows, axis=0) - first_sum)).astype(jnp.bfloat16)
    second_sum = lax.psum_scatter(
        jnp.take(wall_term, second_rows, axis=0).astype(jnp.bfloat16),
        "cell",
        scatter_dimension=2,
        tiled=True,
    ).astype(jnp.float32)
    second_data = lax.dynamic_slice_in_dim(
        jnp.take(wall_data, second_rows, axis=0), position_cell * shard_width, shard_width, 2
    )
    wall_density = 2.0 * (second_data - second_sum)
    first_flat = first_block.reshape(halfway, 3 * wall_count)
    carried = jnp.concatenate([lag_flat, first_flat], axis=0)

    def all_terms(block_index, target):
        return place_block(target, double_term(carried, block_index), block_index)

    membrane_term = lax.fori_loop(
        0, block_count, all_terms, jnp.zeros((columns, 3, point_count), jnp.float32)
    )
    batched = lax.psum_scatter(membrane_term, "wall", scatter_dimension=2, tiled=True)
    membrane_velocity = jnp.zeros_like(batched).at[batch_order].set(batched)
    return (membrane_velocity, wall_density)

LANES = 128
MESH = pl.DeviceIdType.MESH
NT = (((1,), (1,)), ((), ()))


TILES = ((0, 0), (1, 1), (2, 2), (0, 1), (0, 2), (1, 2))


def fused_kernel(
    cells,
    walls,
    mem_hbm,
    force_hbm,
    wall_hbm,
    normal_hbm,
    data_hbm,
    lag_hbm,
    order_hbm,
    out_ref,
    density_ref,
    order_ref,
    order_smem,
    force_ref,
    lag_ref,
    data_ref,
    own_block,
    own_lag,
    block_all,
    second_all,
    lag_all,
    mem_all,
    wall_all,
    data_all,
    wall_cols,
    mem_cols,
    single_all,
    single_rest,
    double_all,
    part_mine,
    part_other,
    share_out,
    share_in,
    load_sem,
    block_send,
    block_recv,
    second_send,
    second_recv,
    lag_send,
    lag_recv,
    mem_send,
    mem_recv,
    wall_send,
    wall_recv,
    data_send,
    data_recv,
    part_send,
    part_recv,
    share_send,
    share_recv,
    ready,
    ready_near,
):
    cell = lax.axis_index("cell")
    wall = lax.axis_index("wall")
    chip = lax.div(wall, 2)
    core = lax.rem(wall, 2)
    other_core = 1 - core
    other_chip = 1 - chip
    columns = order_ref.shape[1]
    halfway = columns // 2
    point_count = mem_hbm.shape[1]
    wall_count = wall_hbm.shape[1]
    own_points = force_ref.shape[2]
    shard_width = lag_ref.shape[2]
    block = 3 * wall_count
    partner = 2 * chip + other_core

    loads = [
        pltpu.make_async_copy(given, held, load_sem.at[at])
        for at, (given, held) in enumerate(
            (
                (order_hbm, order_smem),
                (order_hbm, order_ref),
                (force_hbm, force_ref),
                (lag_hbm, lag_ref),
                (mem_hbm, mem_all.at[cell]),
                (wall_hbm, wall_all.at[wall, 0]),
                (normal_hbm, wall_all.at[wall, 1]),
                (data_hbm, data_ref),
            )
        )
    ]
    for load in loads:
        load.start()

    barrier = pltpu.get_barrier_semaphore()
    for to_cell in range(cells - 1, -1, -1):
        for to_wall in range(walls):

            @pl.when((to_cell > cell) | ((to_cell == cell) & (to_wall > wall)))
            def _(to_cell=to_cell, to_wall=to_wall):
                pl.semaphore_signal(
                    barrier,
                    inc=1,
                    device_id={"cell": to_cell, "wall": to_wall},
                    device_id_type=MESH,
                )

    below = walls * cell + wall

    @pl.when(below > 0)
    def _():
        pl.semaphore_wait(barrier, below)

    for to_cell in range(cells - 1):
        for to_wall in range(walls):

            @pl.when(to_cell < cell)
            def _(to_cell=to_cell, to_wall=to_wall):
                pl.semaphore_signal(
                    ready.at[cell],
                    inc=1,
                    device_id={"cell": to_cell, "wall": to_wall},
                    device_id_type=MESH,
                )

    for to_wall in range(walls - 1):

        @pl.when(to_wall < wall)
        def _(to_wall=to_wall):
            pl.semaphore_signal(
                ready_near.at[wall], inc=1, device_id={"wall": to_wall}, device_id_type=MESH
            )

    def remote(given, held, send, recv, **to):
        return pltpu.make_async_remote_copy(
            given, held, send, recv, device_id=to, device_id_type=MESH
        )

    def block_copy(to_cell, to_chip):
        return remote(
            own_block,
            block_all.at[cell, chip],
            block_send,
            block_recv.at[cell],
            cell=to_cell,
            wall=2 * to_chip + other_core,
        )

    def lag_copy(to_cell, to_wall):
        return remote(
            own_lag, lag_all.at[cell * walls + wall], lag_send, lag_recv, cell=to_cell, wall=to_wall
        )

    def mem_copy(to_cell):
        return remote(
            mem_all.at[cell],
            mem_all.at[cell],
            mem_send,
            mem_recv.at[cell],
            cell=to_cell,
            wall=partner,
        )

    def share_copy(to_cell):
        return remote(
            share_out.at[to_cell],
            share_in.at[cell],
            share_send,
            share_recv,
            cell=to_cell,
            wall=partner,
        )

    def wall_copy(to_wall):
        held = wall_all.at[wall]
        return remote(held, held, wall_send, wall_recv.at[wall], wall=to_wall)

    def second_copy(to_wall):
        held = second_all.at[wall]
        return remote(
            held, held, second_send, second_recv, wall=to_wall
        )

    def data_copy(to_wall):
        held = data_all.at[wall]
        return remote(held, held, data_send, data_recv, wall=to_wall)

    def near_walls(body):
        for to_wall in range(walls):

            @pl.when(to_wall != wall)
            def _(to_wall=to_wall):
                body(to_wall)

    def far_cells(test, body):
        for to_cell in range(cells):

            @pl.when(test(to_cell))
            def _(to_cell=to_cell):
                body(to_cell)

    def start_blocks(to_cell):
        for to_chip in (other_chip, chip):
            block_copy(to_cell, to_chip).start()

    def start_lag(to_cell):
        for to_wall in range(walls):
            lag_copy(to_cell, to_wall).start()

    loads[4].wait()
    far_cells(lambda to_cell: to_cell < cell, lambda to_cell: mem_copy(to_cell).start())
    for load in loads[5:7]:
        load.wait()
    for to_wall in range(walls - 1):

        @pl.when(to_wall < wall)
        def _(to_wall=to_wall):
            wall_copy(to_wall).start()

    row_ids = lax.broadcasted_iota(jnp.int32, (columns, columns), 0)
    col_ids = lax.broadcasted_iota(jnp.int32, (columns, columns), 1)
    loads[0].wait()
    wanted = jnp.zeros((columns, columns), jnp.int32)
    for k in range(columns):
        wanted = jnp.where(row_ids == k, order_smem[0, k], wanted)
    gather_f32 = (wanted == col_ids).astype(jnp.float32)
    gather = gather_f32.astype(jnp.bfloat16)

    loads[2].wait()
    rows = [jnp.dot(gather, force_ref[j], preferred_element_type=jnp.float32) for j in range(3)]
    folded = halfway // 2
    part = [row[:halfway] for row in rows]
    pair = jnp.concatenate([part[0], part[1]], axis=1)
    last = jnp.concatenate([part[2][:folded], part[2][folded:]], axis=1)
    own_block[...] = jnp.concatenate([pair, last], axis=0).astype(jnp.bfloat16)

    part = [row[halfway:] for row in rows]
    unused = jnp.zeros((halfway, LANES - own_points), jnp.float32)
    second_all[wall, 0] = jnp.concatenate([part[0], part[1]], axis=1).astype(jnp.bfloat16)
    second_all[wall, 1] = jnp.concatenate([part[2], unused], axis=1).astype(jnp.bfloat16)

    for to_wall in range(walls - 1):

        @pl.when(to_wall < wall)
        def _(to_wall=to_wall):
            second_copy(to_wall).start()

    far_cells(lambda to_cell: to_cell < cell, start_blocks)

    loads[3].wait()
    pieces = [lag_ref[j].astype(jnp.float32) for j in range(3)]
    if LANES > 3 * shard_width:
        pieces.append(jnp.zeros((halfway, LANES - 3 * shard_width), jnp.float32))
    packed_lag = jnp.concatenate(pieces, axis=1).astype(jnp.bfloat16)
    own_lag[...] = packed_lag
    lag_all[cell * walls + wall] = packed_lag

    far_cells(lambda to_cell: to_cell < cell, start_lag)

    for to_wall in range(1, walls):

        @pl.when(to_wall > wall)
        def _(to_wall=to_wall):
            pl.semaphore_wait(ready_near.at[to_wall], 1)
            wall_copy(to_wall).start()

    def start_near(to_wall):
        @pl.when(to_wall > wall)
        def _():
            second_copy(to_wall).start()

        @pl.when(to_wall % 2 != core)
        def _():
            block_copy(cell, to_wall // 2).start()

    def start_near_lag(to_wall):
        lag_copy(cell, to_wall).start()

    near_walls(start_near)
    near_walls(start_near_lag)

    loads[7].wait()
    data_rows = [
        jnp.dot(gather_f32, data_ref[j], precision=lax.Precision.HIGHEST) for j in range(3)
    ]
    for j in range(3):
        data_all[wall, j] = data_rows[j][:halfway]
    near_walls(lambda to_wall: data_copy(to_wall).start())

    loads[1].wait()
    scatter = (row_ids == order_ref[...]).astype(jnp.float32).astype(jnp.bfloat16)

    def spread_wall(source):
        for j in range(3):
            wall_cols[source, j] = jnp.broadcast_to(
                wall_all[source, 0, j : j + 1, :], (LANES, wall_count)
            ).T

    for j in range(3):
        mem_cols[j] = jnp.broadcast_to(mem_all[cell, j : j + 1, :], (LANES, point_count)).T

    lane_ids = lax.broadcasted_iota(jnp.int32, (8, LANES), 1)

    def mem_rows(source, parity):
        rows = []
        for j in range(3):
            low = jnp.broadcast_to(mem_all[source, j : j + 1, :LANES], (8, LANES))
            high = jnp.broadcast_to(mem_all[source, j : j + 1, LANES:], (8, LANES))
            low = pltpu.roll(low, own_points * parity, 1)
            high = pltpu.roll(high, own_points * (1 - parity), 1)
            rows.append(jnp.where(lane_ids < own_points, low, high)[0:1])
        return rows

    def fill_single(tile, rows, at):
        apart = [wall_cols[at, j] - rows[j] for j in range(3)]
        square = apart[0] * apart[0] + apart[1] * apart[1] + apart[2] * apart[2]
        inverse = lax.rsqrt(square)
        scaled = stokes_coef * inverse
        cube = scaled * (inverse * inverse)
        for j in range(3):
            along = apart[j] * cube
            for i in range(j + 1):
                element = along * apart[i]
                if i == j:
                    element = element + scaled
                at_tile = TILES.index((i, j))
                tile[:, at_tile * LANES : (at_tile + 1) * LANES] = element.astype(jnp.bfloat16)

    def fill_double(source):
        own = pl.ds(pl.multiple_of(wall * own_points, own_points), own_points)
        apart = [mem_cols[j, own, :] - wall_all[source, 0, j : j + 1, :] for j in range(3)]
        square = apart[0] * apart[0] + apart[1] * apart[1] + apart[2] * apart[2]
        inverse = lax.rsqrt(square)
        flux = (
            apart[0] * wall_all[source, 1, 0:1, :]
            + apart[1] * wall_all[source, 1, 1:2, :]
            + apart[2] * wall_all[source, 1, 2:3, :]
        )
        inverse_square = inverse * inverse
        fifth = inverse_square * inverse_square * inverse
        weight = (-6.0 * stokes_coef) * flux * fifth
        for j in range(3):
            along = apart[j] * weight
            for i in range(j + 1):
                element = (along * apart[i]).astype(jnp.bfloat16)
                for a, b in {(i, j), (j, i)}:
                    lanes = pl.multiple_of(source * block + b * wall_count, wall_count)
                    double_all[
                        a * own_points : (a + 1) * own_points, pl.ds(lanes, wall_count)
                    ] = element

    own_rows = mem_rows(cell, other_core)
    spread_wall(wall)
    fill_single(single_all.at[0, wall], own_rows, wall)
    fill_double(wall)

    def wait_into(held, recv):
        remote(held, held, load_sem.at[0], recv, wall=partner).wait_recv()

    def wait_out(held, send):
        remote(held, held, send, load_sem.at[0], wall=partner).wait_send()

    peers = (partner, 2 * other_chip + other_core, 2 * other_chip + core)

    def take_wall(peer):
        wait_into(wall_all.at[peer], wall_recv.at[peer])
        spread_wall(peer)
        fill_single(single_all.at[0, peer], own_rows, peer)
        fill_double(peer)

    def start_above(up):
        def body(to_cell):
            pl.semaphore_wait(ready.at[to_cell], walls)
            mem_copy(to_cell).start()
            start_blocks(to_cell)

        far_cells(lambda to_cell: to_cell == cell + up, body)

    low_lanes = lax.broadcasted_iota(jnp.int32, (halfway, LANES), 1) < own_points

    def low_halves(first, second):
        mask = low_lanes[: first.shape[0]]
        return jnp.where(mask, first, pltpu.roll(second, own_points, 1))

    def high_halves(first, second):
        mask = low_lanes[: first.shape[0]]
        return jnp.where(mask, pltpu.roll(first, own_points, 1), second)

    def stack_rows(parts):
        empty = jnp.zeros((halfway, LANES), jnp.bfloat16)
        groups = []
        for i in range(3):
            row = [empty] * len(TILES)
            for at_tile, (a, b) in enumerate(TILES):
                if i in (a, b):
                    row[at_tile] = parts[a + b - i].astype(jnp.bfloat16)
            groups.append(jnp.concatenate(row, axis=1))
        return jnp.concatenate(groups, axis=0)

    def second_columns(tiles):
        pair = [tile[0].astype(jnp.float32) for tile in tiles]
        last = [tile[1].astype(jnp.float32) for tile in tiles]
        return stack_rows([low_halves(*pair), high_halves(*pair), low_halves(*last)])

    def columns_of(tiles):
        tiles = [tile.astype(jnp.float32) for tile in tiles]
        pair = [tile[:halfway] for tile in tiles]
        last = [tile[halfway:] for tile in tiles]
        last = jnp.concatenate([low_halves(*last), high_halves(*last)], axis=0)
        return stack_rows([low_halves(*pair), high_halves(*pair), last])

    take_wall(partner)
    fill_single(single_rest, mem_rows(cell, core), partner)
    start_above(1)
    for up in range(2, cells - 1):
        start_above(up)
    far_cells(lambda to_cell: (to_cell > cell) & (to_cell < cells - 1), start_lag)

    wait_into(second_all.at[: walls - 1], second_recv)
    share = jnp.zeros((3 * halfway, wall_count), jnp.float32)
    for parity, tile in ((other_core, single_all.at[0, partner]), (core, single_rest)):
        share = share + lax.dot_general(
            second_columns([second_all[2 * at + parity] for at in range(2)]),
            tile[...],
            NT,
            preferred_element_type=jnp.float32,
        )
    for to_cell in range(cells):
        pieces = [
            share[
                i * halfway : (i + 1) * halfway,
                to_cell * shard_width : (to_cell + 1) * shard_width,
            ]
            for i in range(3)
        ]
        if LANES > 3 * shard_width:
            pieces.append(jnp.zeros((halfway, LANES - 3 * shard_width), jnp.float32))
        share_out[to_cell] = jnp.concatenate(pieces, axis=1)
    far_cells(lambda to_cell: to_cell <= cell, lambda to_cell: share_copy(to_cell).start())
    take_wall(peers[1])
    if cells > 2:
        start_above(cells - 1)
    far_cells(lambda to_cell: to_cell > cell, lambda to_cell: share_copy(to_cell).start())
    far_cells(lambda to_cell: (to_cell > cell) & (to_cell == cells - 1), start_lag)
    take_wall(peers[2])

    def source_at(step):
        if step == 0:
            return cell
        return jnp.where(cell + step < cells, cell + step, cells - 1 - step)

    def wait_mem(step):
        source = source_at(step)
        wait_into(mem_all.at[source], mem_recv.at[source])

    def take_mem(step):
        rows = mem_rows(source_at(step), other_core)
        for at in range(walls):
            fill_single(single_all.at[step, at], rows, at)

    def first_columns(step):
        source = source_at(step)
        wait_into(block_all.at[source], block_recv.at[source])
        return columns_of([block_all[source, at] for at in range(2)])

    def exchange(half):
        return remote(
            part_mine.at[half],
            part_other.at[half],
            part_send.at[half],
            part_recv.at[half],
            wall=partner,
        )

    width = walls // 2 * wall_count
    partial = [jnp.zeros((3 * halfway, width), jnp.float32) for _ in range(2)]
    for step in range(cells):
        if step + 1 < cells:
            wait_mem(step + 1)
        left = first_columns(step)
        if step + 1 < cells:
            take_mem(step + 1)
        if step < cells - 1:
            whole = lax.dot_general(
                left,
                single_all[step].reshape(2 * width, len(TILES) * LANES),
                NT,
                preferred_element_type=jnp.float32,
            )
            for half in range(2):
                partial[half] = partial[half] + whole[:, half * width : (half + 1) * width]
            continue
        for half in range(2):
            tile = single_all[step, half * (walls // 2) : (half + 1) * (walls // 2)]
            partial[half] = partial[half] + lax.dot_general(
                left,
                tile.reshape(width, len(TILES) * LANES),
                NT,
                preferred_element_type=jnp.float32,
            )
            if step == cells - 1:
                part_mine[half] = partial[half]
                exchange(half).start()

    wait_out(mem_all.at[: cells - 1], mem_send)
    wait_out(block_all, block_send)
    wait_out(lag_all.at[: cells * walls - 1], lag_send)
    wait_out(wall_all.at[: walls - 1], wall_send)
    wait_out(second_all.at[: walls - 1], second_send)
    wait_into(data_all.at[: walls - 1], data_recv)
    wait_out(data_all.at[: walls - 1], data_send)
    wait_out(share_in, share_send)

    wait_into(lag_all.at[: cells * walls - 1], lag_recv)

    def layer(rows):
        return lax.dot_general(rows, double_all[...], NT, preferred_element_type=jnp.float32)

    lag_row = []
    for source in range(walls):
        lag_row += [
            lag_all[k * walls + source, :, j * shard_width : (j + 1) * shard_width]
            for j in range(3)
            for k in range(cells)
        ]

    moves = [
        jnp.concatenate([scatter[:, :halfway]] * 3, axis=1),
        jnp.concatenate([scatter[:, halfway:]] * 3, axis=1),
    ]

    def move_rows(move, rows):
        held = []
        for _ in range(3):
            piece = rows.astype(jnp.bfloat16)
            held.append(piece)
            rows = rows - piece.astype(jnp.float32)
        return jnp.dot(move, jnp.concatenate(held, axis=0), preferred_element_type=jnp.float32)

    total = move_rows(moves[0], layer(jnp.concatenate(lag_row, axis=1)))

    for half in range(2):
        exchange(half).wait_recv()
    pieces = []
    for source in range(walls):
        for i in range(3):
            half, at = divmod(source, walls // 2)
            held = slice(i * halfway, (i + 1) * halfway)
            lanes = slice(at * wall_count, (at + 1) * wall_count)
            velocity = part_mine[half, held, lanes] + part_other[half, held, lanes]
            dense = 2.0 * (data_all[source, i] - velocity)
            pieces.append(dense.astype(jnp.bfloat16))
    total = total + move_rows(moves[1], layer(jnp.concatenate(pieces, axis=1)))
    for i in range(3):
        out_ref[i] = total[:, i * own_points : (i + 1) * own_points]

    wait_into(share_in, share_recv)
    second_sum = jnp.zeros((halfway, LANES), jnp.float32)
    for source in range(cells):
        second_sum = second_sum + share_in[source]
    shift = lax.rem((cells - cell) * shard_width, wall_count)
    for i in range(3):
        held = pltpu.roll(data_rows[i][halfway:], shift, 1)[:, :shard_width]
        density_ref[i] = 2.0 * (held - second_sum[:, i * shard_width : (i + 1) * shard_width])

    for half in range(2):
        exchange(half).wait_send()


def write_kernel(velocity_ref, density_ref, velocity_hbm, density_hbm, sem):
    first = pltpu.make_async_copy(velocity_ref, velocity_hbm, sem.at[0])
    second = pltpu.make_async_copy(density_ref, density_hbm, sem.at[1])
    first.start()
    second.start()
    first.wait()
    second.wait()


def fused_shards(cells, walls, mem_pos, forces, wall_pos, wall_normal, wall_data, lag_density, batch_order):
    columns = forces.shape[0]
    halfway = columns // 2
    point_count = mem_pos.shape[1]
    wall_count = wall_pos.shape[1]
    own_points = forces.shape[2]
    shard_width = lag_density.shape[2]
    dma = pltpu.SemaphoreType.DMA
    vmem = pl.BlockSpec(memory_space=pltpu.VMEM)
    hbm = pl.BlockSpec(memory_space=pltpu.HBM)
    velocity, density = pl.pallas_call(
        functools.partial(fused_kernel, cells, walls),
        out_shape=(
            pltpu.VMEM((3, columns, own_points), jnp.float32),
            pltpu.VMEM((3, halfway, shard_width), jnp.float32),
        ),
        in_specs=[hbm] * 7,
        out_specs=(vmem, vmem),
        scratch_shapes=[
            pltpu.VMEM((1, columns), jnp.int32),
            pltpu.SMEM((1, columns), jnp.int32),
            pltpu.VMEM((3, columns, own_points), jnp.bfloat16),
            pltpu.VMEM((3, halfway, shard_width), jnp.bfloat16),
            pltpu.VMEM((3, columns, wall_count), jnp.float32),
            pltpu.VMEM((3 * halfway // 2, LANES), jnp.bfloat16),
            pltpu.VMEM((halfway, LANES), jnp.bfloat16),
            pltpu.VMEM((cells, 2, 3 * halfway // 2, LANES), jnp.bfloat16),
            pltpu.VMEM((walls, 2, halfway, LANES), jnp.bfloat16),
            pltpu.VMEM((cells * walls, halfway, LANES), jnp.bfloat16),
            pltpu.VMEM((cells, 3, point_count), jnp.float32),
            pltpu.VMEM((walls, 2, 3, wall_count), jnp.float32),
            pltpu.VMEM((walls, 3, halfway, wall_count), jnp.float32),
            pltpu.VMEM((walls, 3, wall_count, LANES), jnp.float32),
            pltpu.VMEM((3, point_count, LANES), jnp.float32),
            pltpu.VMEM((cells, walls, wall_count, len(TILES) * LANES), jnp.bfloat16),
            pltpu.VMEM((wall_count, len(TILES) * LANES), jnp.bfloat16),
            pltpu.VMEM((3 * own_points, walls * 3 * wall_count), jnp.bfloat16),
            pltpu.VMEM((2, 3 * halfway, walls // 2 * wall_count), jnp.float32),
            pltpu.VMEM((2, 3 * halfway, walls // 2 * wall_count), jnp.float32),
            pltpu.VMEM((cells, halfway, LANES), jnp.float32),
            pltpu.VMEM((cells, halfway, LANES), jnp.float32),
            dma((8,)),
            dma,
            dma((cells,)),
            dma,
            dma,
            dma,
            dma,
            dma,
            dma((cells,)),
            dma,
            dma((walls,)),
            dma,
            dma,
            dma((2,)),
            dma((2,)),
            dma,
            dma,
            pltpu.SemaphoreType.REGULAR((cells,)),
            pltpu.SemaphoreType.REGULAR((walls,)),
        ],
        compiler_params=pltpu.CompilerParams(
            collective_id=0, has_side_effects=True, vmem_limit_bytes=VMEM_GRANT
        ),
        name="coupling",
    )(
        mem_pos,
        jnp.transpose(forces, (1, 0, 2)),
        wall_pos,
        wall_normal,
        jnp.transpose(wall_data, (1, 0, 2)),
        jnp.transpose(lag_density, (1, 0, 2)),
        batch_order.reshape(1, columns),
    )
    velocity, density = pl.pallas_call(
        write_kernel,
        out_shape=(
            jax.ShapeDtypeStruct(velocity.shape, velocity.dtype),
            jax.ShapeDtypeStruct(density.shape, density.dtype),
        ),
        in_specs=[vmem] * 2,
        out_specs=(hbm, hbm),
        scratch_shapes=[dma((2,))],
        compiler_params=pltpu.CompilerParams(vmem_limit_bytes=1024 * 1024),
        name="write",
    )(velocity, density)
    return (jnp.transpose(velocity, (1, 0, 2)), jnp.transpose(density, (1, 0, 2)))


VMEM_GRANT = 60 * 1024 * 1024


def step(cells, walls, mem_pos, forces, wall_pos, *rest):
    point_count = mem_pos.shape[1]
    wall_count = wall_pos.shape[1]
    own_points = forces.shape[2]
    shard_width = rest[2].shape[2]
    tiles = 18 * walls * wall_count * (cells * LANES + own_points)
    fits = tiles <= VMEM_GRANT // 2
    aligned = (
        walls == 4
        and wall_count == LANES
        and 2 * own_points == LANES
        and point_count == walls * own_points
        and wall_count == cells * shard_width
        and 3 * shard_width <= LANES
    )
    if fits and aligned:
        return fused_shards(cells, walls, mem_pos, forces, wall_pos, *rest)
    return shards(mem_pos, forces, wall_pos, *rest)


def solution(mesh):
    placed = (
        P(None, ("groups", "cell")),
        P(None, None, ("groups", "cell", "wall")),
        P(None, ("groups", "wall")),
        P(None, ("groups", "wall")),
        P(None, None, ("groups", "wall")),
        P(None, None, ("groups", "wall", "cell")),
        P(),
    )
    return jax.shard_map(
        functools.partial(step, mesh.shape["cell"], mesh.shape["wall"]),
        mesh=mesh,
        in_specs=placed,
        out_specs=(
            P(None, None, ("groups", "cell", "wall")),
            P(None, None, ("groups", "wall", "cell")),
        ),
        check_vma=False,
    )
```

```python
import functools
import math

import jax
import jax.numpy as jnp
from jax import lax
from jax.experimental import pallas as pl
from jax.experimental.pallas import tpu as pltpu
from jax.sharding import PartitionSpec as P

stokes_coef = 1.0 / (8.0 * math.pi)


def single_tile(targets, sources):
    separation = targets[:, None, :] - sources[:, :, None]
    inverse = lax.rsqrt(jnp.sum(separation * separation, axis=0))
    inverse_cube = inverse * inverse * inverse
    stacked = []
    for second_dim in range(3):
        entries_row = []
        for first_dim in range(3):
            element = separation[first_dim] * separation[second_dim] * inverse_cube
            if first_dim == second_dim:
                element = element + inverse
            entries_row.append(element * stokes_coef)
        stacked.append(jnp.stack(entries_row, axis=1))
    kernel_tile = jnp.stack(stacked, axis=0)
    return kernel_tile.reshape(3 * sources.shape[1], 3 * targets.shape[1]).astype(jnp.bfloat16)


def double_tile(targets, sources, normals):
    separation = targets[:, None, :] - sources[:, :, None]
    inverse = lax.rsqrt(jnp.sum(separation * separation, axis=0))
    normal_flux = jnp.sum(separation * normals[:, :, None], axis=0)
    weight = -6.0 * stokes_coef * normal_flux * inverse**5
    stacked = []
    for second_dim in range(3):
        entries_row = []
        for first_dim in range(3):
            entries_row.append(weight * separation[first_dim] * separation[second_dim])
        stacked.append(jnp.stack(entries_row, axis=1))
    kernel_tile = jnp.stack(stacked, axis=0)
    return kernel_tile.reshape(3 * sources.shape[1], 3 * targets.shape[1]).astype(jnp.bfloat16)


def shards(mem_pos, forces, wall_pos, wall_normal, wall_data, lag_density, batch_order):
    columns = forces.shape[0]
    halfway = columns // 2
    point_count = mem_pos.shape[1]
    wall_count = wall_pos.shape[1]
    shard_width = lag_density.shape[2]
    piece_len = math.gcd(point_count, 128)
    block_count = point_count // piece_len
    first_rows = batch_order[:halfway]
    second_rows = batch_order[halfway:]
    force_block = lax.all_gather(forces, "wall", axis=2, tiled=True)
    lag_block = lax.all_gather(lag_density, "cell", axis=2, tiled=True)
    lag_flat = lag_block.reshape(halfway, 3 * wall_count)

    def position_at(block_index):
        return lax.dynamic_slice_in_dim(mem_pos, block_index * piece_len, piece_len, 1)

    def single_term(block_index):
        loaded = lax.dynamic_slice_in_dim(force_block, block_index * piece_len, piece_len, 2)
        loaded = loaded.reshape(columns, 3 * piece_len)
        return jnp.dot(
            loaded,
            single_tile(wall_pos, position_at(block_index)),
            preferred_element_type=jnp.float32,
        )

    def double_term(dense_rows, block_index):
        kernel_tile = double_tile(position_at(block_index), wall_pos, wall_normal)
        product = jnp.dot(dense_rows, kernel_tile, preferred_element_type=jnp.float32)
        return product.reshape(dense_rows.shape[0], 3, piece_len)

    def place_block(target, piece, block_index):
        return lax.dynamic_update_slice_in_dim(target, piece, block_index * piece_len, 2)

    empty_wall = jnp.zeros((columns, 3 * wall_count), jnp.float32)

    def add_single(block_index, running):
        return running + single_term(block_index)

    running = lax.fori_loop(0, block_count, add_single, empty_wall)
    wall_term = running.reshape(columns, 3, wall_count)
    position_cell = lax.axis_index("cell")
    first_sum = lax.psum(jnp.take(wall_term, first_rows, axis=0), "cell")
    first_block = (2.0 * (jnp.take(wall_data, first_rows, axis=0) - first_sum)).astype(jnp.bfloat16)
    second_sum = lax.psum_scatter(
        jnp.take(wall_term, second_rows, axis=0).astype(jnp.bfloat16),
        "cell",
        scatter_dimension=2,
        tiled=True,
    ).astype(jnp.float32)
    second_data = lax.dynamic_slice_in_dim(
        jnp.take(wall_data, second_rows, axis=0), position_cell * shard_width, shard_width, 2
    )
    wall_density = 2.0 * (second_data - second_sum)
    first_flat = first_block.reshape(halfway, 3 * wall_count)
    carried = jnp.concatenate([lag_flat, first_flat], axis=0)

    def all_terms(block_index, target):
        return place_block(target, double_term(carried, block_index), block_index)

    membrane_term = lax.fori_loop(
        0, block_count, all_terms, jnp.zeros((columns, 3, point_count), jnp.float32)
    )
    batched = lax.psum_scatter(membrane_term, "wall", scatter_dimension=2, tiled=True)
    membrane_velocity = jnp.zeros_like(batched).at[batch_order].set(batched)
    return (membrane_velocity, wall_density)

LANES = 128
MESH = pl.DeviceIdType.MESH
NT = (((1,), (1,)), ((), ()))


TILES = ((0, 0), (1, 1), (2, 2), (0, 1), (0, 2), (1, 2))


def fused_kernel(
    cells,
    walls,
    mem_hbm,
    force_hbm,
    wall_hbm,
    normal_hbm,
    data_hbm,
    lag_hbm,
    order_hbm,
    out_ref,
    density_ref,
    order_ref,
    order_smem,
    force_ref,
    lag_ref,
    data_ref,
    own_block,
    own_lag,
    block_all,
    second_all,
    lag_all,
    mem_all,
    wall_all,
    data_all,
    wall_cols,
    mem_cols,
    single_all,
    single_rest,
    double_all,
    part_mine,
    part_other,
    share_out,
    share_in,
    load_sem,
    block_send,
    block_recv,
    second_send,
    second_recv,
    lag_send,
    lag_recv,
    mem_send,
    mem_recv,
    wall_send,
    wall_recv,
    data_send,
    data_recv,
    part_send,
    part_recv,
    share_send,
    share_recv,
    ready,
    ready_near,
):
    cell = lax.axis_index("cell")
    wall = lax.axis_index("wall")
    chip = lax.div(wall, 2)
    core = lax.rem(wall, 2)
    other_core = 1 - core
    other_chip = 1 - chip
    columns = order_ref.shape[1]
    halfway = columns // 2
    point_count = mem_hbm.shape[1]
    wall_count = wall_hbm.shape[1]
    own_points = force_ref.shape[2]
    shard_width = lag_ref.shape[2]
    block = 3 * wall_count
    partner = 2 * chip + other_core

    loads = [
        pltpu.make_async_copy(given, held, load_sem.at[at])
        for at, (given, held) in enumerate(
            (
                (order_hbm, order_smem),
                (order_hbm, order_ref),
                (force_hbm, force_ref),
                (lag_hbm, lag_ref),
                (mem_hbm, mem_all.at[cell]),
                (wall_hbm, wall_all.at[wall, 0]),
                (normal_hbm, wall_all.at[wall, 1]),
                (data_hbm, data_ref),
            )
        )
    ]
    for load in loads:
        load.start()

    barrier = pltpu.get_barrier_semaphore()
    for to_cell in range(cells - 1, -1, -1):
        for to_wall in range(walls):

            @pl.when((to_cell > cell) | ((to_cell == cell) & (to_wall > wall)))
            def _(to_cell=to_cell, to_wall=to_wall):
                pl.semaphore_signal(
                    barrier,
                    inc=1,
                    device_id={"cell": to_cell, "wall": to_wall},
                    device_id_type=MESH,
                )

    below = walls * cell + wall

    @pl.when(below > 0)
    def _():
        pl.semaphore_wait(barrier, below)

    for to_cell in range(cells - 1):
        for to_wall in range(walls):

            @pl.when(to_cell < cell)
            def _(to_cell=to_cell, to_wall=to_wall):
                pl.semaphore_signal(
                    ready.at[cell],
                    inc=1,
                    device_id={"cell": to_cell, "wall": to_wall},
                    device_id_type=MESH,
                )

    for to_wall in range(walls - 1):

        @pl.when(to_wall < wall)
        def _(to_wall=to_wall):
            pl.semaphore_signal(
                ready_near.at[wall], inc=1, device_id={"wall": to_wall}, device_id_type=MESH
            )

    def remote(given, held, send, recv, **to):
        return pltpu.make_async_remote_copy(
            given, held, send, recv, device_id=to, device_id_type=MESH
        )

    def block_copy(to_cell, to_chip):
        return remote(
            own_block,
            block_all.at[cell, chip],
            block_send,
            block_recv.at[cell],
            cell=to_cell,
            wall=2 * to_chip + other_core,
        )

    def lag_copy(to_cell, to_wall):
        return remote(
            own_lag, lag_all.at[cell * walls + wall], lag_send, lag_recv, cell=to_cell, wall=to_wall
        )

    def mem_copy(to_cell):
        return remote(
            mem_all.at[cell],
            mem_all.at[cell],
            mem_send,
            mem_recv.at[cell],
            cell=to_cell,
            wall=partner,
        )

    def share_copy(to_cell):
        return remote(
            share_out.at[to_cell],
            share_in.at[cell],
            share_send,
            share_recv,
            cell=to_cell,
            wall=partner,
        )

    def wall_copy(to_wall):
        held = wall_all.at[wall]
        return remote(held, held, wall_send, wall_recv.at[wall], wall=to_wall)

    def second_copy(to_wall):
        held = second_all.at[wall]
        return remote(
            held, held, second_send, second_recv, wall=to_wall
        )

    def data_copy(to_wall):
        held = data_all.at[wall]
        return remote(held, held, data_send, data_recv, wall=to_wall)

    def near_walls(body):
        for to_wall in range(walls):

            @pl.when(to_wall != wall)
            def _(to_wall=to_wall):
                body(to_wall)

    def far_cells(test, body):
        for to_cell in range(cells):

            @pl.when(test(to_cell))
            def _(to_cell=to_cell):
                body(to_cell)

    def start_blocks(to_cell):
        for to_chip in (other_chip, chip):
            block_copy(to_cell, to_chip).start()

    def start_lag(to_cell):
        for to_wall in range(walls):
            lag_copy(to_cell, to_wall).start()

    loads[4].wait()
    far_cells(lambda to_cell: to_cell < cell, lambda to_cell: mem_copy(to_cell).start())
    for load in loads[5:7]:
        load.wait()
    for to_wall in range(walls - 1):

        @pl.when(to_wall < wall)
        def _(to_wall=to_wall):
            wall_copy(to_wall).start()

    row_ids = lax.broadcasted_iota(jnp.int32, (columns, columns), 0)
    col_ids = lax.broadcasted_iota(jnp.int32, (columns, columns), 1)
    loads[0].wait()
    wanted = jnp.zeros((columns, columns), jnp.int32)
    for k in range(columns):
        wanted = jnp.where(row_ids == k, order_smem[0, k], wanted)
    gather_f32 = (wanted == col_ids).astype(jnp.float32)
    gather = gather_f32.astype(jnp.bfloat16)

    loads[2].wait()
    rows = [jnp.dot(gather, force_ref[j], preferred_element_type=jnp.float32) for j in range(3)]
    folded = halfway // 2
    part = [row[:halfway] for row in rows]
    pair = jnp.concatenate([part[0], part[1]], axis=1)
    last = jnp.concatenate([part[2][:folded], part[2][folded:]], axis=1)
    own_block[...] = jnp.concatenate([pair, last], axis=0).astype(jnp.bfloat16)

    part = [row[halfway:] for row in rows]
    unused = jnp.zeros((halfway, LANES - own_points), jnp.float32)
    second_all[wall, 0] = jnp.concatenate([part[0], part[1]], axis=1).astype(jnp.bfloat16)
    second_all[wall, 1] = jnp.concatenate([part[2], unused], axis=1).astype(jnp.bfloat16)

    for to_wall in range(walls - 1):

        @pl.when(to_wall < wall)
        def _(to_wall=to_wall):
            second_copy(to_wall).start()

    far_cells(lambda to_cell: to_cell < cell, start_blocks)

    loads[3].wait()
    pieces = [lag_ref[j].astype(jnp.float32) for j in range(3)]
    if LANES > 3 * shard_width:
        pieces.append(jnp.zeros((halfway, LANES - 3 * shard_width), jnp.float32))
    packed_lag = jnp.concatenate(pieces, axis=1).astype(jnp.bfloat16)
    own_lag[...] = packed_lag
    lag_all[cell * walls + wall] = packed_lag

    far_cells(lambda to_cell: to_cell < cell, start_lag)

    for to_wall in range(1, walls):

        @pl.when(to_wall > wall)
        def _(to_wall=to_wall):
            pl.semaphore_wait(ready_near.at[to_wall], 1)
            wall_copy(to_wall).start()

    def start_near(to_wall):
        @pl.when(to_wall > wall)
        def _():
            second_copy(to_wall).start()

        @pl.when(to_wall % 2 != core)
        def _():
            block_copy(cell, to_wall // 2).start()

    def start_near_lag(to_wall):
        lag_copy(cell, to_wall).start()

    near_walls(start_near)
    near_walls(start_near_lag)

    loads[7].wait()
    data_rows = [
        jnp.dot(gather_f32, data_ref[j], precision=lax.Precision.HIGHEST) for j in range(3)
    ]
    for j in range(3):
        data_all[wall, j] = data_rows[j][:halfway]
    near_walls(lambda to_wall: data_copy(to_wall).start())

    loads[1].wait()
    scatter = (row_ids == order_ref[...]).astype(jnp.float32).astype(jnp.bfloat16)

    def spread_wall(source):
        for j in range(3):
            wall_cols[source, j] = jnp.broadcast_to(
                wall_all[source, 0, j : j + 1, :], (LANES, wall_count)
            ).T

    for j in range(3):
        mem_cols[j] = jnp.broadcast_to(mem_all[cell, j : j + 1, :], (LANES, point_count)).T

    lane_ids = lax.broadcasted_iota(jnp.int32, (8, LANES), 1)

    def mem_rows(source, parity):
        rows = []
        for j in range(3):
            low = jnp.broadcast_to(mem_all[source, j : j + 1, :LANES], (8, LANES))
            high = jnp.broadcast_to(mem_all[source, j : j + 1, LANES:], (8, LANES))
            low = pltpu.roll(low, own_points * parity, 1)
            high = pltpu.roll(high, own_points * (1 - parity), 1)
            rows.append(jnp.where(lane_ids < own_points, low, high)[0:1])
        return rows

    def fill_single(tile, rows, at):
        apart = [wall_cols[at, j] - rows[j] for j in range(3)]
        square = apart[0] * apart[0] + apart[1] * apart[1] + apart[2] * apart[2]
        inverse = lax.rsqrt(square)
        scaled = stokes_coef * inverse
        cube = scaled * (inverse * inverse)
        for j in range(3):
            along = apart[j] * cube
            for i in range(j + 1):
                element = along * apart[i]
                if i == j:
                    element = element + scaled
                at_tile = TILES.index((i, j))
                tile[:, at_tile * LANES : (at_tile + 1) * LANES] = element.astype(jnp.bfloat16)

    def fill_double(source):
        own = pl.ds(pl.multiple_of(wall * own_points, own_points), own_points)
        apart = [mem_cols[j, own, :] - wall_all[source, 0, j : j + 1, :] for j in range(3)]
        square = apart[0] * apart[0] + apart[1] * apart[1] + apart[2] * apart[2]
        inverse = lax.rsqrt(square)
        flux = (
            apart[0] * wall_all[source, 1, 0:1, :]
            + apart[1] * wall_all[source, 1, 1:2, :]
            + apart[2] * wall_all[source, 1, 2:3, :]
        )
        inverse_square = inverse * inverse
        fifth = inverse_square * inverse_square * inverse
        weight = (-6.0 * stokes_coef) * flux * fifth
        for j in range(3):
            along = apart[j] * weight
            for i in range(j + 1):
                element = (along * apart[i]).astype(jnp.bfloat16)
                for a, b in {(i, j), (j, i)}:
                    lanes = pl.multiple_of(source * block + b * wall_count, wall_count)
                    double_all[
                        a * own_points : (a + 1) * own_points, pl.ds(lanes, wall_count)
                    ] = element

    own_rows = mem_rows(cell, other_core)
    spread_wall(wall)
    fill_single(single_all.at[0, wall], own_rows, wall)
    fill_double(wall)

    def wait_into(held, recv):
        remote(held, held, load_sem.at[0], recv, wall=partner).wait_recv()

    def wait_out(held, send):
        remote(held, held, send, load_sem.at[0], wall=partner).wait_send()

    peers = (partner, 2 * other_chip + other_core, 2 * other_chip + core)

    def take_wall(peer):
        wait_into(wall_all.at[peer], wall_recv.at[peer])
        spread_wall(peer)
        fill_single(single_all.at[0, peer], own_rows, peer)
        fill_double(peer)

    def start_above(up):
        def body(to_cell):
            pl.semaphore_wait(ready.at[to_cell], walls)
            mem_copy(to_cell).start()
            start_blocks(to_cell)

        far_cells(lambda to_cell: to_cell == cell + up, body)

    low_lanes = lax.broadcasted_iota(jnp.int32, (halfway, LANES), 1) < own_points

    def low_halves(first, second):
        mask = low_lanes[: first.shape[0]]
        return jnp.where(mask, first, pltpu.roll(second, own_points, 1))

    def high_halves(first, second):
        mask = low_lanes[: first.shape[0]]
        return jnp.where(mask, pltpu.roll(first, own_points, 1), second)

    def stack_rows(parts):
        empty = jnp.zeros((halfway, LANES), jnp.bfloat16)
        groups = []
        for i in range(3):
            row = [empty] * len(TILES)
            for at_tile, (a, b) in enumerate(TILES):
                if i in (a, b):
                    row[at_tile] = parts[a + b - i].astype(jnp.bfloat16)
            groups.append(jnp.concatenate(row, axis=1))
        return jnp.concatenate(groups, axis=0)

    def second_columns(tiles):
        pair = [tile[0].astype(jnp.float32) for tile in tiles]
        last = [tile[1].astype(jnp.float32) for tile in tiles]
        return stack_rows([low_halves(*pair), high_halves(*pair), low_halves(*last)])

    def columns_of(tiles):
        tiles = [tile.astype(jnp.float32) for tile in tiles]
        pair = [tile[:halfway] for tile in tiles]
        last = [tile[halfway:] for tile in tiles]
        last = jnp.concatenate([low_halves(*last), high_halves(*last)], axis=0)
        return stack_rows([low_halves(*pair), high_halves(*pair), last])

    take_wall(partner)
    fill_single(single_rest, mem_rows(cell, core), partner)
    start_above(1)
    for up in range(2, cells - 1):
        start_above(up)
    far_cells(lambda to_cell: (to_cell > cell) & (to_cell < cells - 1), start_lag)

    wait_into(second_all.at[: walls - 1], second_recv)
    share = jnp.zeros((3 * halfway, wall_count), jnp.float32)
    for parity, tile in ((other_core, single_all.at[0, partner]), (core, single_rest)):
        share = share + lax.dot_general(
            second_columns([second_all[2 * at + parity] for at in range(2)]),
            tile[...],
            NT,
            preferred_element_type=jnp.float32,
        )
    for to_cell in range(cells):
        pieces = [
            share[
                i * halfway : (i + 1) * halfway,
                to_cell * shard_width : (to_cell + 1) * shard_width,
            ]
            for i in range(3)
        ]
        if LANES > 3 * shard_width:
            pieces.append(jnp.zeros((halfway, LANES - 3 * shard_width), jnp.float32))
        share_out[to_cell] = jnp.concatenate(pieces, axis=1).astype(jnp.bfloat16)
    far_cells(lambda to_cell: to_cell <= cell, lambda to_cell: share_copy(to_cell).start())
    take_wall(peers[1])
    if cells > 2:
        start_above(cells - 1)
    far_cells(lambda to_cell: to_cell > cell, lambda to_cell: share_copy(to_cell).start())
    far_cells(lambda to_cell: (to_cell > cell) & (to_cell == cells - 1), start_lag)
    take_wall(peers[2])

    def source_at(step):
        if step == 0:
            return cell
        return jnp.where(cell + step < cells, cell + step, cells - 1 - step)

    def wait_mem(step):
        source = source_at(step)
        wait_into(mem_all.at[source], mem_recv.at[source])

    def take_mem(step):
        rows = mem_rows(source_at(step), other_core)
        for at in range(walls):
            fill_single(single_all.at[step, at], rows, at)

    def first_columns(step):
        source = source_at(step)
        wait_into(block_all.at[source], block_recv.at[source])
        return columns_of([block_all[source, at] for at in range(2)])

    def exchange(half):
        return remote(
            part_mine.at[half],
            part_other.at[half],
            part_send.at[half],
            part_recv.at[half],
            wall=partner,
        )

    width = walls // 2 * wall_count
    partial = [jnp.zeros((3 * halfway, width), jnp.float32) for _ in range(2)]
    for step in range(cells):
        if step + 1 < cells:
            wait_mem(step + 1)
        left = first_columns(step)
        if step + 1 < cells:
            take_mem(step + 1)
        if step < cells - 1:
            whole = lax.dot_general(
                left,
                single_all[step].reshape(2 * width, len(TILES) * LANES),
                NT,
                preferred_element_type=jnp.float32,
            )
            for half in range(2):
                partial[half] = partial[half] + whole[:, half * width : (half + 1) * width]
            continue
        for half in range(2):
            tile = single_all[step, half * (walls // 2) : (half + 1) * (walls // 2)]
            partial[half] = partial[half] + lax.dot_general(
                left,
                tile.reshape(width, len(TILES) * LANES),
                NT,
                preferred_element_type=jnp.float32,
            )
            if step == cells - 1:
                part_mine[half] = partial[half]
                exchange(half).start()

    wait_out(mem_all.at[: cells - 1], mem_send)
    wait_out(block_all, block_send)
    wait_out(lag_all.at[: cells * walls - 1], lag_send)
    wait_out(wall_all.at[: walls - 1], wall_send)
    wait_out(second_all.at[: walls - 1], second_send)
    wait_into(data_all.at[: walls - 1], data_recv)
    wait_out(data_all.at[: walls - 1], data_send)
    wait_out(share_in, share_send)

    wait_into(lag_all.at[: cells * walls - 1], lag_recv)

    def layer(rows):
        return lax.dot_general(rows, double_all[...], NT, preferred_element_type=jnp.float32)

    lag_row = []
    for source in range(walls):
        lag_row += [
            lag_all[k * walls + source, :, j * shard_width : (j + 1) * shard_width]
            for j in range(3)
            for k in range(cells)
        ]

    moves = [
        jnp.concatenate([scatter[:, :halfway]] * 3, axis=1),
        jnp.concatenate([scatter[:, halfway:]] * 3, axis=1),
    ]

    def move_rows(move, rows):
        held = []
        for _ in range(3):
            piece = rows.astype(jnp.bfloat16)
            held.append(piece)
            rows = rows - piece.astype(jnp.float32)
        return jnp.dot(move, jnp.concatenate(held, axis=0), preferred_element_type=jnp.float32)

    total = move_rows(moves[0], layer(jnp.concatenate(lag_row, axis=1)))

    for half in range(2):
        exchange(half).wait_recv()
    pieces = []
    for source in range(walls):
        for i in range(3):
            half, at = divmod(source, walls // 2)
            held = slice(i * halfway, (i + 1) * halfway)
            lanes = slice(at * wall_count, (at + 1) * wall_count)
            velocity = part_mine[half, held, lanes] + part_other[half, held, lanes]
            dense = 2.0 * (data_all[source, i] - velocity)
            pieces.append(dense.astype(jnp.bfloat16))
    total = total + move_rows(moves[1], layer(jnp.concatenate(pieces, axis=1)))
    for i in range(3):
        out_ref[i] = total[:, i * own_points : (i + 1) * own_points]

    wait_into(share_in, share_recv)
    second_sum = jnp.zeros((halfway, LANES), jnp.float32)
    for source in range(cells):
        second_sum = second_sum + share_in[source].astype(jnp.float32)
    shift = lax.rem((cells - cell) * shard_width, wall_count)
    for i in range(3):
        held = pltpu.roll(data_rows[i][halfway:], shift, 1)[:, :shard_width]
        density_ref[i] = 2.0 * (held - second_sum[:, i * shard_width : (i + 1) * shard_width])

    for half in range(2):
        exchange(half).wait_send()


def write_kernel(velocity_ref, density_ref, velocity_hbm, density_hbm, sem):
    first = pltpu.make_async_copy(velocity_ref, velocity_hbm, sem.at[0])
    second = pltpu.make_async_copy(density_ref, density_hbm, sem.at[1])
    first.start()
    second.start()
    first.wait()
    second.wait()


def fused_shards(cells, walls, mem_pos, forces, wall_pos, wall_normal, wall_data, lag_density, batch_order):
    columns = forces.shape[0]
    halfway = columns // 2
    point_count = mem_pos.shape[1]
    wall_count = wall_pos.shape[1]
    own_points = forces.shape[2]
    shard_width = lag_density.shape[2]
    dma = pltpu.SemaphoreType.DMA
    vmem = pl.BlockSpec(memory_space=pltpu.VMEM)
    hbm = pl.BlockSpec(memory_space=pltpu.HBM)
    velocity, density = pl.pallas_call(
        functools.partial(fused_kernel, cells, walls),
        out_shape=(
            pltpu.VMEM((3, columns, own_points), jnp.float32),
            pltpu.VMEM((3, halfway, shard_width), jnp.float32),
        ),
        in_specs=[hbm] * 7,
        out_specs=(vmem, vmem),
        scratch_shapes=[
            pltpu.VMEM((1, columns), jnp.int32),
            pltpu.SMEM((1, columns), jnp.int32),
            pltpu.VMEM((3, columns, own_points), jnp.bfloat16),
            pltpu.VMEM((3, halfway, shard_width), jnp.bfloat16),
            pltpu.VMEM((3, columns, wall_count), jnp.float32),
            pltpu.VMEM((3 * halfway // 2, LANES), jnp.bfloat16),
            pltpu.VMEM((halfway, LANES), jnp.bfloat16),
            pltpu.VMEM((cells, 2, 3 * halfway // 2, LANES), jnp.bfloat16),
            pltpu.VMEM((walls, 2, halfway, LANES), jnp.bfloat16),
            pltpu.VMEM((cells * walls, halfway, LANES), jnp.bfloat16),
            pltpu.VMEM((cells, 3, point_count), jnp.float32),
            pltpu.VMEM((walls, 2, 3, wall_count), jnp.float32),
            pltpu.VMEM((walls, 3, halfway, wall_count), jnp.float32),
            pltpu.VMEM((walls, 3, wall_count, LANES), jnp.float32),
            pltpu.VMEM((3, point_count, LANES), jnp.float32),
            pltpu.VMEM((cells, walls, wall_count, len(TILES) * LANES), jnp.bfloat16),
            pltpu.VMEM((wall_count, len(TILES) * LANES), jnp.bfloat16),
            pltpu.VMEM((3 * own_points, walls * 3 * wall_count), jnp.bfloat16),
            pltpu.VMEM((2, 3 * halfway, walls // 2 * wall_count), jnp.float32),
            pltpu.VMEM((2, 3 * halfway, walls // 2 * wall_count), jnp.float32),
            pltpu.VMEM((cells, halfway, LANES), jnp.bfloat16),
            pltpu.VMEM((cells, halfway, LANES), jnp.bfloat16),
            dma((8,)),
            dma,
            dma((cells,)),
            dma,
            dma,
            dma,
            dma,
            dma,
            dma((cells,)),
            dma,
            dma((walls,)),
            dma,
            dma,
            dma((2,)),
            dma((2,)),
            dma,
            dma,
            pltpu.SemaphoreType.REGULAR((cells,)),
            pltpu.SemaphoreType.REGULAR((walls,)),
        ],
        compiler_params=pltpu.CompilerParams(
            collective_id=0, has_side_effects=True, vmem_limit_bytes=VMEM_GRANT
        ),
        name="coupling",
    )(
        mem_pos,
        jnp.transpose(forces, (1, 0, 2)),
        wall_pos,
        wall_normal,
        jnp.transpose(wall_data, (1, 0, 2)),
        jnp.transpose(lag_density, (1, 0, 2)),
        batch_order.reshape(1, columns),
    )
    velocity, density = pl.pallas_call(
        write_kernel,
        out_shape=(
            jax.ShapeDtypeStruct(velocity.shape, velocity.dtype),
            jax.ShapeDtypeStruct(density.shape, density.dtype),
        ),
        in_specs=[vmem] * 2,
        out_specs=(hbm, hbm),
        scratch_shapes=[dma((2,))],
        compiler_params=pltpu.CompilerParams(vmem_limit_bytes=1024 * 1024),
        name="write",
    )(velocity, density)
    return (jnp.transpose(velocity, (1, 0, 2)), jnp.transpose(density, (1, 0, 2)))


VMEM_GRANT = 60 * 1024 * 1024


def step(cells, walls, mem_pos, forces, wall_pos, *rest):
    point_count = mem_pos.shape[1]
    wall_count = wall_pos.shape[1]
    own_points = forces.shape[2]
    shard_width = rest[2].shape[2]
    tiles = 18 * walls * wall_count * (cells * LANES + own_points)
    fits = tiles <= VMEM_GRANT // 2
    aligned = (
        walls == 4
        and wall_count == LANES
        and 2 * own_points == LANES
        and point_count == walls * own_points
        and wall_count == cells * shard_width
        and 3 * shard_width <= LANES
    )
    if fits and aligned:
        return fused_shards(cells, walls, mem_pos, forces, wall_pos, *rest)
    return shards(mem_pos, forces, wall_pos, *rest)


def solution(mesh):
    placed = (
        P(None, ("groups", "cell")),
        P(None, None, ("groups", "cell", "wall")),
        P(None, ("groups", "wall")),
        P(None, ("groups", "wall")),
        P(None, None, ("groups", "wall")),
        P(None, None, ("groups", "wall", "cell")),
        P(),
    )
    return jax.shard_map(
        functools.partial(step, mesh.shape["cell"], mesh.shape["wall"]),
        mesh=mesh,
        in_specs=placed,
        out_specs=(
            P(None, None, ("groups", "cell", "wall")),
            P(None, None, ("groups", "wall", "cell")),
        ),
        check_vma=False,
    )
```
